32 devices in a mesh: rep: 4 (over z), shard: 8 (over y, x, core).
Axes of the slice: x: 2, y: 2, z: 4, core: 2. Of those that a mesh axis runs over, the one named last changes fastest.
Arguments:
- tokens: bfloat16 [8192, 2048], P(('rep', 'shard')), may hold values from -6 to 6
- cotangent: bfloat16 [8192, 2048], P(('rep', 'shard')), may hold values from -6 to 6
- placement_order: int32 [4, 8, 2, 128], P('rep', 'shard'), may hold values from 0 to 127, each once within a row
- seq_lengths: int32 [4, 2, 8], P('rep'), may hold values from 0 to 1024, as said below
- ln_gain: bfloat16 [2048], P('shard'), may hold values from 0.25 to 1.75
- ln_bias: bfloat16 [2048], P('shard'), may hold values from -4 to 4
- qkv_weight: bfloat16 [2048, 6144], P('shard'), may hold values from -0.125 to 0.125
- qkv_bias: bfloat16 [6144], P('shard'), may hold values from -6 to 6
- dense_weight: bfloat16 [2048, 2048], P('shard'), may hold values from -2 to 2
- dense_bias: bfloat16 [2048], P('shard'), may hold values from -4 to 4
- fc1_weight: bfloat16 [2048, 8192], P('shard'), may hold values from -0.125 to 0.125
- fc1_bias: bfloat16 [8192], P('shard'), may hold values from -4 to 4
- fc2_weight: bfloat16 [8192, 2048], P('shard'), may hold values from -0.0625 to 0.0625
- fc2_bias: bfloat16 [2048], P('shard'), may hold values from -4 to 4
Outputs:
- mixed: bfloat16 [8192, 2048], P(('rep', 'shard'))
- token_grad: bfloat16 [8192, 2048], P(('rep', 'shard'))
- grad_ln_gain: float32 [2048], P('shard')
- grad_ln_bias: float32 [2048], P('shard')
- grad_qkv_weight: float32 [2048, 6144], P('shard')
- grad_qkv_bias: float32 [6144], P('shard')
- grad_dense_weight: float32 [2048, 2048], P('shard')
- grad_dense_bias: float32 [2048], P('shard')
- grad_fc1_weight: float32 [2048, 8192], P('shard')
- grad_fc1_bias: float32 [8192], P('shard')
- grad_fc2_weight: float32 [8192, 2048], P('shard')
- grad_fc2_bias: float32 [2048], P('shard')
The draws below stay inside these ranges and needn't reach their ends.
Inputs may be any that keep to these rules, and one draw needn't show every extreme that they name: `seq_lengths`: for replica group r and micro-batch m, entry j is the length of the sequence that starts at block j, or 0 where block j continues the sequence before it. Entry 0 is positive. A sequence that starts at block j runs to the block before the next positive entry (or to the last block), b blocks, and its length is over 128 * (b - 1) and at most 128 * b; b is at most 8; some sequence has 1024 tokens. `placement_order`: each device's row for a micro-batch is a permutation; a value b sends that row to the device of shard index b // 16 of the same replica group.
All inputs are finite; a program needn't handle non-finite values.
Results may differ from the reference program's by a relative error of at most 0.013.
Values may be sent and summed in bfloat16 or wider, within the bound.
A program may use at most 704 MiB of HBM per device.

```python
import math
import jax
import jax.numpy as jnp
from jax import lax

D = 2048
HEADS = 32
HDIM = 64
ROT = 32
FF = 8192
BLOCK = 128
MICRO = 2
MAXBLK = 8
ROWS = 128
CAP = 16
NBLK = 8
REPLICAS = 4
TOKENS = 8192
N_REP = 4
N_SHARD = 8


def draw_seq_lengths(key, part):
    flag_key, length_key = jax.random.split(key)
    shape = (REPLICAS, MICRO, NBLK)
    blocks = jnp.arange(NBLK, dtype=jnp.int32)
    replica_ids = jnp.arange(REPLICAS, dtype=jnp.int32)[:, None, None]
    micro_ids = jnp.arange(MICRO, dtype=jnp.int32)[None, :, None]
    coins = jax.random.randint(flag_key, shape, 0, 100)
    kept_free = (replica_ids == 0) & (micro_ids == 0) & (blocks[None, None, :] > 0) & (blocks[None, None, :] < MAXBLK)
    starts = ((blocks[None, None, :] % MAXBLK == 0) | (coins < 35)) & jnp.logical_not(kept_free)
    later = blocks[None, :] > blocks[:, None]
    following = jnp.min(jnp.where(starts[:, :, None, :] & later[None, None, :, :], blocks[None, None, None, :], NBLK), axis=-1)
    run_blocks = following - blocks[None, None, :]
    drawn = jax.random.randint(length_key, shape, BLOCK * (run_blocks - 1) + 1, BLOCK * run_blocks + 1)
    longest = (replica_ids == 0) & (micro_ids == 0) & (blocks[None, None, :] == 0)
    drawn = jnp.where(longest, MAXBLK * BLOCK, drawn)
    return jnp.where(starts, drawn, 0).astype(jnp.int32)


def block_scale(key, dims, cuts, smallest, top_value):
    factor_of, own = 1.0, jax.random.fold_in(key, 6)
    for axis_at, blocks in cuts:
        heights = jnp.exp(jax.random.uniform(jax.random.fold_in(own, axis_at), (blocks,), jnp.float32, smallest / len(cuts), top_value / len(cuts)))
        factor_of = factor_of * jnp.repeat(heights, dims[axis_at] // blocks).reshape([-1 if axis == axis_at else 1 for axis in range(len(dims))])
    return factor_of


def bell_draw(rng, extent, width, bound, pieces=(), kind=jnp.bfloat16):
    gain = block_scale(rng, extent, pieces, -0.22, 0.18) if pieces else 1.0
    entries = jax.random.normal(rng, extent, jnp.float32) * width * gain
    return jnp.minimum(jnp.maximum(entries, -bound), bound).astype(kind)


def setup_inputs(seed: int = 0) -> dict:
    splits = jax.random.split(jax.random.key(seed), 15)
    tokens = bell_draw(splits[0], (TOKENS, D), 1.0, 6.0, ((0, 32),))
    cotangent = bell_draw(splits[1], (TOKENS, D), 1.0, 6.0, ((0, 32),))
    placement_order = jax.vmap(lambda own: jax.random.permutation(own, ROWS))(jax.random.split(splits[2], N_REP * N_SHARD * MICRO)).reshape((N_REP, N_SHARD, MICRO, ROWS)).astype(jnp.int32)
    seq_lengths = draw_seq_lengths(jax.random.fold_in(splits[14], 71), 0)
    ln_gain = jnp.clip(1.0 + 0.15 * jax.random.normal(splits[4], (D,), jnp.float32), 0.25, 1.75).astype(jnp.bfloat16)
    ln_bias = bell_draw(splits[5], (D,), 0.3, 4.0, ((0, 8),))
    qkv_weight = bell_draw(splits[6], (D, 3 * D), D ** -0.5, 0.125, ((0, 8),))
    qkv_bias = bell_draw(splits[7], (3 * D,), 0.5, 6.0, ((0, 8),))
    dense_weight = bell_draw(splits[8], (D, D), (max(D // 256, 4)) ** -0.5, 2.0, ((0, 8),))
    dense_bias = bell_draw(splits[9], (D,), 0.3, 4.0, ((0, 8),))
    fc1_weight = bell_draw(splits[10], (D, FF), D ** -0.5, 0.125, ((0, 8),))
    fc1_bias = bell_draw(splits[11], (FF,), 0.3, 4.0, ((0, 8),))
    fc2_weight = bell_draw(splits[12], (FF, D), FF ** -0.5, 0.0625, ((0, 8),))
    fc2_bias = bell_draw(splits[13], (D,), 0.3, 4.0, ((0, 8),))
    return dict(tokens=tokens, cotangent=cotangent, placement_order=placement_order, seq_lengths=seq_lengths, ln_gain=ln_gain, ln_bias=ln_bias, qkv_weight=qkv_weight, qkv_bias=qkv_bias, dense_weight=dense_weight, dense_bias=dense_bias, fc1_weight=fc1_weight, fc1_bias=fc1_bias, fc2_weight=fc2_weight, fc2_bias=fc2_bias)


@jax.custom_vjp
def low(v):
    return lax.optimization_barrier(v.astype(jnp.bfloat16)).astype(jnp.float32)

@jax.custom_vjp
def low_back(v):
    return v

def low_keep(v):
    return (low(v), None)

def low_pass(kept, grad):
    return (grad,)

def back_keep(v):
    return (v, None)

def back_low(kept, grad):
    return (low(grad),)
low.defvjp(low_keep, low_pass)
low_back.defvjp(back_keep, back_low)
HIGH = lax.Precision.HIGHEST

def matmul(left, right):
    return jnp.dot(left, right, precision=HIGH, preferred_element_type=jnp.float32)

def normalize(inputs, gain_vec, bias_vec):
    average = lax.optimization_barrier(jnp.mean(inputs, axis=-1, keepdims=True))
    centered = inputs - average
    variance = lax.optimization_barrier(jnp.mean(centered * centered, axis=-1, keepdims=True))
    return centered * lax.rsqrt(variance + 1e-05) * gain_vec + bias_vec

def rotary_tables(position):
    half_dim = ROT // 2
    freqs = jnp.exp(-math.log(10000.0) * jnp.arange(half_dim, dtype=jnp.float32) * 2.0 / ROT)
    angles = position.astype(jnp.float32)[:, None] * freqs[None, :]
    angles = jnp.concatenate([angles, angles], axis=1)
    return (jnp.cos(angles)[:, None, :], jnp.sin(angles)[:, None, :])

def rotate(heads, cosine_table, sine_table):
    half_dim = ROT // 2
    turned_part = heads[..., :ROT]
    swapped = jnp.concatenate([-turned_part[..., half_dim:], turned_part[..., :half_dim]], axis=-1)
    return jnp.concatenate([turned_part * cosine_table + swapped * sine_table, heads[..., ROT:]], axis=-1)

def pack_meta(lengths_row):
    blocks = jnp.arange(NBLK, dtype=jnp.int32)
    begins = lax.optimization_barrier(jnp.max(jnp.where((lengths_row[None, :] > 0) & (blocks[None, :] <= blocks[:, None]), blocks[None, :], 0), axis=1))
    all_rows = jnp.arange(NBLK * BLOCK, dtype=jnp.int32)
    segment = begins[all_rows // BLOCK]
    position = all_rows - segment * BLOCK
    usable = position < lengths_row[segment]
    return (segment, position, usable)

def layer(params, inputs, meta):
    gain_vec, bias_vec, w_qkv, b_qkv, w_dense, b_dense, w_fc1, b_fc1, w_fc2, b_fc2 = params
    segment, position, usable = meta
    total_rows = inputs.shape[0]
    hn = low(normalize(inputs, gain_vec, bias_vec))
    qkv = low_back(matmul(hn, w_qkv) + b_qkv)
    queries = qkv[:, :D].reshape(total_rows, HEADS, HDIM)
    keys = qkv[:, D:2 * D].reshape(total_rows, HEADS, HDIM)
    values = qkv[:, 2 * D:].reshape(total_rows, HEADS, HDIM)
    cosine_table, sine_table = rotary_tables(position)
    q_low = low(rotate(queries, cosine_table, sine_table))
    k_low = low(rotate(keys, cosine_table, sine_table))
    v_low = low(values)
    scale = 1.0 / math.sqrt(HDIM)
    q_block = math.gcd(total_rows, 512)
    count = total_rows // q_block

    def attend(items):
        q_part, seg_part, pos_part = items
        scores = jnp.einsum('qhd,khd->hqk', q_part, k_low, precision=HIGH) * scale
        scores = low_back(scores)
        allowed = (seg_part[:, None] == segment[None, :]) & (position[None, :] <= pos_part[:, None]) & usable[None, :]
        masked = jnp.where(allowed[None], scores, -1e+30)
        probs = low(jax.nn.softmax(masked, axis=-1))
        return jnp.einsum('hqk,khd->qhd', probs, v_low, precision=HIGH)
    outputs = lax.map(jax.checkpoint(attend), (q_low.reshape(count, q_block, HEADS, HDIM), segment.reshape(count, q_block), position.reshape(count, q_block)))
    ob = low(low_back(outputs.reshape(total_rows, D)))
    attn_proj = matmul(ob, w_dense) + b_dense
    upper = low_back(matmul(hn, w_fc1) + b_fc1)
    gact = low(jax.nn.gelu(upper, approximate=True))
    mlp_out = matmul(gact, w_fc2) + b_fc2
    return inputs + usable.astype(jnp.float32)[:, None] * (attn_proj + mlp_out)

def reference(tokens, cotangent, placement_order, seq_lengths, ln_gain, ln_bias, qkv_weight, qkv_bias, dense_weight, dense_bias, fc1_weight, fc1_bias, fc2_weight, fc2_bias):
    packs = N_REP * MICRO

    def arrange(array):
        return array.astype(jnp.float32).reshape(N_REP, N_SHARD, MICRO, ROWS, D).transpose(0, 2, 1, 3, 4).reshape(packs, N_SHARD, ROWS, D)
    inputs_all = arrange(tokens)
    cots_all = arrange(cotangent)
    orders_all = placement_order.transpose(0, 2, 1, 3).reshape(packs, N_SHARD, ROWS)
    lengths_all = seq_lengths.reshape(packs, NBLK)
    params = tuple((item.astype(jnp.float32) for item in (ln_gain, ln_bias, qkv_weight, qkv_bias, dense_weight, dense_bias, fc1_weight, fc1_bias, fc2_weight, fc2_bias)))

    def one_pack(carry, items):
        source, cots, order_rows, lengths_row = items
        source_ids = jnp.arange(N_SHARD, dtype=jnp.int32)[:, None]
        target = (order_rows // CAP * ROWS + source_ids * CAP + order_rows % CAP).reshape(-1).astype(jnp.int32)
        packed_x = jnp.zeros((N_SHARD * ROWS, D), jnp.float32).at[target].set(source.reshape(-1, D))
        packed_g = jnp.zeros((N_SHARD * ROWS, D), jnp.float32).at[target].set(cots.reshape(-1, D))
        meta = pack_meta(lengths_row)
        result, pull = jax.vjp(lambda prm, inp: layer(prm, inp, meta), params, packed_x)
        grads, input_grad = pull(packed_g)
        carry = tuple((left + right for left, right in zip(carry, grads)))
        return (carry, (result[target], input_grad[target]))
    zeros = tuple((jnp.zeros(item.shape, jnp.float32) for item in params))
    totals, (outs_all, grads_all) = lax.scan(one_pack, zeros, (inputs_all, cots_all, orders_all, lengths_all))

    def restore(array):
        return array.reshape(N_REP, MICRO, N_SHARD, ROWS, D).transpose(0, 2, 1, 3, 4).reshape(-1, D)
    mixed = restore(outs_all).astype(jnp.bfloat16)
    token_grad = restore(grads_all).astype(jnp.bfloat16)
    return (mixed, token_grad, totals[0], totals[1], totals[2], totals[3], totals[4], totals[5], totals[6], totals[7], totals[8], totals[9])
```

```python
import functools
import math

import jax
import jax.numpy as jnp
from jax import lax
from jax.experimental import pallas as pl
from jax.experimental.pallas import tpu as pltpu
from jax.sharding import PartitionSpec as P

HEADS = 32
HDIM = 64
ROT = 32
BLOCK = 128
MICRO = 2
MAXBLK = 8
PAIR = 2 * HDIM
NEG = -1e30


def dot(left, right, dims, out=jnp.float32):
    return lax.dot_general(left, right, (dims, ((), ())), preferred_element_type=out)


def block_begins(lengths):
    blocks = jnp.arange(lengths.shape[1], dtype=jnp.int32)
    started = (lengths[:, None, :] > 0) & (blocks[None, None, :] <= blocks[None, :, None])
    begins = jnp.max(jnp.where(started, blocks[None, None, :], 0), axis=2)
    own = begins[:, :, None] == blocks[None, None, :]
    limits = jnp.sum(jnp.where(own, lengths[:, None, :], 0), axis=2)
    return begins, limits


def attention_kernel(begin_ref, q_ref, k_ref, v_ref, do_ref, cos_ref, low_ref, high_ref, kid_ref,
                     ob_ref, dq_ref, dk_ref, dv_ref, ks, vs, dks, dvs):
    micro = pl.program_id(0)
    blocks = q_ref.shape[1]
    lane = lax.broadcasted_iota(jnp.int32, (BLOCK, PAIR), 1)
    half = ROT // 2

    def rows(ref, j):
        return ref[:, j].reshape(BLOCK, PAIR)

    def table(ref, j):
        return ref[j * BLOCK:(j + 1) * BLOCK, :]

    def turn(x, j, back):
        up = pltpu.roll(x, PAIR - half, 1)
        down = pltpu.roll(x, half, 1)
        low, high = table(low_ref, j), table(high_ref, j)
        if back:
            return x * table(cos_ref, j) - up * low - down * high
        return x * table(cos_ref, j) + up * low + down * high

    for j in range(blocks):
        ks[j * BLOCK:(j + 1) * BLOCK, :] = turn(rows(k_ref, j), j, False).astype(jnp.bfloat16)
        vs[j * BLOCK:(j + 1) * BLOCK, :] = rows(v_ref, j).astype(jnp.bfloat16)
    dks[...] = jnp.zeros_like(dks)
    dvs[...] = jnp.zeros_like(dvs)
    causal = lax.broadcasted_iota(jnp.int32, (BLOCK, BLOCK), 1) <= lax.broadcasted_iota(
        jnp.int32, (BLOCK, BLOCK), 0
    )
    scale = 1.0 / math.sqrt(HDIM)
    zero = jnp.zeros((), jnp.bfloat16)
    for j in range(blocks):
        first = max(0, j - MAXBLK + 1)
        span = slice(first * BLOCK, (j + 1) * BLOCK)
        q_all = turn(rows(q_ref, j), j, False).astype(jnp.bfloat16)
        do_all = rows(do_ref, j).astype(jnp.bfloat16)
        keys, values = ks[span, :], vs[span, :]
        same = kid_ref[:, span] == begin_ref[micro, j]
        bias = jnp.where(same, 0.0, NEG)
        width = (j + 1 - first) * BLOCK
        outs, dqs = [], []
        for head in range(PAIR // HDIM):
            mine = (lane >= head * HDIM) & (lane < (head + 1) * HDIM)
            q = jnp.where(mine, q_all, zero)
            do = jnp.where(mine, do_all, zero)
            scores = dot(q, keys, ((1,), (1,))) * scale + bias
            tail = jnp.where(causal, scores[:, width - BLOCK:], NEG)
            if width > BLOCK:
                scores = jnp.concatenate([scores[:, :width - BLOCK], tail], axis=1)
            else:
                scores = tail
            top = jnp.max(scores, axis=1, keepdims=True)
            expo = jnp.exp(scores - top)
            probs = expo / jnp.sum(expo, axis=1, keepdims=True)
            low_probs = probs.astype(jnp.bfloat16)
            outs.append(dot(low_probs, values, ((1,), (0,))))
            dprobs = dot(do, values, ((1,), (1,)))
            weighted = probs * dprobs
            delta = jnp.sum(weighted, axis=1, keepdims=True)
            dscores = (weighted - probs * delta).astype(jnp.bfloat16)
            dqs.append(dot(dscores, keys, ((1,), (0,))))
            dks[span, :] += dot(dscores, q, ((0,), (0,)))
            dvs[span, :] += dot(low_probs, do, ((0,), (0,)))
        first_head = lane < HDIM
        shape = (q_ref.shape[0], q_ref.shape[2], PAIR)
        ob = jnp.where(first_head, outs[0], outs[1])
        ob_ref[:, j] = ob.astype(jnp.bfloat16).astype(jnp.float32).reshape(shape)
        dq = turn(jnp.where(first_head, dqs[0], dqs[1]) * scale, j, True)
        dq_ref[:, j] = dq.astype(jnp.bfloat16).astype(jnp.float32).reshape(shape)
    for j in range(blocks):
        here = slice(j * BLOCK, (j + 1) * BLOCK)
        shape = (q_ref.shape[0], q_ref.shape[2], PAIR)
        dk = turn(dks[here, :] * scale, j, True)
        dk_ref[:, j] = dk.astype(jnp.bfloat16).astype(jnp.float32).reshape(shape)
        dv_ref[:, j] = dvs[here, :].astype(jnp.bfloat16).astype(jnp.float32).reshape(shape)


def attention(begins, qkv, dout, cosine, low, high, kid):
    group, micros, blocks, cap, _ = qkv.shape
    width = dout.shape[-1]
    pairs = width // PAIR
    total = blocks * BLOCK

    def rows_spec(offset):
        return pl.BlockSpec(
            (group, None, blocks, cap, PAIR), lambda m, p, *_: (0, m, 0, 0, offset + p)
        )

    table_spec = pl.BlockSpec((None, total, PAIR), lambda m, p, *_: (m, 0, 0))
    out = jax.ShapeDtypeStruct(dout.shape, jnp.float32)
    work = micros * pairs * 2 * blocks * (min(blocks, MAXBLK) + 1) // 2 * BLOCK * BLOCK
    return pl.pallas_call(
        attention_kernel,
        grid_spec=pltpu.PrefetchScalarGridSpec(
            num_scalar_prefetch=1,
            grid=(micros, pairs),
            in_specs=[
                rows_spec(0), rows_spec(pairs), rows_spec(2 * pairs), rows_spec(0),
                table_spec, table_spec, table_spec,
                pl.BlockSpec((None, 1, total), lambda m, p, *_: (m, 0, 0)),
            ],
            out_specs=[rows_spec(0)] * 4,
            scratch_shapes=[
                pltpu.VMEM((total, PAIR), jnp.bfloat16),
                pltpu.VMEM((total, PAIR), jnp.bfloat16),
                pltpu.VMEM((total, PAIR), jnp.float32),
                pltpu.VMEM((total, PAIR), jnp.float32),
            ],
        ),
        out_shape=[out] * 4,
        compiler_params=pltpu.CompilerParams(vmem_limit_bytes=48 << 20),
        cost_estimate=pl.CostEstimate(
            flops=12 * work * PAIR, bytes_accessed=8 * dout.size * 4, transcendentals=work
        ),
    )(begins, qkv, qkv, qkv, dout, cosine, low, high, kid)


def body(
    tokens, cotangent, placement_order, seq_lengths, ln_gain, ln_bias, qkv_weight, qkv_bias,
    dense_weight, dense_bias, fc1_weight, fc1_bias, fc2_weight, fc2_bias,
):
    bf16, f32 = jnp.bfloat16, jnp.float32
    group = lax.axis_size("shard")
    reps = lax.axis_size("rep")
    me = lax.axis_index("shard")
    width = tokens.shape[1]
    rows = tokens.shape[0] // MICRO
    cap = rows // group
    mine = width // group
    ff_mine = fc1_weight.shape[1] // group
    blocks = seq_lengths.shape[2]
    all_rows = MICRO * rows * group

    pieces = (ln_gain, ln_bias, dense_bias, fc2_bias, qkv_bias, fc1_bias)
    packed = jnp.concatenate(pieces)
    spread = lax.all_gather(packed, "shard", axis=0).astype(f32)
    full, at = [], 0
    for piece in pieces:
        full.append(spread[:, at:at + piece.shape[0]].reshape(-1))
        at += piece.shape[0]
    gain, lnb, b_dense, b_fc2, b_qkv, b_fc1 = full
    b_qkv = lax.dynamic_slice_in_dim(b_qkv.reshape(3, width), me * mine, mine, 1).reshape(-1)
    b_fc1 = lax.dynamic_slice_in_dim(b_fc1, me * ff_mine, ff_mine, 0)

    fc1 = lax.all_to_all(
        fc1_weight.reshape(mine, group, ff_mine).transpose(1, 0, 2), "shard", 0, 0, tiled=True
    ).reshape(width, ff_mine)
    w_qkv = lax.all_to_all(
        qkv_weight.reshape(mine, 3, group, mine).transpose(2, 0, 1, 3), "shard", 0, 0, tiled=True
    ).reshape(width, 3 * mine)

    begins, limits = block_begins(seq_lengths[0])
    spot = jnp.arange(BLOCK, dtype=jnp.int32)
    index = jnp.arange(blocks, dtype=jnp.int32)
    position = (index[None, :, None] - begins[:, :, None]) * BLOCK + spot[None, None, :]
    valid = position < limits[:, :, None]
    key_id = jnp.where(valid, begins[:, :, None], -1).reshape(MICRO, 1, blocks * BLOCK)
    lane = jnp.arange(PAIR, dtype=jnp.int32) % HDIM
    half = ROT // 2
    freqs = jnp.exp(-math.log(10000.0) * jnp.arange(half, dtype=f32) * 2.0 / ROT)
    angles = position.reshape(MICRO, -1, 1).astype(f32) * freqs[lane % half]
    sines = jnp.sin(angles)
    cosine = jnp.where(lane < ROT, jnp.cos(angles), 1.0)
    low = jnp.where(lane < half, -sines, 0.0)
    high = jnp.where((lane >= half) & (lane < ROT), sines, 0.0)

    orders = placement_order[0, 0]
    select = (orders[:, None, :] == jnp.arange(rows, dtype=jnp.int32)[None, :, None]).astype(bf16)

    def arrange(array):
        return jnp.einsum(
            "mti,mid->mtd", select, array.reshape(MICRO, rows, width),
            preferred_element_type=f32,
        ).astype(bf16).reshape(MICRO * rows, width)

    x_home, g_home = arrange(tokens), arrange(cotangent)
    valid_home = lax.dynamic_index_in_dim(
        valid.reshape(MICRO, group, group, cap), me, 2, keepdims=False
    ).reshape(MICRO * rows, 1)
    gy_home = jnp.where(valid_home, g_home, jnp.zeros((), bf16))
    x32 = x_home.astype(f32)
    centered = x32 - jnp.mean(x32, axis=1, keepdims=True)
    rstd = lax.rsqrt(jnp.mean(centered * centered, axis=1, keepdims=True) + 1e-05)
    hn_home = (centered * rstd * gain + lnb).astype(bf16)
    gy = lax.all_gather(gy_home, "shard", axis=0, tiled=True)
    hn = lax.all_gather(hn_home, "shard", axis=0, tiled=True)

    upper = dot(hn, fc1, ((1,), (0,))) + b_fc1
    inner = math.sqrt(2.0 / math.pi) * (upper + 0.044715 * upper * upper * upper)
    curve = jnp.tanh(inner)
    act = (0.5 * upper * (1.0 + curve)).astype(bf16)
    slope = 0.5 * (1.0 + curve) + 0.5 * upper * (1.0 - curve * curve) * math.sqrt(
        2.0 / math.pi
    ) * (1.0 + 3 * 0.044715 * upper * upper)
    dup = (dot(gy, fc2_weight, ((1,), (1,))) * slope).astype(bf16)
    g_fc2 = dot(act, gy, ((0,), (0,)), f32).astype(bf16)
    g_fc1 = dot(hn, dup, ((0,), (0,)), f32).astype(bf16)

    def over_reps(part):
        return lax.psum_scatter(part, "rep", scatter_dimension=0, tiled=True)

    def from_reps(part):
        return lax.all_gather(part, "rep", axis=0, tiled=True)

    def by_rows(grad):
        cols = grad.shape[1]
        split = grad.reshape(group, reps, mine // reps, cols).transpose(1, 0, 2, 3)
        part = over_reps(split.reshape(reps * group, mine // reps, cols))
        part = lax.all_to_all(part, "shard", 0, 0, tiled=True)
        whole = from_reps(part)
        return whole.reshape(reps, group, mine // reps, cols)

    grad_fc2 = from_reps(over_reps(g_fc2)).astype(f32)
    grad_fc1 = by_rows(g_fc1).transpose(0, 2, 1, 3).reshape(mine, -1).astype(f32)

    qkv = dot(hn, w_qkv, ((1,), (0,))) + b_qkv
    dout = dot(gy, dense_weight, ((1,), (1,)))
    shape = (group, MICRO, blocks, cap)
    ob, dq, dk, dv = attention(
        begins, qkv.reshape(*shape, 3 * mine), dout.reshape(*shape, mine), cosine, low, high,
        key_id,
    )
    ob = ob.reshape(all_rows, mine).astype(bf16)
    dqkv = jnp.concatenate(
        [part.reshape(all_rows, mine).astype(bf16) for part in (dq, dk, dv)], axis=1
    )
    g_qkv = dot(hn, dqkv, ((0,), (0,)), f32).astype(bf16)
    g_dense = dot(ob, gy, ((0,), (0,)), f32).astype(bf16)
    grad_dense = from_reps(over_reps(g_dense)).astype(f32)
    grad_qkv = by_rows(g_qkv).reshape(reps, group, mine // reps, 3, mine)
    grad_qkv = grad_qkv.transpose(0, 2, 3, 1, 4).reshape(mine, 3 * width).astype(f32)

    def home(part):
        got = lax.all_to_all(part.reshape(group, MICRO * rows, width), "shard", 0, 0, tiled=True)
        return jnp.sum(got.astype(f32), axis=0)

    out_part = (
        dot(act, fc2_weight, ((1,), (0,))) + dot(ob, dense_weight, ((1,), (0,)))
    ).astype(bf16)
    dh_part = (dot(dqkv, w_qkv, ((1,), (1,))) + dot(dup, fc1, ((1,), (1,)))).astype(bf16)
    branch = home(out_part) + (b_dense + b_fc2)
    mixed = (x32 + jnp.where(valid_home, branch, 0.0)).astype(bf16)
    dh = home(dh_part)
    xhat = centered * rstd
    scaled = dh * gain
    dx = (
        scaled
        - jnp.mean(scaled, axis=1, keepdims=True)
        - xhat * jnp.mean(scaled * xhat, axis=1, keepdims=True)
    ) * rstd
    token_grad = (g_home.astype(f32) + dx).astype(bf16)

    def back(array):
        return jnp.einsum(
            "mti,mtd->mid", select, array.reshape(MICRO, rows, width),
            preferred_element_type=f32,
        ).astype(bf16).reshape(MICRO * rows, width)

    def placed(part, count, offset):
        return lax.dynamic_update_slice_in_dim(
            jnp.zeros((count,) + part.shape[1:], f32), part, offset, 0
        )

    v_qkv = jnp.sum(dqkv.astype(f32), axis=0).reshape(3, mine).T
    v_qkv = placed(v_qkv, width, me * mine).T.reshape(-1)
    v_fc1 = placed(jnp.sum(dup.astype(f32), axis=0), group * ff_mine, me * ff_mine)
    v_out = jnp.sum(gy_home.astype(f32), axis=0)
    v_gain = jnp.sum(dh * xhat, axis=0)
    v_lnb = jnp.sum(dh, axis=0)
    sums = lax.psum(jnp.concatenate([v_qkv, v_fc1, v_out, v_gain, v_lnb]), ("rep", "shard"))
    outs, at = [], 0
    for count in (3 * width, group * ff_mine, width, width, width):
        share = count // group
        outs.append(lax.dynamic_slice_in_dim(sums, at + me * share, share, 0))
        at += count
    bias_qkv, bias_fc1, bias_out, gain_grad, lnb_grad = outs
    return (
        back(mixed), back(token_grad), gain_grad, lnb_grad, grad_qkv, bias_qkv, grad_dense,
        bias_out, grad_fc1, bias_fc1, grad_fc2, bias_out,
    )


def solution(mesh):
    rows = P(("rep", "shard"), None)
    vector, matrix = P("shard"), P("shard", None)
    layer = (vector, vector, matrix, vector, matrix, vector, matrix, vector, matrix, vector)
    return jax.shard_map(
        body,
        mesh=mesh,
        in_specs=(rows, rows, P("rep", "shard", None, None), P("rep", None, None)) + layer,
        out_specs=(rows, rows) + layer,
        check_vma=False,
    )
```

```python
import math

import jax
import jax.numpy as jnp
import numpy as np
from jax import lax
from jax.experimental import pallas as pl
from jax.experimental.pallas import tpu as pltpu
from jax.sharding import PartitionSpec as P

HEADS = 32
HDIM = 64
ROT = 32
BLOCK = 128
MICRO = 2
MAXBLK = 8
PAIR = 2 * HDIM
NEG = -1e30
FUSED_BYTES = 48 << 20


def dot(left, right, dims, out=jnp.float32):
    return lax.dot_general(left, right, (dims, ((), ())), preferred_element_type=out)


def block_begins(lengths):
    blocks = jnp.arange(lengths.shape[1], dtype=jnp.int32)
    started = (lengths[:, None, :] > 0) & (blocks[None, None, :] <= blocks[None, :, None])
    begins = jnp.max(jnp.where(started, blocks[None, None, :], 0), axis=2)
    own = begins[:, :, None] == blocks[None, None, :]
    limits = jnp.sum(jnp.where(own, lengths[:, None, :], 0), axis=2)
    return begins, limits


def rotary_tables():
    half = ROT // 2
    lane = np.arange(PAIR) % HDIM
    freqs = np.exp(-math.log(10000.0) * np.arange(half) * 2.0 / ROT).astype(np.float32)
    position = np.arange(MAXBLK * BLOCK, dtype=np.float32)
    angles = (position[:, None] * freqs[lane % half][None, :]).astype(np.float64)
    sines = np.sin(angles)
    cosine = np.where(lane < ROT, np.cos(angles), 1.0)
    signed = np.where(lane < half, -sines, np.where(lane < ROT, sines, 0.0))
    return [jnp.asarray(t.astype(np.float32)) for t in (cosine, signed)]


def attention_kernel(begin_ref, q_ref, k_ref, v_ref, do_ref, cos_ref, sin_ref, kid_ref,
                     ob_ref, dq_ref, dk_ref, dv_ref, ks, vs, dks, dvs):
    micro = pl.program_id(0)
    blocks = q_ref.shape[1]
    lane = lax.broadcasted_iota(jnp.int32, (BLOCK, PAIR), 1)
    half = ROT // 2

    def rows(ref, j):
        return ref[:, j].reshape(BLOCK, PAIR)

    def table(ref, j):
        return ref[pl.ds(pl.multiple_of((j - begin_ref[micro, j]) * BLOCK, BLOCK), BLOCK), :]

    def turn(x, j, back):
        other = jnp.where(
            lane % HDIM < half, pltpu.roll(x, PAIR - half, 1), pltpu.roll(x, half, 1)
        ) * table(sin_ref, j)
        straight = x * table(cos_ref, j)
        return straight - other if back else straight + other

    for j in range(blocks):
        ks[j * BLOCK:(j + 1) * BLOCK, :] = turn(rows(k_ref, j), j, False).astype(jnp.bfloat16)
        vs[j * BLOCK:(j + 1) * BLOCK, :] = rows(v_ref, j).astype(jnp.bfloat16)
    dks[...] = jnp.zeros_like(dks)
    dvs[...] = jnp.zeros_like(dvs)
    causal = lax.broadcasted_iota(jnp.int32, (BLOCK, BLOCK), 1) <= lax.broadcasted_iota(
        jnp.int32, (BLOCK, BLOCK), 0
    )
    scale = 1.0 / math.sqrt(HDIM)
    zero = jnp.zeros((), jnp.bfloat16)
    for j in range(blocks):
        first = max(0, j - MAXBLK + 1)
        span = slice(first * BLOCK, (j + 1) * BLOCK)
        q_all = turn(rows(q_ref, j), j, False).astype(jnp.bfloat16)
        do_all = rows(do_ref, j).astype(jnp.bfloat16)
        keys, values = ks[span, :], vs[span, :]
        same = kid_ref[:, span] == begin_ref[micro, j]
        bias = jnp.where(same, 0.0, NEG)
        width = (j + 1 - first) * BLOCK
        outs, dqs = [], []
        for head in range(PAIR // HDIM):
            mine = (lane >= head * HDIM) & (lane < (head + 1) * HDIM)
            q = jnp.where(mine, q_all, zero)
            do = jnp.where(mine, do_all, zero)
            scores = dot(q, keys, ((1,), (1,))) * scale + bias
            tail = jnp.where(causal, scores[:, width - BLOCK:], NEG)
            if width > BLOCK:
                scores = jnp.concatenate([scores[:, :width - BLOCK], tail], axis=1)
            else:
                scores = tail
            top = jnp.max(scores, axis=1, keepdims=True)
            expo = jnp.exp(scores - top)
            probs = expo / jnp.sum(expo, axis=1, keepdims=True)
            low_probs = probs.astype(jnp.bfloat16)
            outs.append(dot(low_probs, values, ((1,), (0,))))
            dprobs = dot(do, values, ((1,), (1,)))
            weighted = probs * dprobs
            delta = jnp.sum(weighted, axis=1, keepdims=True)
            dscores = (weighted - probs * delta).astype(jnp.bfloat16)
            dqs.append(dot(dscores, keys, ((1,), (0,))))
            dks[span, :] += dot(dscores, q, ((0,), (0,)))
            dvs[span, :] += dot(low_probs, do, ((0,), (0,)))
        first_head = lane < HDIM
        shape = (q_ref.shape[0], q_ref.shape[2], PAIR)
        ob = jnp.where(first_head, outs[0], outs[1])
        ob_ref[:, j] = ob.astype(jnp.bfloat16).astype(jnp.float32).reshape(shape)
        dq = turn(jnp.where(first_head, dqs[0], dqs[1]) * scale, j, True)
        dq_ref[:, j] = dq.astype(jnp.bfloat16).astype(jnp.float32).reshape(shape)
    for j in range(blocks):
        here = slice(j * BLOCK, (j + 1) * BLOCK)
        shape = (q_ref.shape[0], q_ref.shape[2], PAIR)
        dk = turn(dks[here, :] * scale, j, True)
        dk_ref[:, j] = dk.astype(jnp.bfloat16).astype(jnp.float32).reshape(shape)
        dv_ref[:, j] = dvs[here, :].astype(jnp.bfloat16).astype(jnp.float32).reshape(shape)


def attention(begins, qkv, dout, kid):
    group, micros, blocks, cap, _ = qkv.shape
    width = dout.shape[-1]
    pairs = width // PAIR
    total = blocks * BLOCK

    def rows_spec(offset):
        return pl.BlockSpec(
            (group, None, blocks, cap, PAIR), lambda m, p, *_: (0, m, 0, 0, offset + p)
        )

    table_spec = pl.BlockSpec((MAXBLK * BLOCK, PAIR), lambda m, p, *_: (0, 0))
    out = jax.ShapeDtypeStruct(dout.shape, jnp.float32)
    work = micros * pairs * 2 * blocks * (min(blocks, MAXBLK) + 1) // 2 * BLOCK * BLOCK
    return pl.pallas_call(
        attention_kernel,
        grid_spec=pltpu.PrefetchScalarGridSpec(
            num_scalar_prefetch=1,
            grid=(micros, pairs),
            in_specs=[
                rows_spec(0), rows_spec(pairs), rows_spec(2 * pairs), rows_spec(0),
                table_spec, table_spec,
                pl.BlockSpec((None, 1, total), lambda m, p, *_: (m, 0, 0)),
            ],
            out_specs=[rows_spec(0)] * 4,
            scratch_shapes=[
                pltpu.VMEM((total, PAIR), jnp.bfloat16),
                pltpu.VMEM((total, PAIR), jnp.bfloat16),
                pltpu.VMEM((total, PAIR), jnp.float32),
                pltpu.VMEM((total, PAIR), jnp.float32),
            ],
        ),
        out_shape=[out] * 4,
        compiler_params=pltpu.CompilerParams(vmem_limit_bytes=48 << 20),
        cost_estimate=pl.CostEstimate(
            flops=12 * work * PAIR, bytes_accessed=8 * dout.size * 4, transcendentals=work
        ),
    )(begins, qkv, qkv, qkv, dout, *rotary_tables(), kid)


MESH = pl.DeviceIdType.MESH
SLOTS = 4
TILES = 4


def fused_kernel(
    begin_ref, kid_ref, bq_ref, bf_ref, tables, gy_home, hn_home, fc1_w, qkv_w, fc2_w, dense_w,
    grad, grad_a, grad_b, grad_t, gq, gq_a, gq_b, gq_t, part_in, home, vec_f, vec_q,
    gy, hn, fc1, fc2, wqkv, dense, act, dup, ob, dqkv, qkv, dout, ks, vs, dks, dvs, tt, gst, ast,
    pb, vb, table,
    load, ag_send, ag_recv, w_send, w_recv, st, g_send, g_own, g_recv, za_s, za_r, zb_s, zb_r, zc_s,
    zc_r, zt, zl, d_send, p_recv, h_recv,
):
    bf16, f32 = jnp.bfloat16, jnp.float32
    me, rep = lax.axis_index("shard"), lax.axis_index("rep")
    core, cx, cy = me % 2, (me // 2) % 2, me // 4
    near = rep + 1 - 2 * (rep % 2)
    far = 3 - rep
    inner = (rep == 1) | (rep == 2)
    outer = (rep == 0) | (rep == 3)
    rows_home = gy_home.shape[0]
    width = gy_home.shape[1]
    ff = fc1.shape[1]
    tile = ff // TILES
    wide = 512
    pairs = wqkv.shape[0]
    cols3 = 3 * PAIR

    def flip(e):
        return ((cy + e // 4) % 2) * 4 + ((cx + (e // 2) % 2) % 2) * 2 + (core + e % 2) % 2

    def at_shard(d):
        return {"shard": d}

    def at_rep(d):
        return {"rep": d}

    def remote(src, dst, send, recv, dev):
        return pltpu.make_async_remote_copy(
            src_ref=src, dst_ref=dst, send_sem=send, recv_sem=recv, device_id=dev,
            device_id_type=MESH,
        )

    def local(src, dst, sem):
        return pltpu.make_async_copy(src, dst, sem)

    def span(i, size):
        return pl.ds(pl.multiple_of(i * size, size), size)

    def own(ref, q):
        return ref.at[span(q, rows_home), :]

    loads = [
        local(gy_home, own(gy, me), load.at[0]),
        local(hn_home, own(hn, me), load.at[1]),
        local(fc2_w, fc2, load.at[2]),
        local(dense_w, dense, load.at[3]),
        local(fc1_w.at[:, span(me, ff)], own(fc1, me), load.at[4]),
        local(qkv_w.at[me], wqkv.at[:, span(me, rows_home), :], load.at[5]),
    ]
    for copy in loads:
        copy.start()

    barrier = pltpu.get_barrier_semaphore()
    for e in range(1, 8):
        pl.semaphore_signal(barrier, inc=1, device_id=at_shard(flip(e)), device_id_type=MESH)
    pl.semaphore_signal(barrier, inc=1, device_id=at_rep(near), device_id_type=MESH)
    pl.semaphore_signal(barrier, inc=1, device_id=at_rep(far), device_id_type=MESH)
    pl.semaphore_wait(barrier, 9)

    pairs_in = ((gy_home, gy), (hn_home, hn))
    for a, (source, buf) in enumerate(pairs_in):
        for n, e in enumerate((2, 4, 1)):
            remote(source, own(buf, me), ag_send.at[a, n], ag_recv.at[a, e], at_shard(flip(e))).start()

    def send_fc1(i):
        for e in range(1, 8):
            d = flip(e)
            remote(
                fc1_w.at[:, pl.ds(pl.multiple_of(d * ff + i * tile, tile), tile)],
                fc1.at[span(me, rows_home), pl.ds(i * tile, tile)],
                w_send.at[0], w_recv.at[i], at_shard(d),
            ).start()

    def ag_wait(a, e):
        buf = pairs_in[a][1]
        remote(own(buf, me), own(buf, flip(e)), ag_send.at[a, 0], ag_recv.at[a, e],
               at_shard(flip(e))).wait_recv()

    def forward(a, have, to, n):
        buf = pairs_in[a][1]
        q = own(buf, flip(have))
        remote(q, q, ag_send.at[a, n], ag_recv.at[a, have ^ to], at_shard(flip(to))).start()

    send_fc1(0)
    for a in range(2):
        ag_wait(a, 2)
        forward(a, 2, 1, 4)

        @pl.when(core == 0)
        def _():
            forward(a, 2, 4, 3)

        ag_wait(a, 4)
        forward(a, 4, 1, 5)

        @pl.when(core == 1)
        def _():
            forward(a, 4, 2, 3)

    for i in range(1, TILES):
        send_fc1(i)
    for e in range(1, 8):
        d = flip(e)
        remote(qkv_w.at[d], wqkv.at[:, span(me, rows_home), :], w_send.at[1], w_recv.at[TILES],
               at_shard(d)).start()
    for copy in loads:
        copy.wait()
    for a in range(2):
        ag_wait(a, 6)
        forward(a, 6, 1, 6)
    for a in range(2):
        for e in (1, 3, 5, 7):
            ag_wait(a, e)

    uniform = 2 * grad.shape[0]
    half = rows_home // 2
    units = uniform + 2 * pairs

    def unit(u):
        if isinstance(u, int) and u >= uniform:
            v = u - uniform
            where = (v // 2, pl.ds((v % 2) * half, half), slice(None))
            return [ref.at[where] for ref in (gq, gq_a, gq_b, gq_t)] + [gq.shape[2]]
        where = (u // 2, pl.ds(pl.multiple_of((u % 2) * half, half), half), slice(None))
        return [ref.at[where] for ref in (grad, grad_a, grad_b, grad_t)] + [width]

    def chain_a(u):
        g, a, _, _, _ = unit(u)

        @pl.when(outer)
        def _():
            remote(g, a, za_s.at[u], za_r.at[u], at_rep(near)).start()

    def chain_b(u):
        g, a, b, t, n = unit(u)
        slot = u % SLOTS
        mine = pb.at[slot, :, 0:n]

        @pl.when(inner)
        def _():
            remote(g, a, za_s.at[u], za_r.at[u], at_rep(near)).wait_recv()
            two = local(a, vb.at[:, 0:n], zl.at[1])
            two.start()

            def clear():
                old = unit(u - SLOTS)
                past = pb.at[slot, :, 0:old[4]]
                remote(past, old[3], zc_s.at[u - SLOTS], zc_r.at[u - SLOTS], at_rep(near)).wait_send()
                local(past, old[3], zt.at[u - SLOTS]).wait()

            if not isinstance(u, int) or u >= SLOTS:
                clear()
            one = local(g, mine, zl.at[0])
            one.start()
            one.wait()
            two.wait()
            pb[slot, :, 0:n] = (
                pb[slot, :, 0:n].astype(f32) + vb[:, 0:n].astype(f32)
            ).astype(bf16)
            remote(mine, b, zb_s.at[u], zb_r.at[u], at_rep(far)).start()

    def chain_c(u):
        g, a, b, t, n = unit(u)
        slot = u % SLOTS
        mine = pb.at[slot, :, 0:n]

        @pl.when(inner)
        def _():
            remote(mine, b, zb_s.at[u], zb_r.at[u], at_rep(far)).wait()
            two = local(b, vb.at[:, 0:n], zl.at[1])
            two.start()
            two.wait()
            pb[slot, :, 0:n] = (
                pb[slot, :, 0:n].astype(f32) + vb[:, 0:n].astype(f32)
            ).astype(bf16)
            remote(mine, t, zc_s.at[u], zc_r.at[u], at_rep(near)).start()
            local(mine, t, zt.at[u]).start()

    done = [0]

    def advance(count=1):
        for _ in range(count):
            u = done[0]
            if u < units:
                chain_b(u)
            if 0 < u <= units:
                chain_c(u - 1)
            done[0] = u + 1

    scale_in = math.sqrt(2.0 / math.pi)

    def hidden(i):
        cols = slice(i * tile, (i + 1) * tile)
        bias = bf_ref[:, cols]

        def step(rb, total):
            rows = span(rb, rows_home)
            u = dot(hn[rows, :], fc1[:, cols], ((1,), (0,))) + bias
            d = dot(gy[rows, :], fc2[cols, :], ((1,), (1,)))
            square = u * u
            t = jnp.tanh(scale_in * u * (1.0 + 0.044715 * square))
            a = 0.5 * u * (1.0 + t)
            slope = 0.5 * (1.0 + t) + 0.5 * u * (1.0 - t * t) * scale_in * (
                1.0 + 3 * 0.044715 * square
            )
            d = d * slope
            act[rows, cols] = a.astype(bf16)
            tt[0:tile, rows] = a.T.astype(bf16)
            low = d.astype(bf16)
            dup[rows, cols] = low
            tt[tile:2 * tile, rows] = d.T.astype(bf16)
            return total + jnp.sum(low.astype(f32), axis=0, keepdims=True)

        vec_f[:, cols] = lax.fori_loop(0, width // rows_home, step, jnp.zeros((1, tile), f32))

    def grad_fc2(i, slot):
        def step(cb, _):
            cols = span(cb, wide)
            gst[slot, :, cols] = dot(tt[0:tile, :], gy[:, cols], ((1,), (0,))).astype(bf16)
            return 0

        lax.fori_loop(0, width // wide, step, 0)
        local(gst.at[slot], grad.at[2 * i], st.at[slot]).start()

    def spread(slot, n, place, index):
        local(ast.at[slot, me, :, 0:n], place(me), g_own.at[slot]).start()
        for e in range(1, 8):
            d = flip(e)
            remote(ast.at[slot, d, :, 0:n], place(me), g_send.at[slot], g_recv.at[index],
                   at_shard(d)).start()

    def spread_sent(slot, n):
        block = ast.at[slot, 0:7, :, 0:n]
        local(block, block, g_send.at[slot]).wait()

    def spread_here(slot, n, place, block, index):
        local(ast.at[slot, me, :, 0:n], place(me), g_own.at[slot]).wait()
        local(block, block, g_recv.at[index]).wait()

    def fc1_place(i):
        return lambda q: grad.at[2 * i + 1, :, span(q, tile)]

    def grad_fc1(i, slot):
        if i >= 2:
            spread_sent(slot, tile)

        def step(db, _):
            g = dot(tt[tile:2 * tile, :], hn[:, span(db, rows_home)], ((1,), (0,)))
            ast[slot, db, :, 0:tile] = g.T.astype(bf16)
            return 0

        lax.fori_loop(0, width // rows_home, step, 0)
        spread(slot, tile, fc1_place(i), i)

    def fc1_here(i):
        spread_here(i % 2, tile, fc1_place(i), grad.at[2 * i + 1, :, 0:7 * tile], i)
        chain_a(4 * i + 2)
        chain_a(4 * i + 3)

    for i in range(TILES):
        block = fc1.at[0:7 * rows_home, pl.ds(i * tile, tile)]
        local(block, block, w_recv.at[i]).wait()
        hidden(i)
        if i:
            fc1_here(i - 1)
        if i >= 2:
            advance()
        grad_fc2(i, i % 2)
        grad_fc1(i, i % 2)
        local(gst.at[i % 2], grad.at[2 * i], st.at[i % 2]).wait()
        chain_a(4 * i)
        chain_a(4 * i + 1)
        if i:
            advance()
    block = wqkv.at[:, 0:7 * rows_home, :]
    local(block, block, w_recv.at[TILES]).wait()

    blocks = kid_ref.shape[2] // BLOCK
    packs = kid_ref.shape[0]
    cap = qkv.shape[3]
    scale = 1.0 / math.sqrt(HDIM)
    turn_by = ROT // 2
    lane = lax.broadcasted_iota(jnp.int32, (BLOCK, PAIR), 1)
    causal = lax.broadcasted_iota(jnp.int32, (BLOCK, BLOCK), 1) <= lax.broadcasted_iota(
        jnp.int32, (BLOCK, BLOCK), 0
    )
    zero = jnp.zeros((), bf16)

    def attend(it, first_unit):
        p, m = it // packs, it % packs
        fetch = local(tables.at[m], table, load.at[0])
        fetch.start()

        @pl.when(m == 0)
        def _():
            def project(sb, _):
                rows = span(sb, rows_home)
                r = dot(hn[rows, :], wqkv[p], ((1,), (0,))) + bq_ref[p]
                qkv[sb] = r.reshape(packs, blocks, cap, cols3)
                d = dot(gy[rows, :], dense[p], ((1,), (1,)))
                dout[sb] = d.astype(bf16).reshape(packs, blocks, cap, PAIR)
                return 0

            lax.fori_loop(0, width // rows_home, project, 0)
            vec_q[p] = jnp.zeros((1, cols3), f32)

        chain_b(first_unit)
        chain_c(first_unit - 1)
        fetch.wait()

        def rows_of(which, j):
            return qkv[:, m, j, :, which * PAIR:(which + 1) * PAIR].reshape(BLOCK, PAIR)

        def turn(x, j, back):
            here = slice(j * BLOCK, (j + 1) * BLOCK)
            other = jnp.where(
                lane % HDIM < turn_by, pltpu.roll(x, PAIR - turn_by, 1), pltpu.roll(x, turn_by, 1)
            ) * table[1, here, :]
            straight = x * table[0, here, :]
            return straight - other if back else straight + other

        for j in range(blocks):
            ks[j * BLOCK:(j + 1) * BLOCK, :] = turn(rows_of(1, j), j, False).astype(bf16)
            vs[j * BLOCK:(j + 1) * BLOCK, :] = rows_of(2, j).astype(bf16)
        dks[...] = jnp.zeros_like(dks)
        dvs[...] = jnp.zeros_like(dvs)
        first_head = lane < HDIM

        def put(ref, j, lanes, value):
            ref[p, :, m, j, :, lanes] = value.astype(bf16).reshape(width // rows_home, cap, PAIR)

        total_q = jnp.zeros((1, PAIR), f32)
        for j in range(blocks):
            first = max(0, j - MAXBLK + 1)
            keys_at = slice(first * BLOCK, (j + 1) * BLOCK)
            q_all = turn(rows_of(0, j), j, False).astype(bf16)
            do_all = dout[:, m, j, :, :].reshape(BLOCK, PAIR)
            keys, values = ks[keys_at, :], vs[keys_at, :]
            bias = jnp.where(kid_ref[m, :, keys_at] == begin_ref[m, j], 0.0, NEG)
            long = (j - first) * BLOCK
            outs, dqs = [], []
            for head in range(PAIR // HDIM):
                mine = first_head if head == 0 else jnp.logical_not(first_head)
                q = jnp.where(mine, q_all, zero)
                do = jnp.where(mine, do_all, zero)
                scores = dot(q, keys, ((1,), (1,))) * scale + bias
                tail = jnp.where(causal, scores[:, long:], NEG)
                scores = jnp.concatenate([scores[:, :long], tail], axis=1) if long else tail
                top = jnp.max(scores, axis=1, keepdims=True)
                expo = jnp.exp(scores - top)
                probs = expo * (1.0 / jnp.sum(expo, axis=1, keepdims=True))
                low_probs = probs.astype(bf16)
                outs.append(dot(low_probs, values, ((1,), (0,))))
                dprobs = dot(do, values, ((1,), (1,)))
                weighted = probs * dprobs
                delta = jnp.sum(weighted, axis=1, keepdims=True)
                dscores = (weighted - probs * delta).astype(bf16)
                dqs.append(dot(dscores, keys, ((1,), (0,))))
                dks[keys_at, :] += dot(dscores, q, ((0,), (0,)))
                dvs[keys_at, :] += dot(low_probs, do, ((0,), (0,)))
            put(ob, j, slice(0, PAIR), jnp.where(first_head, outs[0], outs[1]))
            dq = turn(jnp.where(first_head, dqs[0], dqs[1]) * scale, j, True)
            put(dqkv, j, slice(0, PAIR), dq)
            total_q += jnp.sum(dq.astype(bf16).astype(f32), axis=0, keepdims=True)
        total_k = jnp.zeros((1, PAIR), f32)
        total_v = jnp.zeros((1, PAIR), f32)
        for j in range(blocks):
            here = slice(j * BLOCK, (j + 1) * BLOCK)
            dk = turn(dks[here, :] * scale, j, True)
            dv = dvs[here, :]
            put(dqkv, j, slice(PAIR, 2 * PAIR), dk)
            put(dqkv, j, slice(2 * PAIR, 3 * PAIR), dv)
            total_k += jnp.sum(dk.astype(bf16).astype(f32), axis=0, keepdims=True)
            total_v += jnp.sum(dv.astype(bf16).astype(f32), axis=0, keepdims=True)
        vec_q[p] += jnp.concatenate([total_q, total_k, total_v], axis=1)
        chain_b(first_unit + 1)
        chain_c(first_unit)

    fc1_here(TILES - 1)
    start = done[0]

    def attend_step(it, _):
        attend(it, start + 2 * it)
        return 0

    lax.fori_loop(0, pairs * packs, attend_step, 0)
    done[0] = start + 2 * pairs * packs

    def qkv_place(p):
        return lambda q: gq.at[p, :, pl.ds(pl.multiple_of(q * cols3, PAIR), cols3)]

    dense_chunk = grad.shape[0] - 1
    for p in range(pairs):
        def turn_round(sb, _):
            cols = span(sb, rows_home)
            t = dqkv[p, sb].reshape(rows_home, cols3).astype(f32)
            tt[0:cols3, cols] = t.T.astype(bf16)
            o = ob[p, sb].reshape(rows_home, PAIR).astype(f32)
            tt[cols3:cols3 + PAIR, cols] = o.T.astype(bf16)
            return 0

        lax.fori_loop(0, width // rows_home, turn_round, 0)

        def step(cb, _):
            cols = span(cb, wide)
            gst[0, pl.ds(p * PAIR, PAIR), cols] = dot(
                tt[cols3:cols3 + PAIR, :], gy[:, cols], ((1,), (0,))
            ).astype(bf16)
            return 0

        lax.fori_loop(0, width // wide, step, 0)
        spread_sent(p % 2, tile)

        def step_qkv(db, _):
            g = dot(tt[0:cols3, :], hn[:, span(db, rows_home)], ((1,), (0,)))
            ast[p % 2, db, :, :] = g.T.astype(bf16)
            return 0

        lax.fori_loop(0, width // rows_home, step_qkv, 0)
        spread(p % 2, cols3, qkv_place(p), TILES + p)
        advance()
    local(gst.at[0], grad.at[dense_chunk], st.at[0]).start()
    local(gst.at[0], grad.at[dense_chunk], st.at[0]).wait()
    chain_a(2 * dense_chunk)
    chain_a(2 * dense_chunk + 1)
    for p in range(pairs):
        spread_here(p % 2, cols3, qkv_place(p), gq.at[p, :, 0:7 * cols3], TILES + p)
        chain_a(uniform + 2 * p)
        chain_a(uniform + 2 * p + 1)

    def part(which, q, cols):
        rows = span(q, rows_home)
        if which == 0:
            acc = dot(act[rows, :], fc2[:, cols], ((1,), (0,)))
            for p in range(pairs):
                acc += dot(ob[p, q].reshape(rows_home, PAIR), dense[p, :, cols], ((1,), (0,)))
            return acc
        acc = dot(dup[rows, :], fc1[cols, :], ((1,), (1,)))
        for p in range(pairs):
            acc += dot(dqkv[p, q].reshape(rows_home, cols3), wqkv[p, cols, :], ((1,), (1,)))
        return acc

    chips = part_in.shape[1]
    for which in range(2):
        def give(c, _):
            slot = c % 2

            @pl.when(c >= 2)
            def _():
                local(gst.at[slot], gst.at[slot], d_send.at[slot]).wait()

            def step(cb, _):
                cols = span(cb, wide)
                gst[slot, :, cols] = part(which, 2 * c + 1 - core, cols).astype(bf16)
                return 0

            lax.fori_loop(0, width // wide, step, 0)
            remote(gst.at[slot], part_in.at[which, c], d_send.at[slot],
                   p_recv.at[which * chips + c], at_shard(flip(1))).start()
            return 0

        lax.fori_loop(0, chips, give, 0)
        for slot in range(2):
            local(gst.at[slot], gst.at[slot], d_send.at[slot]).wait()
        advance()

    partner = tt.at[0:rows_home, :]
    for which in range(2):
        def chip_of(c):
            return ((cy + c // 2) % 2) * 2 + (cx + c % 2) % 2

        def total(c, slot):
            chip = chip_of(c)
            remote(gst.at[slot], part_in.at[which, chip], d_send.at[slot],
                   p_recv.at[which * chips + chip], at_shard(flip(1))).wait_recv()
            copy = local(part_in.at[which, chip], partner, load.at[0])
            copy.start()
            copy.wait()

            def step(cb, _):
                cols = span(cb, wide)
                gst[slot, :, cols] = (
                    part(which, 2 * chip + core, cols) + tt[0:rows_home, cols].astype(f32)
                ).astype(bf16)
                return 0

            lax.fori_loop(0, width // wide, step, 0)

        def keep(c, _):
            slot = c % 2

            @pl.when(c >= 3)
            def _():
                local(gst.at[slot], gst.at[slot], d_send.at[slot]).wait()

            total(c, slot)
            remote(gst.at[slot], home.at[which, c], d_send.at[slot],
                   h_recv.at[which * chips + c], at_shard(2 * chip_of(c) + core)).start()
            return 0

        lax.fori_loop(1, chips, keep, 0)
        local(gst.at[0], gst.at[0], d_send.at[0]).wait()
        total(0, 0)
        local(gst.at[0], home.at[which, 0], st.at[0]).start()
        local(gst.at[0], home.at[which, 0], st.at[0]).wait()
        local(gst.at[1], gst.at[1], d_send.at[1]).wait()
        advance()

    while done[0] <= units:
        advance()

    @pl.when(outer)
    def _():
        for u in range(units):
            g, a, b, t, _ = unit(u)
            remote(g, a, za_s.at[u], za_r.at[u], at_rep(near)).wait_send()
            remote(g, t, zc_s.at[u], zc_r.at[u], at_rep(near)).wait_recv()

    @pl.when(inner)
    def _():
        for u in range(units - SLOTS, units):
            g, a, b, t, n = unit(u)
            past = pb.at[u % SLOTS, :, 0:n]
            remote(past, t, zc_s.at[u], zc_r.at[u], at_rep(near)).wait_send()
            local(past, t, zt.at[u]).wait()

    for a in range(2):
        for n in range(7):
            buf = pairs_in[a][1]
            remote(own(buf, me), own(buf, me), ag_send.at[a, n], ag_recv.at[a, 1],
                   at_shard(flip(1))).wait_send()
    block = fc1.at[0:7 * rows_home, :]
    local(block, block, w_send.at[0]).wait()
    block = wqkv.at[:, 0:7 * rows_home, :]
    local(block, block, w_send.at[1]).wait()
    for p in range(pairs):
        spread_sent(p % 2, cols3)
    for which in range(2):
        for c in range(1, chips):
            remote(gst.at[0], home.at[which, c], d_send.at[0], h_recv.at[which * chips + c],
                   at_shard(flip(2))).wait_recv()


def fused(begins, key_id, bq, bf, turns, gy_home, hn_home, fc1_w, qkv_w, fc2_w, dense_w, group):
    bf16, f32 = jnp.bfloat16, jnp.float32
    rows, width = gy_home.shape
    ff = fc1_w.shape[1] // group
    tile = ff // TILES
    pairs = dense_w.shape[0]
    packs, blocks = begins.shape
    cap = rows // packs // blocks
    total = group * rows
    chips = group // 2
    units = 2 * (2 * TILES + 1) + 2 * pairs
    chunk = jax.ShapeDtypeStruct((2 * TILES + 1, rows, width), bf16)
    chunk_q = jax.ShapeDtypeStruct((pairs, rows, group * 3 * PAIR), bf16)
    parts = jax.ShapeDtypeStruct((2, chips, rows, width), bf16)
    out_shape = [chunk] * 4 + [chunk_q] * 4 + [parts] * 2 + [
        jax.ShapeDtypeStruct((1, ff), f32), jax.ShapeDtypeStruct((pairs, 1, 3 * PAIR), f32)
    ]
    vmem = pl.BlockSpec(memory_space=pltpu.VMEM)
    anywhere = pl.BlockSpec(memory_space=pl.ANY)
    dma = pltpu.SemaphoreType.DMA
    per = (group, packs, blocks, cap)
    pack_rows = blocks * BLOCK
    scratch = [
        pltpu.VMEM((total, width), bf16), pltpu.VMEM((total, width), bf16),
        pltpu.VMEM((width, ff), bf16), pltpu.VMEM((ff, width), bf16),
        pltpu.VMEM((pairs, width, 3 * PAIR), bf16), pltpu.VMEM((pairs, PAIR, width), bf16),
        pltpu.VMEM((total, ff), bf16), pltpu.VMEM((total, ff), bf16),
        pltpu.VMEM((pairs,) + per + (PAIR,), bf16), pltpu.VMEM((pairs,) + per + (3 * PAIR,), bf16),
        pltpu.VMEM(per + (3 * PAIR,), f32), pltpu.VMEM(per + (PAIR,), bf16),
        pltpu.VMEM((pack_rows, PAIR), bf16), pltpu.VMEM((pack_rows, PAIR), bf16),
        pltpu.VMEM((pack_rows, PAIR), f32), pltpu.VMEM((pack_rows, PAIR), f32),
        pltpu.VMEM((2 * tile, total), bf16),
        pltpu.VMEM((2, rows, width), bf16), pltpu.VMEM((2, group, rows, 3 * PAIR), bf16),
        pltpu.VMEM((SLOTS, rows // 2, group * 3 * PAIR), bf16),
        pltpu.VMEM((rows // 2, group * 3 * PAIR), bf16),
        pltpu.VMEM((2, pack_rows, PAIR), f32),
        dma((6,)), dma((2, 7)), dma((2, 8)), dma((2,)), dma((TILES + 1,)), dma((2,)), dma((2,)),
        dma((2,)), dma((TILES + pairs,)),
        dma((units,)), dma((units,)), dma((units,)), dma((units,)), dma((units,)), dma((units,)),
        dma((units,)), dma((2,)), dma((2,)), dma((2 * chips,)), dma((2 * chips,)),
    ]
    flops = 6 * total * (2 * width * ff + width * pairs * 4 * PAIR)
    return pl.pallas_call(
        fused_kernel,
        in_specs=[pl.BlockSpec(memory_space=pltpu.SMEM)] + [vmem] * 3 + [anywhere] * 7,
        out_specs=[anywhere] * 10 + [vmem] * 2,
        out_shape=out_shape,
        scratch_shapes=scratch,
        compiler_params=pltpu.CompilerParams(
            vmem_limit_bytes=60 << 20, collective_id=0, has_side_effects=True
        ),
        cost_estimate=pl.CostEstimate(
            flops=flops, bytes_accessed=64 << 20, transcendentals=total * ff
        ),
    )(begins, key_id, bq, bf, turns, gy_home, hn_home, fc1_w, qkv_w, fc2_w, dense_w)


def spread_layer(
    gy_home, hn_home, begins, key_id, qkv_weight, b_qkv, dense_weight, fc1_weight, b_fc1, fc2_weight
):
    bf16, f32 = jnp.bfloat16, jnp.float32
    group, reps = lax.axis_size("shard"), lax.axis_size("rep")
    width = gy_home.shape[1]
    rows = gy_home.shape[0] // MICRO
    cap = rows // group
    mine = width // group
    ff_mine = fc1_weight.shape[1] // group
    blocks = begins.shape[1]
    all_rows = MICRO * rows * group

    fc1 = lax.all_to_all(
        fc1_weight.reshape(mine, group, ff_mine).transpose(1, 0, 2), "shard", 0, 0, tiled=True
    ).reshape(width, ff_mine)
    w_qkv = lax.all_to_all(
        qkv_weight.reshape(mine, 3, group, mine).transpose(2, 0, 1, 3), "shard", 0, 0, tiled=True
    ).reshape(width, 3 * mine)

    gy = lax.all_gather(gy_home, "shard", axis=0, tiled=True)
    hn = lax.all_gather(hn_home, "shard", axis=0, tiled=True)

    upper = dot(hn, fc1, ((1,), (0,))) + b_fc1
    inner = math.sqrt(2.0 / math.pi) * (upper + 0.044715 * upper * upper * upper)
    curve = jnp.tanh(inner)
    act = (0.5 * upper * (1.0 + curve)).astype(bf16)
    slope = 0.5 * (1.0 + curve) + 0.5 * upper * (1.0 - curve * curve) * math.sqrt(
        2.0 / math.pi
    ) * (1.0 + 3 * 0.044715 * upper * upper)
    dup = (dot(gy, fc2_weight, ((1,), (1,))) * slope).astype(bf16)
    g_fc2 = dot(act, gy, ((0,), (0,)), f32).astype(bf16)
    g_fc1 = dot(hn, dup, ((0,), (0,)), f32).astype(bf16)

    def over_reps(part):
        return lax.psum_scatter(part, "rep", scatter_dimension=0, tiled=True)

    def from_reps(part):
        return lax.all_gather(part, "rep", axis=0, tiled=True)

    def by_rows(grad):
        cols = grad.shape[1]
        split = grad.reshape(group, reps, mine // reps, cols).transpose(1, 0, 2, 3)
        part = over_reps(split.reshape(reps * group, mine // reps, cols))
        part = lax.all_to_all(part, "shard", 0, 0, tiled=True)
        whole = from_reps(part)
        return whole.reshape(reps, group, mine // reps, cols)

    grad_fc2 = from_reps(over_reps(g_fc2)).astype(f32)
    grad_fc1 = by_rows(g_fc1).transpose(0, 2, 1, 3).reshape(mine, -1).astype(f32)

    qkv = dot(hn, w_qkv, ((1,), (0,))) + b_qkv
    dout = dot(gy, dense_weight, ((1,), (1,)))
    shape = (group, MICRO, blocks, cap)
    ob, dq, dk, dv = attention(
        begins, qkv.reshape(*shape, 3 * mine), dout.reshape(*shape, mine), key_id
    )
    ob = ob.reshape(all_rows, mine).astype(bf16)
    dqkv = jnp.concatenate(
        [part.reshape(all_rows, mine).astype(bf16) for part in (dq, dk, dv)], axis=1
    )
    g_qkv = dot(hn, dqkv, ((0,), (0,)), f32).astype(bf16)
    g_dense = dot(ob, gy, ((0,), (0,)), f32).astype(bf16)
    grad_dense = from_reps(over_reps(g_dense)).astype(f32)
    grad_qkv = by_rows(g_qkv).reshape(reps, group, mine // reps, 3, mine)
    grad_qkv = grad_qkv.transpose(0, 2, 3, 1, 4).reshape(mine, 3 * width).astype(f32)

    def home(part):
        got = lax.all_to_all(part.reshape(group, MICRO * rows, width), "shard", 0, 0, tiled=True)
        return jnp.sum(got.astype(f32), axis=0)

    out_part = (
        dot(act, fc2_weight, ((1,), (0,))) + dot(ob, dense_weight, ((1,), (0,)))
    ).astype(bf16)
    dh_part = (dot(dqkv, w_qkv, ((1,), (1,))) + dot(dup, fc1, ((1,), (1,)))).astype(bf16)
    v_qkv = jnp.sum(dqkv.astype(f32), axis=0).reshape(3, mine)
    v_fc1 = jnp.sum(dup.astype(f32), axis=0)
    return (
        home(out_part), home(dh_part), grad_qkv, grad_dense, grad_fc1, grad_fc2, v_qkv, v_fc1
    )


def fused_layer(
    gy_home, hn_home, begins, key_id, qkv_weight, b_qkv, dense_weight, fc1_weight, b_fc1, fc2_weight
):
    f32 = jnp.float32
    group = lax.axis_size("shard")
    width = gy_home.shape[1]
    mine = width // group
    pairs = mine // PAIR
    ff_mine = fc1_weight.shape[1] // group
    tile = ff_mine // TILES
    qkv_w = qkv_weight.reshape(mine, 3, group, pairs, PAIR).transpose(2, 3, 0, 1, 4)
    bq = b_qkv.reshape(3, pairs, PAIR).transpose(1, 0, 2).reshape(pairs, 1, 3 * PAIR)
    blocks = begins.shape[1]
    index = jnp.arange(blocks, dtype=jnp.int32)
    offset = index[None, :] - begins
    pick = (offset[:, :, None] == jnp.arange(MAXBLK, dtype=jnp.int32)[None, None, :]).astype(f32)
    turns = jnp.einsum(
        "mjo,tox->mtjx", pick, jnp.stack(rotary_tables()).reshape(2, MAXBLK, BLOCK * PAIR),
        precision=lax.Precision.HIGHEST,
    ).reshape(begins.shape[0], 2, blocks * BLOCK, PAIR)
    outs = fused(
        begins, key_id, bq, b_fc1.reshape(1, ff_mine), turns, gy_home, hn_home, fc1_weight,
        qkv_w.reshape(group, pairs, mine, 3 * PAIR), fc2_weight,
        dense_weight.reshape(pairs, PAIR, width), group,
    )
    grad_t, gq_t, home, vec_f, vec_q = outs[3], outs[7], outs[9], outs[10], outs[11]
    grad_fc2 = grad_t[0:2 * TILES:2].reshape(ff_mine, width).astype(f32)
    grad_fc1 = grad_t[1:2 * TILES:2].reshape(TILES, mine, group, tile).transpose(1, 2, 0, 3)
    grad_fc1 = grad_fc1.reshape(mine, group * ff_mine).astype(f32)
    grad_dense = grad_t[2 * TILES].astype(f32)
    grad_qkv = gq_t.reshape(pairs, mine, group, 3, PAIR).transpose(1, 3, 2, 0, 4)
    grad_qkv = grad_qkv.reshape(mine, 3 * width).astype(f32)
    v_qkv = vec_q.reshape(pairs, 3, PAIR).transpose(1, 0, 2).reshape(3, mine)
    sums = jnp.sum(home.astype(f32), axis=1)
    return sums[0], sums[1], grad_qkv, grad_dense, grad_fc1, grad_fc2, v_qkv, vec_f.reshape(-1)


def body(
    tokens, cotangent, placement_order, seq_lengths, ln_gain, ln_bias, qkv_weight, qkv_bias,
    dense_weight, dense_bias, fc1_weight, fc1_bias, fc2_weight, fc2_bias,
):
    bf16, f32 = jnp.bfloat16, jnp.float32
    group = lax.axis_size("shard")
    reps = lax.axis_size("rep")
    me = lax.axis_index("shard")
    width = tokens.shape[1]
    rows = tokens.shape[0] // MICRO
    cap = rows // group
    mine = width // group
    ff_mine = fc1_weight.shape[1] // group
    blocks = seq_lengths.shape[2]
    all_rows = MICRO * rows * group

    pieces = (ln_gain, ln_bias, dense_bias, fc2_bias, qkv_bias, fc1_bias)
    packed = jnp.concatenate(pieces)
    spread = lax.all_gather(packed, "shard", axis=0).astype(f32)
    full, at = [], 0
    for piece in pieces:
        full.append(spread[:, at:at + piece.shape[0]].reshape(-1))
        at += piece.shape[0]
    gain, lnb, b_dense, b_fc2, b_qkv, b_fc1 = full
    b_qkv = lax.dynamic_slice_in_dim(b_qkv.reshape(3, width), me * mine, mine, 1).reshape(-1)
    b_fc1 = lax.dynamic_slice_in_dim(b_fc1, me * ff_mine, ff_mine, 0)

    begins, limits = block_begins(seq_lengths[0])
    spot = jnp.arange(BLOCK, dtype=jnp.int32)
    index = jnp.arange(blocks, dtype=jnp.int32)
    position = (index[None, :, None] - begins[:, :, None]) * BLOCK + spot[None, None, :]
    valid = position < limits[:, :, None]
    key_id = jnp.where(valid, begins[:, :, None], -1).reshape(MICRO, 1, blocks * BLOCK)

    orders = placement_order[0, 0]
    select = (orders[:, None, :] == jnp.arange(rows, dtype=jnp.int32)[None, :, None]).astype(bf16)

    def arrange(array):
        return jnp.einsum(
            "mti,mid->mtd", select, array.reshape(MICRO, rows, width),
            preferred_element_type=f32,
        ).astype(bf16).reshape(MICRO * rows, width)

    x_home, g_home = arrange(tokens), arrange(cotangent)
    valid_home = lax.dynamic_index_in_dim(
        valid.reshape(MICRO, group, group, cap), me, 2, keepdims=False
    ).reshape(MICRO * rows, 1)
    gy_home = jnp.where(valid_home, g_home, jnp.zeros((), bf16))
    x32 = x_home.astype(f32)
    centered = x32 - jnp.mean(x32, axis=1, keepdims=True)
    rstd = lax.rsqrt(jnp.mean(centered * centered, axis=1, keepdims=True) + 1e-05)
    hn_home = (centered * rstd * gain + lnb).astype(bf16)
    split = (
        gy_home, hn_home, begins, key_id, qkv_weight, b_qkv, dense_weight, fc1_weight, b_fc1,
        fc2_weight,
    )
    held = 2 * MICRO * rows * group * (2 * width + 2 * ff_mine + 7 * mine)
    held += 2 * width * (2 * ff_mine + 4 * mine)
    if (group, reps) == (8, 4) and cap % 16 == 0 and held <= FUSED_BYTES:
        result = fused_layer(*split)
    else:
        result = spread_layer(*split)
    out_sum, dh, grad_qkv, grad_dense, grad_fc1, grad_fc2, v_qkv, v_fc1 = result
    branch = out_sum + (b_dense + b_fc2)
    mixed = (x32 + jnp.where(valid_home, branch, 0.0)).astype(bf16)
    xhat = centered * rstd
    scaled = dh * gain
    dx = (
        scaled
        - jnp.mean(scaled, axis=1, keepdims=True)
        - xhat * jnp.mean(scaled * xhat, axis=1, keepdims=True)
    ) * rstd
    token_grad = (g_home.astype(f32) + dx).astype(bf16)

    def back(array):
        return jnp.einsum(
            "mti,mtd->mid", select, array.reshape(MICRO, rows, width),
            preferred_element_type=f32,
        ).astype(bf16).reshape(MICRO * rows, width)

    v_out = jnp.sum(gy_home.astype(f32), axis=0)
    v_gain = jnp.sum(dh * xhat, axis=0)
    v_lnb = jnp.sum(dh, axis=0)
    mixed_vec = jnp.concatenate([v_qkv.reshape(-1), v_fc1, v_out, v_gain, v_lnb])
    table = lax.all_gather(mixed_vec, ("rep", "shard"), axis=0).reshape(reps, group, -1)
    table = jnp.sum(table, axis=0)
    at = 3 * mine
    bias_qkv = table[:, :at].reshape(group, 3, mine).transpose(1, 0, 2).reshape(-1)
    bias_qkv = lax.dynamic_slice_in_dim(bias_qkv, me * 3 * mine, 3 * mine, 0)
    bias_fc1 = lax.dynamic_index_in_dim(table[:, at:at + ff_mine], me, 0, keepdims=False)
    full = jnp.sum(table[:, at + ff_mine:], axis=0).reshape(3, group, mine)
    bias_out, gain_grad, lnb_grad = lax.dynamic_index_in_dim(full, me, 1, keepdims=False)
    return (
        back(mixed), back(token_grad), gain_grad, lnb_grad, grad_qkv, bias_qkv, grad_dense,
        bias_out, grad_fc1, bias_fc1, grad_fc2, bias_out,
    )


def solution(mesh):
    rows = P(("rep", "shard"), None)
    vector, matrix = P("shard"), P("shard", None)
    layer = (vector, vector, matrix, vector, matrix, vector, matrix, vector, matrix, vector)
    return jax.shard_map(
        body,
        mesh=mesh,
        in_specs=(rows, rows, P("rep", "shard", None, None), P("rep", None, None)) + layer,
        out_specs=(rows, rows) + layer,
        check_vma=False,
    )
```

```python
import math

import jax
import jax.numpy as jnp
import numpy as np
from jax import lax
from jax.experimental import pallas as pl
from jax.experimental.pallas import tpu as pltpu
from jax.sharding import PartitionSpec as P

HEADS = 32
HDIM = 64
ROT = 32
BLOCK = 128
MICRO = 2
MAXBLK = 8
PAIR = 2 * HDIM
NEG = -1e30
FUSED_BYTES = 48 << 20


def dot(left, right, dims, out=jnp.float32):
    return lax.dot_general(left, right, (dims, ((), ())), preferred_element_type=out)


def block_begins(lengths):
    blocks = jnp.arange(lengths.shape[1], dtype=jnp.int32)
    started = (lengths[:, None, :] > 0) & (blocks[None, None, :] <= blocks[None, :, None])
    begins = jnp.max(jnp.where(started, blocks[None, None, :], 0), axis=2)
    own = begins[:, :, None] == blocks[None, None, :]
    limits = jnp.sum(jnp.where(own, lengths[:, None, :], 0), axis=2)
    return begins, limits


def rotary_tables():
    half = ROT // 2
    lane = np.arange(PAIR) % HDIM
    freqs = np.exp(-math.log(10000.0) * np.arange(half) * 2.0 / ROT).astype(np.float32)
    position = np.arange(MAXBLK * BLOCK, dtype=np.float32)
    angles = (position[:, None] * freqs[lane % half][None, :]).astype(np.float64)
    sines = np.sin(angles)
    cosine = np.where(lane < ROT, np.cos(angles), 1.0)
    signed = np.where(lane < half, -sines, np.where(lane < ROT, sines, 0.0))
    return [jnp.asarray(t.astype(np.float32)) for t in (cosine, signed)]


def attention_kernel(begin_ref, q_ref, k_ref, v_ref, do_ref, cos_ref, sin_ref, kid_ref,
                     ob_ref, dq_ref, dk_ref, dv_ref, ks, vs, dks, dvs):
    micro = pl.program_id(0)
    blocks = q_ref.shape[1]
    lane = lax.broadcasted_iota(jnp.int32, (BLOCK, PAIR), 1)
    half = ROT // 2

    def rows(ref, j):
        return ref[:, j].reshape(BLOCK, PAIR)

    def table(ref, j):
        return ref[pl.ds(pl.multiple_of((j - begin_ref[micro, j]) * BLOCK, BLOCK), BLOCK), :]

    def turn(x, j, back):
        other = jnp.where(
            lane % HDIM < half, pltpu.roll(x, PAIR - half, 1), pltpu.roll(x, half, 1)
        ) * table(sin_ref, j)
        straight = x * table(cos_ref, j)
        return straight - other if back else straight + other

    for j in range(blocks):
        ks[j * BLOCK:(j + 1) * BLOCK, :] = turn(rows(k_ref, j), j, False).astype(jnp.bfloat16)
        vs[j * BLOCK:(j + 1) * BLOCK, :] = rows(v_ref, j).astype(jnp.bfloat16)
    dks[...] = jnp.zeros_like(dks)
    dvs[...] = jnp.zeros_like(dvs)
    causal = lax.broadcasted_iota(jnp.int32, (BLOCK, BLOCK), 1) <= lax.broadcasted_iota(
        jnp.int32, (BLOCK, BLOCK), 0
    )
    scale = 1.0 / math.sqrt(HDIM)
    zero = jnp.zeros((), jnp.bfloat16)
    for j in range(blocks):
        first = max(0, j - MAXBLK + 1)
        span = slice(first * BLOCK, (j + 1) * BLOCK)
        q_all = turn(rows(q_ref, j), j, False).astype(jnp.bfloat16)
        do_all = rows(do_ref, j).astype(jnp.bfloat16)
        keys, values = ks[span, :], vs[span, :]
        same = kid_ref[:, span] == begin_ref[micro, j]
        bias = jnp.where(same, 0.0, NEG)
        width = (j + 1 - first) * BLOCK
        outs, dqs = [], []
        for head in range(PAIR // HDIM):
            mine = (lane >= head * HDIM) & (lane < (head + 1) * HDIM)
            q = jnp.where(mine, q_all, zero)
            do = jnp.where(mine, do_all, zero)
            scores = dot(q, keys, ((1,), (1,))) * scale + bias
            tail = jnp.where(causal, scores[:, width - BLOCK:], NEG)
            if width > BLOCK:
                scores = jnp.concatenate([scores[:, :width - BLOCK], tail], axis=1)
            else:
                scores = tail
            top = jnp.max(scores, axis=1, keepdims=True)
            expo = jnp.exp(scores - top)
            probs = expo / jnp.sum(expo, axis=1, keepdims=True)
            low_probs = probs.astype(jnp.bfloat16)
            outs.append(dot(low_probs, values, ((1,), (0,))))
            dprobs = dot(do, values, ((1,), (1,)))
            weighted = probs * dprobs
            delta = jnp.sum(weighted, axis=1, keepdims=True)
            dscores = (weighted - probs * delta).astype(jnp.bfloat16)
            dqs.append(dot(dscores, keys, ((1,), (0,))))
            dks[span, :] += dot(dscores, q, ((0,), (0,)))
            dvs[span, :] += dot(low_probs, do, ((0,), (0,)))
        first_head = lane < HDIM
        shape = (q_ref.shape[0], q_ref.shape[2], PAIR)
        ob = jnp.where(first_head, outs[0], outs[1])
        ob_ref[:, j] = ob.astype(jnp.bfloat16).astype(jnp.float32).reshape(shape)
        dq = turn(jnp.where(first_head, dqs[0], dqs[1]) * scale, j, True)
        dq_ref[:, j] = dq.astype(jnp.bfloat16).astype(jnp.float32).reshape(shape)
    for j in range(blocks):
        here = slice(j * BLOCK, (j + 1) * BLOCK)
        shape = (q_ref.shape[0], q_ref.shape[2], PAIR)
        dk = turn(dks[here, :] * scale, j, True)
        dk_ref[:, j] = dk.astype(jnp.bfloat16).astype(jnp.float32).reshape(shape)
        dv_ref[:, j] = dvs[here, :].astype(jnp.bfloat16).astype(jnp.float32).reshape(shape)


def attention(begins, qkv, dout, kid):
    group, micros, blocks, cap, _ = qkv.shape
    width = dout.shape[-1]
    pairs = width // PAIR
    total = blocks * BLOCK

    def rows_spec(offset):
        return pl.BlockSpec(
            (group, None, blocks, cap, PAIR), lambda m, p, *_: (0, m, 0, 0, offset + p)
        )

    table_spec = pl.BlockSpec((MAXBLK * BLOCK, PAIR), lambda m, p, *_: (0, 0))
    out = jax.ShapeDtypeStruct(dout.shape, jnp.float32)
    work = micros * pairs * 2 * blocks * (min(blocks, MAXBLK) + 1) // 2 * BLOCK * BLOCK
    return pl.pallas_call(
        attention_kernel,
        grid_spec=pltpu.PrefetchScalarGridSpec(
            num_scalar_prefetch=1,
            grid=(micros, pairs),
            in_specs=[
                rows_spec(0), rows_spec(pairs), rows_spec(2 * pairs), rows_spec(0),
                table_spec, table_spec,
                pl.BlockSpec((None, 1, total), lambda m, p, *_: (m, 0, 0)),
            ],
            out_specs=[rows_spec(0)] * 4,
            scratch_shapes=[
                pltpu.VMEM((total, PAIR), jnp.bfloat16),
                pltpu.VMEM((total, PAIR), jnp.bfloat16),
                pltpu.VMEM((total, PAIR), jnp.float32),
                pltpu.VMEM((total, PAIR), jnp.float32),
            ],
        ),
        out_shape=[out] * 4,
        compiler_params=pltpu.CompilerParams(vmem_limit_bytes=48 << 20),
        cost_estimate=pl.CostEstimate(
            flops=12 * work * PAIR, bytes_accessed=8 * dout.size * 4, transcendentals=work
        ),
    )(begins, qkv, qkv, qkv, dout, *rotary_tables(), kid)


MESH = pl.DeviceIdType.MESH
SLOTS = 4
TILES = 4
VROWS = 16
HOLD = 4
WAIT = 5
STAGES = 3


def fused_kernel(
    begin_ref, kid_ref, base_ref, turn_ref, select_ref, valid_ref, vec_in,
    tokens, cotangent, fc1_w, qkv_w, fc2_w, dense_w,
    grad, grad_a, grad_b, grad_t, part_in, home, mid_in, mixed_out, token_out, vec_out,
    gy, hn, fc1, fc2, wqkv, dense, act, dup, ob, dqkv, qkv, dout, ks, vs, dks, dvs, tt, gst, ast,
    pb, va, vb, vecs, full, sums, vsend, vgot, zgot, bq_row,
    load, ag_send, ag_recv, w_send, w_recv, x_send, x_recv, st, g_send, g_own, g_recv, za_s, za_r, zb_s, zb_r, zc_s,
    zc_r, zt, zl, d_send, p_recv, h_recv, k_send, m_recv, v_send, v_recv,
):
    bf16, f32 = jnp.bfloat16, jnp.float32
    me, rep = lax.axis_index("shard"), lax.axis_index("rep")
    core, cx, cy = me % 2, (me // 2) % 2, me // 4
    near = rep + 1 - 2 * (rep % 2)
    far = 3 - rep
    inner = (rep == 1) | (rep == 2)
    outer = (rep == 0) | (rep == 3)
    rows_home = tokens.shape[0]
    width = tokens.shape[1]
    group = width // rows_home
    ff = fc1.shape[1]
    tile = ff // TILES
    wide = 512
    packs = kid_ref.shape[0]
    pack_rows = rows_home // packs
    blocks = kid_ref.shape[2] // BLOCK
    cap = qkv.shape[3]
    pairs = rows_home // PAIR
    kinds = 3

    def flip(e):
        return ((cy + e // 4) % 2) * 4 + ((cx + (e // 2) % 2) % 2) * 2 + (core + e % 2) % 2

    def at_shard(d):
        return {"shard": d}

    def at_rep(d):
        return {"rep": d}

    def remote(src, dst, send, recv, dev):
        return pltpu.make_async_remote_copy(
            src_ref=src, dst_ref=dst, send_sem=send, recv_sem=recv, device_id=dev,
            device_id_type=MESH,
        )

    def local(src, dst, sem):
        return pltpu.make_async_copy(src, dst, sem)

    def span(i, size):
        return pl.ds(pl.multiple_of(i * size, size), size)

    def own(ref, q):
        return ref.at[span(q, rows_home), :]

    def loop(count, step):
        def run(i, _):
            step(i)
            return 0

        lax.fori_loop(0, count, run, 0)

    first_loads = [
        local(cotangent, gst.at[1], load.at[1]),
        local(tokens, gst.at[0], load.at[0]),
    ]
    loads = [
        local(fc1_w.at[:, span(me, ff)], own(fc1, me), load.at[2]),
        local(fc2_w, fc2, load.at[3]),
        local(dense_w, dense, load.at[4]),
        local(vec_in, vecs.at[me], load.at[5]),
    ] + [
        local(
            qkv_w.at[:, span(kind * group + me, rows_home)],
            wqkv.at[span(me, rows_home), pl.ds(kind * rows_home, rows_home)], load.at[6 + kind],
        )
        for kind in range(kinds)
    ]
    for copy in first_loads + loads:
        copy.start()

    barrier = pltpu.get_barrier_semaphore()
    for e in range(1, 8):
        pl.semaphore_signal(barrier, inc=1, device_id=at_shard(flip(e)), device_id_type=MESH)
    for z in range(1, 4):
        pl.semaphore_signal(
            barrier, inc=1, device_id=at_rep((rep + z) % 4), device_id_type=MESH
        )
    pl.semaphore_wait(barrier, 10)

    for e in range(1, 8):
        remote(vec_in, vecs.at[me], v_send.at[0], v_recv.at[0], at_shard(flip(e))).start()
    buffers = (gy, hn)

    def send_own(a):
        buf = buffers[a]
        for n, e in enumerate((2, 4, 1)):
            remote(own(buf, me), own(buf, me), ag_send.at[a, n], ag_recv.at[a, e],
                   at_shard(flip(e))).start()

    def chip_of(c):
        return ((cy + c // 2) % 2) * 2 + (cx + c % 2) % 2

    def in_plane():
        return [2 * chip_of(c) + (core + rep) % 2 for c in (1, 2, 3)]

    def send_fc1(i):
        for d in [flip(1)] + in_plane():
            remote(
                fc1_w.at[:, pl.ds(pl.multiple_of(d * ff + i * tile, tile), tile)],
                fc1.at[span(me, rows_home), pl.ds(i * tile, tile)],
                w_send.at[0], w_recv.at[i], at_shard(d),
            ).start()

    def send_qkv():
        for e in range(1, 8):
            d = flip(e)
            for kind in range(kinds):
                remote(
                    qkv_w.at[:, span(kind * group + d, rows_home)],
                    wqkv.at[span(me, rows_home), pl.ds(kind * rows_home, rows_home)],
                    w_send.at[1], w_recv.at[TILES], at_shard(d),
                ).start()

    def fc1_part(i, count, sem):
        block = fc1.at[0:count * rows_home, pl.ds(i * tile, tile)]
        return local(block, block, sem)

    def pass_on(i):
        fc1_part(i, 4, w_recv.at[i]).wait()
        for q in in_plane():
            block = fc1.at[span(q, rows_home), pl.ds(i * tile, tile)]
            remote(block, block, x_send.at[0], x_recv.at[i], at_rep(near)).start()

    def ag_wait(a, e):
        buf = buffers[a]
        remote(own(buf, me), own(buf, flip(e)), ag_send.at[a, 0], ag_recv.at[a, e],
               at_shard(flip(e))).wait_recv()

    def forward(a, have, to, n):
        q = own(buffers[a], flip(have))
        remote(q, q, ag_send.at[a, n], ag_recv.at[a, have ^ to], at_shard(flip(to))).start()

    def relay(a):
        ag_wait(a, 2)
        forward(a, 2, 1, 4)

        @pl.when(core == 0)
        def _():
            forward(a, 2, 4, 3)

        ag_wait(a, 4)
        forward(a, 4, 1, 5)

        @pl.when(core == 1)
        def _():
            forward(a, 4, 2, 3)

    def sort_rows(source, put):
        for m in range(packs):
            def step(cb):
                cols = span(cb, wide)
                put(m, cols, dot(
                    select_ref[m], gst[source, m * pack_rows:(m + 1) * pack_rows, cols],
                    ((1,), (0,)),
                ))

            loop(width // wide, step)

    def put_gy(m, cols, value):
        keep = valid_ref[m * pack_rows:(m + 1) * pack_rows, :]
        gy[pl.ds(pl.multiple_of(me * rows_home + m * pack_rows, pack_rows), pack_rows), cols] = (
            value * keep
        ).astype(bf16)

    def put_tt(first):
        def put(m, cols, value):
            tt[first + m * pack_rows:first + (m + 1) * pack_rows, cols] = value.astype(bf16)

        return put

    few = 32

    def statistics(x):
        centered = x - jnp.mean(x, axis=1, keepdims=True)
        rstd = lax.rsqrt(jnp.mean(centered * centered, axis=1, keepdims=True) + 1e-05)
        return centered * rstd, rstd

    for i in range(TILES):
        send_fc1(i)
    first_loads[0].wait()
    sort_rows(1, put_gy)
    send_own(0)
    first_loads[1].wait()
    sort_rows(0, put_tt(0))
    block = vecs.at[0:7]
    local(block, block, v_recv.at[0]).wait()
    for copy in loads:
        copy.wait()
    for q in range(group):
        cols = slice(q * rows_home, (q + 1) * rows_home)
        full[0:4, cols] = vecs[q, 0:4, :]
    for kind in range(kinds):
        piece = kind * group + me
        bq_row[0:1, kind * rows_home:(kind + 1) * rows_home] = vecs[
            piece // kinds, pl.ds(4 + piece % kinds, 1), :
        ]

    def norm_rows(rb):
        xhat, _ = statistics(tt[span(rb, few), :].astype(f32))
        hn[pl.ds(pl.multiple_of(me * rows_home + rb * few, few), few), :] = (
            xhat * full[0:1, :] + full[1:2, :]
        ).astype(bf16)

    loop(rows_home // few, norm_rows)
    send_own(1)
    for i in range(TILES):
        pass_on(i)
    for a in range(2):
        relay(a)
    send_qkv()
    for a in range(2):
        ag_wait(a, 6)
        forward(a, 6, 1, 6)
    for a in range(2):
        for e in (1, 3, 5, 7):
            ag_wait(a, e)

    half = rows_home // 2
    units = 2 * grad.shape[0]

    def unit(u):
        at = (u // 2, pl.ds(pl.multiple_of((u % 2) * half, half), half), slice(None))
        return [ref.at[at] for ref in (grad, grad_a, grad_b, grad_t)]

    def chain_a(chunk):
        @pl.when(outer)
        def _():
            for u in (2 * chunk, 2 * chunk + 1):
                g, a, _, _ = unit(u)
                remote(g, a, za_s.at[u], za_r.at[u], at_rep(near)).start()

    def add_into(slot, ref):
        few = 32

        def step(rb):
            rows = span(rb, few)
            pb[slot, rows, :] = (pb[slot, rows, :].astype(f32) + ref[rows, :].astype(f32)).astype(bf16)

        loop(half // few, step)

    def b_load(u):
        g, a, _, _ = unit(u)
        return local(g, pb.at[u % SLOTS], zl.at[0]), local(a, va, zl.at[1])

    def b_first(u):
        g, a, _, _ = unit(u)
        remote(g, a, za_s.at[u], za_r.at[u], at_rep(near)).wait_recv()

        def clear():
            t = unit(u - SLOTS)[3]
            past = pb.at[u % SLOTS]
            remote(past, t, zc_s.at[u - SLOTS], zc_r.at[u - SLOTS], at_rep(near)).wait_send()
            local(past, t, zt.at[u - SLOTS]).wait()

        if not isinstance(u, int):
            pl.when(u >= SLOTS)(clear)
        elif u >= SLOTS:
            clear()
        for copy in b_load(u):
            copy.start()

    def b_second(u):
        for copy in b_load(u):
            copy.wait()
        add_into(u % SLOTS, va)
        remote(pb.at[u % SLOTS], unit(u)[2], zb_s.at[u], zb_r.at[u], at_rep(far)).start()

    def c_first(u):
        b = unit(u)[2]
        remote(pb.at[u % SLOTS], b, zb_s.at[u], zb_r.at[u], at_rep(far)).wait_recv()
        local(b, vb, zl.at[2]).start()

    def c_second(u):
        slot = u % SLOTS
        _, _, b, t = unit(u)
        local(b, vb, zl.at[2]).wait()
        remote(pb.at[slot], b, zb_s.at[u], zb_r.at[u], at_rep(far)).wait_send()
        add_into(slot, vb)
        remote(pb.at[slot], t, zc_s.at[u], zc_r.at[u], at_rep(near)).start()
        local(pb.at[slot], t, zt.at[u]).start()

    def half_step(k, odd):
        def known(u):
            return not isinstance(u, int) or 0 <= u < units

        @pl.when(inner)
        def _():
            if odd:
                if known(k):
                    b_second(k)
                if known(k - 1):
                    c_first(k - 1)
            else:
                if known(k):
                    b_first(k)
                if known(k - 2):
                    c_second(k - 2)

    done = [0]
    last_half = 2 * (units + 1)

    def advance(count=1):
        for _ in range(count):
            if done[0] <= last_half:
                half_step(done[0] // 2, done[0] % 2)
                done[0] += 1

    scale_in = math.sqrt(2.0 / math.pi)

    def hidden(i):
        cols = slice(i * tile, (i + 1) * tile)
        bias = vec_in_rows[i]

        def step(rb, total):
            rows = span(rb, rows_home)
            u = dot(hn[rows, :], fc1[:, cols], ((1,), (0,))) + bias
            d = dot(gy[rows, :], fc2[cols, :], ((1,), (1,)))
            square = u * u
            t = jnp.tanh(scale_in * u * (1.0 + 0.044715 * square))
            a = 0.5 * u * (1.0 + t)
            slope = 0.5 * (1.0 + t) + 0.5 * u * (1.0 - t * t) * scale_in * (
                1.0 + 3 * 0.044715 * square
            )
            d = d * slope
            act[rows, cols] = a.astype(bf16)
            tt[0:tile, rows] = a.T.astype(bf16)
            low = d.astype(bf16)
            dup[rows, cols] = low
            tt[tile:2 * tile, rows] = d.T.astype(bf16)
            return total + jnp.sum(low.astype(f32), axis=0, keepdims=True)

        middle = lax.fori_loop(0, group // 2, step, jnp.zeros((1, tile), f32))
        if i:
            advance()
        sums[6 + i:7 + i, :] = lax.fori_loop(group // 2, group, step, middle)

    vec_in_rows = [vecs[me, 7 + i:8 + i, :] for i in range(TILES)]

    def grad_rows(first, height, slot, at):
        def step(cb):
            cols = span(cb, wide)
            gst[slot, at:at + height, cols] = dot(
                tt[first:first + height, :], gy[:, cols], ((1,), (0,))
            ).astype(bf16)

        loop(width // wide, step)

    def store_chunk(slot, chunk):
        return local(gst.at[slot], grad.at[chunk], st.at[slot])

    def place(chunk):
        return grad.at[chunk, :, span(me, rows_home)]

    def sent(slot):
        block = ast.at[slot, 0:7]
        local(block, block, g_send.at[slot]).wait()
        local(ast.at[slot, me], place(0), g_own.at[slot]).wait()

    def spread(first, slot, chunk):
        def step(db):
            g = dot(tt[first:first + rows_home, :], hn[:, span(db, rows_home)], ((1,), (0,)))
            ast[slot, db] = g.T.astype(bf16)

        loop(group, step)
        local(ast.at[slot, me], place(chunk), g_own.at[slot]).start()
        for e in range(1, 8):
            d = flip(e)
            remote(ast.at[slot, d], place(chunk), g_send.at[slot], g_recv.at[chunk],
                   at_shard(d)).start()

    def arrived(chunk):
        block = grad.at[chunk, :, 0:7 * rows_home]
        local(block, block, g_recv.at[chunk]).wait()
        chain_a(chunk)

    for i in range(TILES):
        fc1_part(i, 3, x_recv.at[i]).wait()
        hidden(i)
        if i:
            advance()
        grad_rows(0, tile, i % 2, 0)
        store_chunk(i % 2, i).start()
        store_chunk(i % 2, i).wait()
        chain_a(i)
        if i:
            advance()
        if i >= STAGES:
            sent(i % STAGES)
        spread(tile, i % STAGES, TILES + i)
        if i:
            advance()

    block = wqkv.at[0:7 * rows_home, :]
    local(block, block, w_recv.at[TILES]).wait()
    turn_by = ROT // 2

    def rotated(x, cosine, signed, low_half):
        other = jnp.where(
            low_half, pltpu.roll(x, x.shape[-1] - turn_by, x.ndim - 1),
            pltpu.roll(x, turn_by, x.ndim - 1),
        )
        return x * cosine + other * signed

    def project(sb):
        rows = span(sb, rows_home)
        tall = (packs, blocks, cap, PAIR)
        spots = pl.ds(pl.multiple_of(sb * cap, cap), cap)
        base_c, base_s = base_ref[0, spots, :], base_ref[1, spots, :]
        lane = lax.broadcasted_iota(jnp.int32, (rows_home, PAIR), 1)
        low_half = lane % HDIM < turn_by
        plain = lane % HDIM >= ROT
        parts_c, parts_s = [], []
        for m in range(packs):
            for t in range(blocks):
                row_c, row_s = turn_ref[m, t, 0:1, :], turn_ref[m, t, 1:2, :]
                parts_c.append(base_c * row_c - base_s * row_s)
                parts_s.append(base_s * row_c + base_c * row_s)
        cosine = jnp.where(plain, 1.0, jnp.concatenate(parts_c, axis=0))
        sine = jnp.concatenate(parts_s, axis=0)
        signed = jnp.where(plain, 0.0, jnp.where(low_half, -sine, sine))
        for kind in range(kinds):
            cols = slice(kind * rows_home, (kind + 1) * rows_home)
            r = dot(hn[rows, :], wqkv[:, cols], ((1,), (0,))) + bq_row[0:1, cols]
            for p in range(pairs):
                x = r[:, p * PAIR:(p + 1) * PAIR]
                if kind < 2:
                    x = rotated(x, cosine, signed, low_half)
                qkv[sb, :, :, :, kind * rows_home + p * PAIR:kind * rows_home + (p + 1) * PAIR] = (
                    x.astype(bf16).reshape(tall)
                )
        d = dot(gy[rows, :], dense[...], ((1,), (1,)))
        dout[sb] = d.astype(bf16).reshape(packs, blocks, cap, rows_home)

    loop(group // 2, project)
    advance()
    loop_tail = group // 2

    def project_tail(sb):
        project(sb + loop_tail)

    loop(group - loop_tail, project_tail)
    advance()
    sent(1)
    sent(2)
    for n in range(3):
        arrived(TILES + n)

    scale = 1.0 / math.sqrt(HDIM)
    lane = lax.broadcasted_iota(jnp.int32, (BLOCK, PAIR), 1)
    causal = lax.broadcasted_iota(jnp.int32, (BLOCK, BLOCK), 1) <= lax.broadcasted_iota(
        jnp.int32, (BLOCK, BLOCK), 0
    )
    zero = jnp.zeros((), bf16)
    first_head = lane < HDIM
    low_half = lane % HDIM < turn_by
    plain = lane % HDIM >= ROT

    def attend(p, m, steps):
        def lanes(kind):
            return pl.ds(pl.multiple_of(kind * rows_home + p * PAIR, PAIR), PAIR)

        def rows_of(kind, j):
            return qkv[:, m, j, :, lanes(kind)].reshape(BLOCK, PAIR)

        def turn_back(x, j):
            row_c, row_s = turn_ref[m, j, 0:1, :], turn_ref[m, j, 1:2, :]
            cosine = jnp.where(plain, 1.0, base_ref[0] * row_c - base_ref[1] * row_s)
            sine = base_ref[1] * row_c + base_ref[0] * row_s
            signed = jnp.where(plain, 0.0, jnp.where(low_half, sine, -sine))
            return rotated(x, cosine, signed, low_half)

        for j in range(blocks):
            ks[j * BLOCK:(j + 1) * BLOCK, :] = rows_of(1, j)
            vs[j * BLOCK:(j + 1) * BLOCK, :] = rows_of(2, j)
        dks[...] = jnp.zeros_like(dks)
        dvs[...] = jnp.zeros_like(dvs)

        def put(ref, j, kind, value):
            ref[:, m, j, :, lanes(kind)] = value.reshape(group, cap, PAIR)

        def summed(value):
            return jnp.sum(value.astype(f32), axis=0, keepdims=True)

        total_q = jnp.zeros((1, PAIR), f32)
        for j in range(blocks):
            first = max(0, j - MAXBLK + 1)
            keys_at = slice(first * BLOCK, (j + 1) * BLOCK)
            q_all = rows_of(0, j)
            do_all = dout[:, m, j, :, pl.ds(pl.multiple_of(p * PAIR, PAIR), PAIR)].reshape(BLOCK, PAIR)
            keys, values = ks[keys_at, :], vs[keys_at, :]
            bias = jnp.where(kid_ref[m, :, keys_at] == begin_ref[m, j], 0.0, NEG)
            long = (j - first) * BLOCK
            outs, dqs = [], []
            for head in range(PAIR // HDIM):
                mine = first_head if head == 0 else jnp.logical_not(first_head)
                q = jnp.where(mine, q_all, zero)
                do = jnp.where(mine, do_all, zero)
                scores = dot(q, keys, ((1,), (1,))) * scale + bias
                tail = jnp.where(causal, scores[:, long:], NEG)
                scores = jnp.concatenate([scores[:, :long], tail], axis=1) if long else tail
                top = jnp.max(scores, axis=1, keepdims=True)
                expo = jnp.exp(scores - top)
                probs = expo * (1.0 / jnp.sum(expo, axis=1, keepdims=True))
                low_probs = probs.astype(bf16)
                outs.append(dot(low_probs, values, ((1,), (0,))))
                dprobs = dot(do, values, ((1,), (1,)))
                weighted = probs * dprobs
                delta = jnp.sum(weighted, axis=1, keepdims=True)
                dscores = (weighted - probs * delta).astype(bf16)
                dqs.append(dot(dscores, keys, ((1,), (0,))))
                dks[keys_at, :] += dot(dscores, q, ((0,), (0,)))
                dvs[keys_at, :] += dot(low_probs, do, ((0,), (0,)))
            put(ob, j, 0, jnp.where(first_head, outs[0], outs[1]).astype(bf16))
            dq = turn_back(jnp.where(first_head, dqs[0], dqs[1]) * scale, j).astype(bf16)
            put(dqkv, j, 0, dq)
            total_q += summed(dq)
            if j in (3, 5):
                half_step(*steps[j // 4])
        total_k = jnp.zeros((1, PAIR), f32)
        total_v = jnp.zeros((1, PAIR), f32)
        for j in range(blocks):
            here = slice(j * BLOCK, (j + 1) * BLOCK)
            dk = turn_back(dks[here, :] * scale, j).astype(bf16)
            dv = dvs[here, :].astype(bf16)
            put(dqkv, j, 1, dk)
            put(dqkv, j, 2, dv)
            total_k += summed(dk)
            total_v += summed(dv)
        half_step(*steps[2])
        for kind, total in enumerate((total_q, total_k, total_v)):
            cols = pl.ds(pl.multiple_of(p * PAIR, PAIR), PAIR)
            past = sums[kind:kind + 1, cols] if m else 0.0
            sums[kind:kind + 1, cols] = past + total

    per = packs * 3
    if done[0] % 2:
        advance()
    start = done[0] // 2

    def attend_pair(p):
        for m in range(packs):
            steps = [(start + (per // 2) * p + (3 * m + n) // 2, (3 * m + n) % 2) for n in range(3)]
            attend(p, m, steps)

    loop(pairs, attend_pair)
    done[0] += per * pairs

    dense_chunk = 2 * TILES

    def turn_round(source, first, kind):
        def step(sb):
            lanes = slice(kind * rows_home, (kind + 1) * rows_home)
            t = source[sb, :, :, :, lanes].reshape(rows_home, rows_home).astype(f32)
            tt[first:first + rows_home, span(sb, rows_home)] = t.T.astype(bf16)

        loop(group, step)

    sent(0)
    arrived(TILES + 3)
    turn_round(ob, 0, 0)
    grad_rows(0, rows_home, 0, 0)
    store_chunk(0, dense_chunk).start()
    advance()
    for kind in range(kinds):
        turn_round(dqkv, (kind % 2) * rows_home, kind)
        spread((kind % 2) * rows_home, kind, dense_chunk + 1 + kind)
        advance()
    store_chunk(0, dense_chunk).wait()
    chain_a(dense_chunk)

    def part(which, q, cols):
        rows = span(q, rows_home)
        if which == 0:
            return dot(act[rows, :], fc2[:, cols], ((1,), (0,))) + dot(
                ob[q].reshape(rows_home, rows_home), dense[:, cols], ((1,), (0,))
            )
        return dot(dup[rows, :], fc1[cols, :], ((1,), (1,))) + dot(
            dqkv[q].reshape(rows_home, kinds * rows_home), wqkv[cols, :], ((1,), (1,))
        )

    chips = part_in.shape[1]

    def give(which, c):
        mine = own(hn, which * chips + c)
        rows = span(which * chips + c, rows_home)

        def step(cb):
            cols = span(cb, wide)
            hn[rows, cols] = part(which, 2 * c + 1 - core, cols).astype(bf16)

        loop(width // wide, step)
        remote(mine, part_in.at[which, c], d_send.at[which * chips + c],
               p_recv.at[which * chips + c], at_shard(flip(1))).start()

    for a in range(2):
        for n in range(7):
            buf = buffers[a]
            remote(own(buf, me), own(buf, me), ag_send.at[a, n], ag_recv.at[a, 1],
                   at_shard(flip(1))).wait_send()
    for which in range(2):
        for first in range(0, chips, 2):
            loop(2, lambda n: give(which, first + n))
            advance()
        sent(which)
        arrived(dense_chunk + 1 + which)
    sent(2)
    arrived(dense_chunk + 3)

    toward, across = 1 + core, 2 - core

    def total(which, c, n, extra):
        chip = chip_of(c)
        rows = span(which * chips + n, rows_home)
        block = part_in.at[which, chip]
        remote(block, block, d_send.at[0], p_recv.at[which * chips + chip],
               at_shard(flip(1))).wait_recv()
        copies = [local(block, tt.at[0:rows_home, :], load.at[0])]
        if extra:
            block = mid_in.at[which]
            remote(block, block, k_send.at[0], m_recv.at[which], at_shard(flip(2))).wait_recv()
            copies.append(local(block, tt.at[rows_home:2 * rows_home, :], load.at[1]))
        for copy in copies:
            copy.start()
        for copy in copies:
            copy.wait()

        def step(cb):
            cols = span(cb, wide)
            acc = part(which, 2 * chip + core, cols) + tt[0:rows_home, cols].astype(f32)
            if extra:
                acc = acc + tt[rows_home:2 * rows_home, cols].astype(f32)
            gy[rows, cols] = acc.astype(bf16)

        loop(width // wide, step)
        return own(gy, which * chips + n)

    def keep(which, c, n, target, recv, to):
        src = total(which, c, n, n == 2)
        if n == 3:
            local(src, target, k_send.at[which * chips + n]).start()
        else:
            remote(src, target, k_send.at[which * chips + n], recv,
                   at_shard(2 * chip_of(to) + core)).start()

    for which in range(2):
        keep(which, 3, 0, mid_in.at[which], m_recv.at[which], toward)
    advance()
    for which in range(2):
        keep(which, toward, 1, home.at[which, 1], h_recv.at[3 * which + 1], toward)
        advance()
    for which in range(2):
        keep(which, 0, 3, home.at[which, 0], None, 0)
    advance(WAIT)
    for which in range(2):
        keep(which, across, 2, home.at[which, 2], h_recv.at[3 * which + 2], across)
        advance()
    advance(HOLD)

    again = [local(tokens, gst.at[0], load.at[0]), local(cotangent, gst.at[1], load.at[1])]
    for copy in again:
        copy.start()
    again[0].wait()
    sort_rows(0, put_tt(0))
    again[1].wait()
    sort_rows(1, put_tt(rows_home))
    advance()
    for n in range(2 * chips):
        block = part_in.at[n // chips, n % chips]
        remote(block, block, d_send.at[n], p_recv.at[n], at_shard(flip(1))).wait_send()
    bring = []
    for which in range(2):
        block = home.at[which, 0]
        local(own(gy, which * chips + 3), block, k_send.at[which * chips + 3]).wait()
        for c in range(3):
            block = home.at[which, c]
            if c:
                remote(block, block, k_send.at[0], h_recv.at[3 * which + c],
                       at_shard(flip(2))).wait_recv()
            bring.append(local(block, own(hn, 3 * which + c), load.at[3 * which + c]))
            bring[-1].start()
    advance()
    for copy in bring:
        copy.wait()
    gain = full[0:1, :]
    out_bias = full[2:3, :] + full[3:4, :]
    full[8:16, :] = jnp.zeros((8, width), f32)

    def finish(rb):
        rows = span(rb, few)
        keep = valid_ref[rows, :]
        x = tt[rows, :].astype(f32)
        g = tt[pl.ds(pl.multiple_of(rows_home + rb * few, few), few), :].astype(f32)
        branch, dh = out_bias, 0.0
        for c in range(3):
            branch = branch + hn[pl.ds(pl.multiple_of(c * rows_home + rb * few, few), few), :].astype(f32)
            dh = dh + hn[
                pl.ds(pl.multiple_of((3 + c) * rows_home + rb * few, few), few), :
            ].astype(f32)
        gst[0, rows, :] = (x + branch * keep).astype(bf16)
        xhat, rstd = statistics(x)
        scaled = dh * gain
        dx = (
            scaled
            - jnp.mean(scaled, axis=1, keepdims=True)
            - xhat * jnp.mean(scaled * xhat, axis=1, keepdims=True)
        ) * rstd
        gst[1, rows, :] = (g + dx).astype(bf16)
        full[8:9, :] += jnp.sum(g * keep, axis=0, keepdims=True)
        full[9:10, :] += jnp.sum(dh * xhat, axis=0, keepdims=True)
        full[10:11, :] += jnp.sum(dh, axis=0, keepdims=True)

    loop(rows_home // few, finish)
    for which, out in enumerate((mixed_out, token_out)):
        for m in range(packs):
            rows = slice(m * pack_rows, (m + 1) * pack_rows)

            def step(cb):
                cols = span(cb, wide)
                tt[which * rows_home + m * pack_rows:which * rows_home + (m + 1) * pack_rows, cols] = dot(
                    select_ref[m], gst[which, rows, cols], ((0,), (0,))
                ).astype(bf16)

            loop(width // wide, step)
        local(tt.at[which * rows_home:(which + 1) * rows_home, :], out, load.at[which]).start()
    advance()

    for d in range(group):
        cols = slice(d * rows_home, (d + 1) * rows_home)
        vsend[d, 0:3, :] = full[8:11, cols]
        for n in range(kinds):
            piece = kinds * d + n
            vsend[d, 3 + n:4 + n, :] = jnp.where(
                me == piece % group, sums[piece // group:piece // group + 1, :], 0.0
            )
    for e in range(1, 8):
        d = flip(e)
        remote(vsend.at[d], vgot.at[me], v_send.at[1], v_recv.at[1], at_shard(d)).start()
    vgot[me] = vsend[me]
    block = vgot.at[0:7]
    local(block, block, v_recv.at[1]).wait()
    advance()
    total = vgot[0]
    for q in range(1, group):
        total = total + vgot[q]
    zgot[rep, 0:6, :] = total[0:6, :]
    zgot[rep, 6:6 + TILES, :] = sums[6:6 + TILES, :]
    for z in range(1, 4):
        remote(zgot.at[rep], zgot.at[rep], v_send.at[2], v_recv.at[2],
               at_rep((rep + z) % 4)).start()
    block = zgot.at[0:3]
    local(block, block, v_recv.at[2]).wait()
    vec_out[...] = (zgot[0] + zgot[1]) + (zgot[2] + zgot[3])
    local(block, block, v_send.at[2]).wait()
    block = vsend.at[0:7]
    local(block, block, v_send.at[1]).wait()
    block = vecs.at[0:7]
    local(block, block, v_send.at[0]).wait()

    advance(last_half + 1)

    @pl.when(outer)
    def _():
        def end(u):
            g, a, b, t = unit(u)
            remote(g, a, za_s.at[u], za_r.at[u], at_rep(near)).wait_send()
            remote(g, t, zc_s.at[u], zc_r.at[u], at_rep(near)).wait_recv()

        loop(units, end)

    @pl.when(inner)
    def _():
        for u in range(units - SLOTS, units):
            t = unit(u)[3]
            past = pb.at[u % SLOTS]
            remote(past, t, zc_s.at[u], zc_r.at[u], at_rep(near)).wait_send()
            local(past, t, zt.at[u]).wait()

    for which, out in enumerate((mixed_out, token_out)):
        local(tt.at[which * rows_home:(which + 1) * rows_home, :], out, load.at[which]).wait()
    for which in range(2):
        for n in range(3):
            block = home.at[which, n]
            remote(block, block, k_send.at[which * chips + n], m_recv.at[which],
                   at_shard(flip(2))).wait_send()
    for block, sem in (
        (fc1.at[0:4 * rows_home, :], w_send.at[0]), (wqkv.at[0:7 * rows_home, :], w_send.at[1]),
        (fc1.at[0:3 * rows_home, :], x_send.at[0]),
    ):
        local(block, block, sem).wait()


def spread_out(in_ref, out_ref):
    size = in_ref.shape[-1]
    for i in range(in_ref.shape[0]):
        out_ref[:, i * size:(i + 1) * size] = in_ref[i].astype(jnp.float32)


def fused(begins, key_id, base, turns, select, valid, vec, tokens, cotangent, fc1_w, qkv_w, fc2_w,
          dense_w, group):
    bf16, f32 = jnp.bfloat16, jnp.float32
    rows, width = tokens.shape
    ff = fc1_w.shape[1] // group
    tile = ff // TILES
    packs, blocks = begins.shape
    cap = rows // packs // blocks
    total = group * rows
    chips = group // 2
    chunks = 2 * TILES + 4
    chunk = jax.ShapeDtypeStruct((chunks, rows, width), bf16)
    parts = [jax.ShapeDtypeStruct((2, n, rows, width), bf16) for n in (chips, 3)]
    parts.append(jax.ShapeDtypeStruct((2, rows, width), bf16))
    rows_out = jax.ShapeDtypeStruct((rows, width), bf16)
    out_shape = [chunk] * 4 + parts + [rows_out] * 2 + [
        jax.ShapeDtypeStruct((VROWS, rows), f32)
    ]
    vmem = pl.BlockSpec(memory_space=pltpu.VMEM)
    anywhere = pl.BlockSpec(memory_space=pl.ANY)
    dma = pltpu.SemaphoreType.DMA
    per = (group, packs, blocks, cap)
    pack = blocks * BLOCK
    scratch = [
        pltpu.VMEM((total, width), bf16), pltpu.VMEM((total, width), bf16),
        pltpu.VMEM((width, ff), bf16), pltpu.VMEM((ff, width), bf16),
        pltpu.VMEM((width, 3 * rows), bf16), pltpu.VMEM((rows, width), bf16),
        pltpu.VMEM((total, ff), bf16), pltpu.VMEM((total, ff), bf16),
        pltpu.VMEM(per + (rows,), bf16), pltpu.VMEM(per + (3 * rows,), bf16),
        pltpu.VMEM(per + (3 * rows,), bf16), pltpu.VMEM(per + (rows,), bf16),
        pltpu.VMEM((pack, PAIR), bf16), pltpu.VMEM((pack, PAIR), bf16),
        pltpu.VMEM((pack, PAIR), f32), pltpu.VMEM((pack, PAIR), f32),
        pltpu.VMEM((2 * tile, total), bf16),
        pltpu.VMEM((2, rows, width), bf16), pltpu.VMEM((STAGES, group, rows, rows), bf16),
        pltpu.VMEM((SLOTS, rows // 2, width), bf16), pltpu.VMEM((rows // 2, width), bf16),
        pltpu.VMEM((rows // 2, width), bf16),
        pltpu.VMEM((group, VROWS, rows), f32), pltpu.VMEM((VROWS, width), f32),
        pltpu.VMEM((VROWS, rows), f32), pltpu.VMEM((group, VROWS, rows), f32),
        pltpu.VMEM((group, VROWS, rows), f32), pltpu.VMEM((4, VROWS, rows), f32),
        pltpu.VMEM((8, 3 * rows), f32),
        dma((9,)), dma((2, 7)), dma((2, 8)), dma((2,)), dma((TILES + 1,)), dma((1,)),
        dma((TILES,)), dma((2,)), dma((STAGES,)), dma((STAGES,)), dma((chunks,)),
        dma((2 * chunks,)), dma((2 * chunks,)), dma((2 * chunks,)), dma((2 * chunks,)),
        dma((2 * chunks,)), dma((2 * chunks,)), dma((2 * chunks,)), dma((3,)),
        dma((2 * chips,)), dma((2 * chips,)), dma((6,)), dma((2 * chips,)), dma((2,)), dma((3,)),
        dma((3,)),
    ]
    flops = 6 * total * width * (2 * ff + 4 * rows)
    outs = pl.pallas_call(
        fused_kernel,
        in_specs=[pl.BlockSpec(memory_space=pltpu.SMEM)] + [vmem] * 5 + [anywhere] * 7,
        out_specs=[anywhere] * 9 + [vmem],
        out_shape=out_shape,
        scratch_shapes=scratch,
        compiler_params=pltpu.CompilerParams(
            vmem_limit_bytes=60 << 20, collective_id=0, has_side_effects=True
        ),
        cost_estimate=pl.CostEstimate(
            flops=flops, bytes_accessed=64 << 20, transcendentals=total * ff
        ),
    )(begins, key_id, base, turns, select, valid, vec, tokens, cotangent, fc1_w, qkv_w, fc2_w, dense_w)
    sums = outs[3]
    grad_fc1 = pl.pallas_call(
        spread_out,
        grid=(group,),
        in_specs=[pl.BlockSpec((TILES, rows, tile), lambda q: (1, 0, q))],
        out_specs=pl.BlockSpec((rows, ff), lambda q: (0, q)),
        out_shape=jax.ShapeDtypeStruct((rows, group * ff), f32),
    )(sums)
    grad_qkv = pl.pallas_call(
        spread_out,
        grid=(3,),
        in_specs=[pl.BlockSpec((1, rows, width), lambda k: (2 * TILES + 1 + k, 0, 0))],
        out_specs=pl.BlockSpec((rows, width), lambda k: (0, k)),
        out_shape=jax.ShapeDtypeStruct((rows, 3 * width), f32),
    )(sums)
    grad_fc2 = sums[0:TILES].reshape(ff, width).astype(f32)
    grad_dense = sums[2 * TILES].astype(f32)
    return outs[7], outs[8], outs[9], grad_qkv, grad_dense, grad_fc1, grad_fc2


def spread_layer(
    gy_home, hn_home, begins, key_id, qkv_weight, b_qkv, dense_weight, fc1_weight, b_fc1, fc2_weight
):
    bf16, f32 = jnp.bfloat16, jnp.float32
    group, reps = lax.axis_size("shard"), lax.axis_size("rep")
    width = gy_home.shape[1]
    rows = gy_home.shape[0] // MICRO
    cap = rows // group
    mine = width // group
    ff_mine = fc1_weight.shape[1] // group
    blocks = begins.shape[1]
    all_rows = MICRO * rows * group

    fc1 = lax.all_to_all(
        fc1_weight.reshape(mine, group, ff_mine).transpose(1, 0, 2), "shard", 0, 0, tiled=True
    ).reshape(width, ff_mine)
    w_qkv = lax.all_to_all(
        qkv_weight.reshape(mine, 3, group, mine).transpose(2, 0, 1, 3), "shard", 0, 0, tiled=True
    ).reshape(width, 3 * mine)

    gy = lax.all_gather(gy_home, "shard", axis=0, tiled=True)
    hn = lax.all_gather(hn_home, "shard", axis=0, tiled=True)

    upper = dot(hn, fc1, ((1,), (0,))) + b_fc1
    inner = math.sqrt(2.0 / math.pi) * (upper + 0.044715 * upper * upper * upper)
    curve = jnp.tanh(inner)
    act = (0.5 * upper * (1.0 + curve)).astype(bf16)
    slope = 0.5 * (1.0 + curve) + 0.5 * upper * (1.0 - curve * curve) * math.sqrt(
        2.0 / math.pi
    ) * (1.0 + 3 * 0.044715 * upper * upper)
    dup = (dot(gy, fc2_weight, ((1,), (1,))) * slope).astype(bf16)
    g_fc2 = dot(act, gy, ((0,), (0,)), f32).astype(bf16)
    g_fc1 = dot(hn, dup, ((0,), (0,)), f32).astype(bf16)

    def over_reps(part):
        return lax.psum_scatter(part, "rep", scatter_dimension=0, tiled=True)

    def from_reps(part):
        return lax.all_gather(part, "rep", axis=0, tiled=True)

    def by_rows(grad):
        cols = grad.shape[1]
        split = grad.reshape(group, reps, mine // reps, cols).transpose(1, 0, 2, 3)
        part = over_reps(split.reshape(reps * group, mine // reps, cols))
        part = lax.all_to_all(part, "shard", 0, 0, tiled=True)
        whole = from_reps(part)
        return whole.reshape(reps, group, mine // reps, cols)

    grad_fc2 = from_reps(over_reps(g_fc2)).astype(f32)
    grad_fc1 = by_rows(g_fc1).transpose(0, 2, 1, 3).reshape(mine, -1).astype(f32)

    qkv = dot(hn, w_qkv, ((1,), (0,))) + b_qkv
    dout = dot(gy, dense_weight, ((1,), (1,)))
    shape = (group, MICRO, blocks, cap)
    ob, dq, dk, dv = attention(
        begins, qkv.reshape(*shape, 3 * mine), dout.reshape(*shape, mine), key_id
    )
    ob = ob.reshape(all_rows, mine).astype(bf16)
    dqkv = jnp.concatenate(
        [part.reshape(all_rows, mine).astype(bf16) for part in (dq, dk, dv)], axis=1
    )
    g_qkv = dot(hn, dqkv, ((0,), (0,)), f32).astype(bf16)
    g_dense = dot(ob, gy, ((0,), (0,)), f32).astype(bf16)
    grad_dense = from_reps(over_reps(g_dense)).astype(f32)
    grad_qkv = by_rows(g_qkv).reshape(reps, group, mine // reps, 3, mine)
    grad_qkv = grad_qkv.transpose(0, 2, 3, 1, 4).reshape(mine, 3 * width).astype(f32)

    def home(part):
        got = lax.all_to_all(part.reshape(group, MICRO * rows, width), "shard", 0, 0, tiled=True)
        return jnp.sum(got.astype(f32), axis=0)

    out_part = (
        dot(act, fc2_weight, ((1,), (0,))) + dot(ob, dense_weight, ((1,), (0,)))
    ).astype(bf16)
    dh_part = (dot(dqkv, w_qkv, ((1,), (1,))) + dot(dup, fc1, ((1,), (1,)))).astype(bf16)
    v_qkv = jnp.sum(dqkv.astype(f32), axis=0).reshape(3, mine)
    v_fc1 = jnp.sum(dup.astype(f32), axis=0)
    return (
        home(out_part), home(dh_part), grad_qkv, grad_dense, grad_fc1, grad_fc2, v_qkv, v_fc1
    )


def fused_layer(
    tokens, cotangent, select, valid_home, begins, key_id, ln_gain, ln_bias, qkv_weight, qkv_bias,
    dense_weight, dense_bias, fc1_weight, fc1_bias, fc2_weight, fc2_bias,
):
    f32 = jnp.float32
    group = lax.axis_size("shard")
    rows = tokens.shape[0]
    half = ROT // 2
    lane = np.arange(PAIR) % HDIM
    freqs = np.exp(-math.log(10000.0) * np.arange(half) * 2.0 / ROT).astype(np.float32)[lane % half]
    spots = np.arange(BLOCK)[:, None] * freqs[None, :].astype(np.float64)
    base = jnp.asarray(np.stack([np.cos(spots), np.sin(spots)]).astype(np.float32))
    steps = np.arange(MAXBLK)[:, None] * BLOCK * freqs[None, :].astype(np.float64)
    table = jnp.asarray(np.stack([np.cos(steps), np.sin(steps)], axis=1).astype(np.float32))
    blocks = jnp.arange(begins.shape[1], dtype=jnp.int32)
    offset = blocks[None, :] - begins
    turns = jnp.sum(jnp.where(
        offset[:, :, None, None, None] == jnp.arange(MAXBLK, dtype=jnp.int32)[:, None, None],
        table, 0.0,
    ), axis=2)
    vec = jnp.concatenate(
        [ln_gain, ln_bias, dense_bias, fc2_bias, qkv_bias, fc1_bias]
    ).astype(f32).reshape(-1, rows)
    vec = jnp.pad(vec, ((0, VROWS - vec.shape[0]), (0, 0)))
    mixed, token_grad, sums, grad_qkv, grad_dense, grad_fc1, grad_fc2 = fused(
        begins, key_id, base, turns, select, valid_home.astype(f32), vec, tokens, cotangent,
        fc1_weight, qkv_weight, fc2_weight, dense_weight, group,
    )
    bias_out, gain_grad, lnb_grad = sums[0], sums[1], sums[2]
    return (
        mixed, token_grad, gain_grad, lnb_grad, grad_qkv, sums[3:6].reshape(-1), grad_dense,
        bias_out, grad_fc1, sums[6:6 + TILES].reshape(-1), grad_fc2, bias_out,
    )


def body(
    tokens, cotangent, placement_order, seq_lengths, ln_gain, ln_bias, qkv_weight, qkv_bias,
    dense_weight, dense_bias, fc1_weight, fc1_bias, fc2_weight, fc2_bias,
):
    bf16, f32 = jnp.bfloat16, jnp.float32
    group = lax.axis_size("shard")
    reps = lax.axis_size("rep")
    me = lax.axis_index("shard")
    width = tokens.shape[1]
    rows = tokens.shape[0] // MICRO
    cap = rows // group
    mine = width // group
    ff_mine = fc1_weight.shape[1] // group
    blocks = seq_lengths.shape[2]
    all_rows = MICRO * rows * group

    begins, limits = block_begins(seq_lengths[0])
    spot = jnp.arange(BLOCK, dtype=jnp.int32)
    index = jnp.arange(blocks, dtype=jnp.int32)
    position = (index[None, :, None] - begins[:, :, None]) * BLOCK + spot[None, None, :]
    valid = position < limits[:, :, None]
    key_id = jnp.where(valid, begins[:, :, None], -1).reshape(MICRO, 1, blocks * BLOCK)

    orders = placement_order[0, 0]
    select = (orders[:, None, :] == jnp.arange(rows, dtype=jnp.int32)[None, :, None]).astype(bf16)

    valid_home = lax.dynamic_index_in_dim(
        valid.reshape(MICRO, group, group, cap), me, 2, keepdims=False
    ).reshape(MICRO * rows, 1)
    held = 2 * MICRO * rows * group * (2 * width + 2 * ff_mine + 7 * mine)
    held += 2 * width * (2 * ff_mine + 4 * mine)
    if (group, reps) == (8, 4) and cap % 16 == 0 and held <= FUSED_BYTES:
        return fused_layer(
            tokens, cotangent, select, valid_home, begins, key_id, ln_gain, ln_bias, qkv_weight,
            qkv_bias, dense_weight, dense_bias, fc1_weight, fc1_bias, fc2_weight, fc2_bias,
        )

    pieces = (ln_gain, ln_bias, dense_bias, fc2_bias, qkv_bias, fc1_bias)
    packed = jnp.concatenate(pieces)
    spread = lax.all_gather(packed, "shard", axis=0).astype(f32)
    full, at = [], 0
    for piece in pieces:
        full.append(spread[:, at:at + piece.shape[0]].reshape(-1))
        at += piece.shape[0]
    gain, lnb, b_dense, b_fc2, b_qkv, b_fc1 = full
    b_qkv = lax.dynamic_slice_in_dim(b_qkv.reshape(3, width), me * mine, mine, 1).reshape(-1)
    b_fc1 = lax.dynamic_slice_in_dim(b_fc1, me * ff_mine, ff_mine, 0)

    def arrange(array):
        return jnp.einsum(
            "mti,mid->mtd", select, array.reshape(MICRO, rows, width),
            preferred_element_type=f32,
        ).astype(bf16).reshape(MICRO * rows, width)

    x_home, g_home = arrange(tokens), arrange(cotangent)
    gy_home = jnp.where(valid_home, g_home, jnp.zeros((), bf16))
    x32 = x_home.astype(f32)
    centered = x32 - jnp.mean(x32, axis=1, keepdims=True)
    rstd = lax.rsqrt(jnp.mean(centered * centered, axis=1, keepdims=True) + 1e-05)
    hn_home = (centered * rstd * gain + lnb).astype(bf16)
    split = (
        gy_home, hn_home, begins, key_id, qkv_weight, b_qkv, dense_weight, fc1_weight, b_fc1,
        fc2_weight,
    )
    result = spread_layer(*split)
    out_sum, dh, grad_qkv, grad_dense, grad_fc1, grad_fc2, v_qkv, v_fc1 = result
    branch = out_sum + (b_dense + b_fc2)
    mixed = (x32 + jnp.where(valid_home, branch, 0.0)).astype(bf16)
    xhat = centered * rstd
    scaled = dh * gain
    dx = (
        scaled
        - jnp.mean(scaled, axis=1, keepdims=True)
        - xhat * jnp.mean(scaled * xhat, axis=1, keepdims=True)
    ) * rstd
    token_grad = (g_home.astype(f32) + dx).astype(bf16)

    def back(array):
        return jnp.einsum(
            "mti,mtd->mid", select, array.reshape(MICRO, rows, width),
            preferred_element_type=f32,
        ).astype(bf16).reshape(MICRO * rows, width)

    v_out = jnp.sum(gy_home.astype(f32), axis=0)
    v_gain = jnp.sum(dh * xhat, axis=0)
    v_lnb = jnp.sum(dh, axis=0)
    mixed_vec = jnp.concatenate([v_qkv.reshape(-1), v_fc1, v_out, v_gain, v_lnb])
    table = lax.all_gather(mixed_vec, ("rep", "shard"), axis=0).reshape(reps, group, -1)
    table = jnp.sum(table, axis=0)
    at = 3 * mine
    bias_qkv = table[:, :at].reshape(group, 3, mine).transpose(1, 0, 2).reshape(-1)
    bias_qkv = lax.dynamic_slice_in_dim(bias_qkv, me * 3 * mine, 3 * mine, 0)
    bias_fc1 = lax.dynamic_index_in_dim(table[:, at:at + ff_mine], me, 0, keepdims=False)
    full = jnp.sum(table[:, at + ff_mine:], axis=0).reshape(3, group, mine)
    bias_out, gain_grad, lnb_grad = lax.dynamic_index_in_dim(full, me, 1, keepdims=False)
    return (
        back(mixed), back(token_grad), gain_grad, lnb_grad, grad_qkv, bias_qkv, grad_dense,
        bias_out, grad_fc1, bias_fc1, grad_fc2, bias_out,
    )


def solution(mesh):
    rows = P(("rep", "shard"), None)
    vector, matrix = P("shard"), P("shard", None)
    layer = (vector, vector, matrix, vector, matrix, vector, matrix, vector, matrix, vector)
    return jax.shard_map(
        body,
        mesh=mesh,
        in_specs=(rows, rows, P("rep", "shard", None, None), P("rep", None, None)) + layer,
        out_specs=(rows, rows) + layer,
        check_vma=False,
    )
```

```python
import math

import jax
import jax.numpy as jnp
import numpy as np
from jax import lax
from jax.experimental import pallas as pl
from jax.experimental.pallas import tpu as pltpu
from jax.sharding import PartitionSpec as P

HEADS = 32
HDIM = 64
ROT = 32
BLOCK = 128
MICRO = 2
MAXBLK = 8
PAIR = 2 * HDIM
NEG = -1e30
FUSED_BYTES = 48 << 20


def dot(left, right, dims, out=jnp.float32):
    return lax.dot_general(left, right, (dims, ((), ())), preferred_element_type=out)


def block_begins(lengths):
    blocks = jnp.arange(lengths.shape[1], dtype=jnp.int32)
    started = (lengths[:, None, :] > 0) & (blocks[None, None, :] <= blocks[None, :, None])
    begins = jnp.max(jnp.where(started, blocks[None, None, :], 0), axis=2)
    own = begins[:, :, None] == blocks[None, None, :]
    limits = jnp.sum(jnp.where(own, lengths[:, None, :], 0), axis=2)
    return begins, limits


def rotary_tables():
    half = ROT // 2
    lane = np.arange(PAIR) % HDIM
    freqs = np.exp(-math.log(10000.0) * np.arange(half) * 2.0 / ROT).astype(np.float32)
    position = np.arange(MAXBLK * BLOCK, dtype=np.float32)
    angles = (position[:, None] * freqs[lane % half][None, :]).astype(np.float64)
    sines = np.sin(angles)
    cosine = np.where(lane < ROT, np.cos(angles), 1.0)
    signed = np.where(lane < half, -sines, np.where(lane < ROT, sines, 0.0))
    return [jnp.asarray(t.astype(np.float32)) for t in (cosine, signed)]


def attention_kernel(begin_ref, q_ref, k_ref, v_ref, do_ref, cos_ref, sin_ref, kid_ref,
                     ob_ref, dq_ref, dk_ref, dv_ref, ks, vs, dks, dvs):
    micro = pl.program_id(0)
    blocks = q_ref.shape[1]
    lane = lax.broadcasted_iota(jnp.int32, (BLOCK, PAIR), 1)
    half = ROT // 2

    def rows(ref, j):
        return ref[:, j].reshape(BLOCK, PAIR)

    def table(ref, j):
        return ref[pl.ds(pl.multiple_of((j - begin_ref[micro, j]) * BLOCK, BLOCK), BLOCK), :]

    def turn(x, j, back):
        other = jnp.where(
            lane % HDIM < half, pltpu.roll(x, PAIR - half, 1), pltpu.roll(x, half, 1)
        ) * table(sin_ref, j)
        straight = x * table(cos_ref, j)
        return straight - other if back else straight + other

    for j in range(blocks):
        ks[j * BLOCK:(j + 1) * BLOCK, :] = turn(rows(k_ref, j), j, False).astype(jnp.bfloat16)
        vs[j * BLOCK:(j + 1) * BLOCK, :] = rows(v_ref, j).astype(jnp.bfloat16)
    dks[...] = jnp.zeros_like(dks)
    dvs[...] = jnp.zeros_like(dvs)
    causal = lax.broadcasted_iota(jnp.int32, (BLOCK, BLOCK), 1) <= lax.broadcasted_iota(
        jnp.int32, (BLOCK, BLOCK), 0
    )
    scale = 1.0 / math.sqrt(HDIM)
    zero = jnp.zeros((), jnp.bfloat16)
    for j in range(blocks):
        first = max(0, j - MAXBLK + 1)
        span = slice(first * BLOCK, (j + 1) * BLOCK)
        q_all = turn(rows(q_ref, j), j, False).astype(jnp.bfloat16)
        do_all = rows(do_ref, j).astype(jnp.bfloat16)
        keys, values = ks[span, :], vs[span, :]
        same = kid_ref[:, span] == begin_ref[micro, j]
        bias = jnp.where(same, 0.0, NEG)
        width = (j + 1 - first) * BLOCK
        outs, dqs = [], []
        for head in range(PAIR // HDIM):
            mine = (lane >= head * HDIM) & (lane < (head + 1) * HDIM)
            q = jnp.where(mine, q_all, zero)
            do = jnp.where(mine, do_all, zero)
            scores = dot(q, keys, ((1,), (1,))) * scale + bias
            tail = jnp.where(causal, scores[:, width - BLOCK:], NEG)
            if width > BLOCK:
                scores = jnp.concatenate([scores[:, :width - BLOCK], tail], axis=1)
            else:
                scores = tail
            top = jnp.max(scores, axis=1, keepdims=True)
            expo = jnp.exp(scores - top)
            probs = expo / jnp.sum(expo, axis=1, keepdims=True)
            low_probs = probs.astype(jnp.bfloat16)
            outs.append(dot(low_probs, values, ((1,), (0,))))
            dprobs = dot(do, values, ((1,), (1,)))
            weighted = probs * dprobs
            delta = jnp.sum(weighted, axis=1, keepdims=True)
            dscores = (weighted - probs * delta).astype(jnp.bfloat16)
            dqs.append(dot(dscores, keys, ((1,), (0,))))
            dks[span, :] += dot(dscores, q, ((0,), (0,)))
            dvs[span, :] += dot(low_probs, do, ((0,), (0,)))
        first_head = lane < HDIM
        shape = (q_ref.shape[0], q_ref.shape[2], PAIR)
        ob = jnp.where(first_head, outs[0], outs[1])
        ob_ref[:, j] = ob.astype(jnp.bfloat16).astype(jnp.float32).reshape(shape)
        dq = turn(jnp.where(first_head, dqs[0], dqs[1]) * scale, j, True)
        dq_ref[:, j] = dq.astype(jnp.bfloat16).astype(jnp.float32).reshape(shape)
    for j in range(blocks):
        here = slice(j * BLOCK, (j + 1) * BLOCK)
        shape = (q_ref.shape[0], q_ref.shape[2], PAIR)
        dk = turn(dks[here, :] * scale, j, True)
        dk_ref[:, j] = dk.astype(jnp.bfloat16).astype(jnp.float32).reshape(shape)
        dv_ref[:, j] = dvs[here, :].astype(jnp.bfloat16).astype(jnp.float32).reshape(shape)


def attention(begins, qkv, dout, kid):
    group, micros, blocks, cap, _ = qkv.shape
    width = dout.shape[-1]
    pairs = width // PAIR
    total = blocks * BLOCK

    def rows_spec(offset):
        return pl.BlockSpec(
            (group, None, blocks, cap, PAIR), lambda m, p, *_: (0, m, 0, 0, offset + p)
        )

    table_spec = pl.BlockSpec((MAXBLK * BLOCK, PAIR), lambda m, p, *_: (0, 0))
    out = jax.ShapeDtypeStruct(dout.shape, jnp.float32)
    work = micros * pairs * 2 * blocks * (min(blocks, MAXBLK) + 1) // 2 * BLOCK * BLOCK
    return pl.pallas_call(
        attention_kernel,
        grid_spec=pltpu.PrefetchScalarGridSpec(
            num_scalar_prefetch=1,
            grid=(micros, pairs),
            in_specs=[
                rows_spec(0), rows_spec(pairs), rows_spec(2 * pairs), rows_spec(0),
                table_spec, table_spec,
                pl.BlockSpec((None, 1, total), lambda m, p, *_: (m, 0, 0)),
            ],
            out_specs=[rows_spec(0)] * 4,
            scratch_shapes=[
                pltpu.VMEM((total, PAIR), jnp.bfloat16),
                pltpu.VMEM((total, PAIR), jnp.bfloat16),
                pltpu.VMEM((total, PAIR), jnp.float32),
                pltpu.VMEM((total, PAIR), jnp.float32),
            ],
        ),
        out_shape=[out] * 4,
        compiler_params=pltpu.CompilerParams(vmem_limit_bytes=48 << 20),
        cost_estimate=pl.CostEstimate(
            flops=12 * work * PAIR, bytes_accessed=8 * dout.size * 4, transcendentals=work
        ),
    )(begins, qkv, qkv, qkv, dout, *rotary_tables(), kid)


MESH = pl.DeviceIdType.MESH
SLOTS = 5
TILES = 4
VROWS = 16
HOLD = 4
WAIT = 5
STAGES = 3
EARLY = 1


def fused_kernel(
    begin_ref, kid_ref, base_ref, turn_ref, select_ref, valid_ref, vec_in,
    tokens, cotangent, fc1_w, qkv_w, fc2_w, dense_w,
    grad, grad_a, grad_b, grad_t, part_in, home, mid_in, mixed_out, token_out, vec_out,
    gy, hn, fc1, fc2, wqkv, dense, act, dup, ob, dqkv, qkv, dout, ks, vs, dks, dvs, tt, gst, ast,
    pb, va, vb, vecs, full, sums, vsend, vgot, zgot, bq_row,
    load, ag_send, ag_recv, w_send, w_recv, x_send, x_recv, st, g_send, g_own, g_recv, za_s, za_r, zb_s, zb_r, zc_s,
    zc_r, zt, zl, d_send, p_recv, h_recv, k_send, m_recv, v_send, v_recv,
):
    bf16, f32 = jnp.bfloat16, jnp.float32
    me, rep = lax.axis_index("shard"), lax.axis_index("rep")
    core, cx, cy = me % 2, (me // 2) % 2, me // 4
    near = rep + 1 - 2 * (rep % 2)
    far = 3 - rep
    inner = (rep == 1) | (rep == 2)
    outer = (rep == 0) | (rep == 3)
    rows_home = tokens.shape[0]
    width = tokens.shape[1]
    group = width // rows_home
    ff = fc1.shape[1]
    tile = ff // TILES
    wide = 512
    packs = kid_ref.shape[0]
    pack_rows = rows_home // packs
    blocks = kid_ref.shape[2] // BLOCK
    cap = qkv.shape[3]
    pairs = rows_home // PAIR
    kinds = 3

    def flip(e):
        return ((cy + e // 4) % 2) * 4 + ((cx + (e // 2) % 2) % 2) * 2 + (core + e % 2) % 2

    def at_shard(d):
        return {"shard": d}

    def at_rep(d):
        return {"rep": d}

    def remote(src, dst, send, recv, dev):
        return pltpu.make_async_remote_copy(
            src_ref=src, dst_ref=dst, send_sem=send, recv_sem=recv, device_id=dev,
            device_id_type=MESH,
        )

    def local(src, dst, sem):
        return pltpu.make_async_copy(src, dst, sem)

    def span(i, size):
        return pl.ds(pl.multiple_of(i * size, size), size)

    def own(ref, q):
        return ref.at[span(q, rows_home), :]

    def loop(count, step):
        def run(i, _):
            step(i)
            return 0

        lax.fori_loop(0, count, run, 0)

    first_loads = [
        local(cotangent, gst.at[1], load.at[1]),
        local(tokens, gst.at[0], load.at[0]),
    ]
    loads = [
        local(fc1_w.at[:, span(me, ff)], own(fc1, me), load.at[2]),
        local(fc2_w, fc2, load.at[3]),
        local(dense_w, dense, load.at[4]),
        local(vec_in, vecs.at[me], load.at[5]),
    ] + [
        local(
            qkv_w.at[:, span(kind * group + me, rows_home)],
            wqkv.at[span(me, rows_home), pl.ds(kind * rows_home, rows_home)], load.at[6 + kind],
        )
        for kind in range(kinds)
    ]
    for copy in first_loads + loads:
        copy.start()

    barrier = pltpu.get_barrier_semaphore()
    for e in range(1, 8):
        pl.semaphore_signal(barrier, inc=1, device_id=at_shard(flip(e)), device_id_type=MESH)
    for z in range(1, 4):
        pl.semaphore_signal(
            barrier, inc=1, device_id=at_rep((rep + z) % 4), device_id_type=MESH
        )
    pl.semaphore_wait(barrier, 10)

    for e in range(1, 8):
        remote(vec_in, vecs.at[me], v_send.at[0], v_recv.at[0], at_shard(flip(e))).start()
    buffers = (gy, hn)

    def send_own(a):
        buf = buffers[a]
        for n, e in enumerate((2, 4, 1)):
            remote(own(buf, me), own(buf, me), ag_send.at[a, n], ag_recv.at[a, e],
                   at_shard(flip(e))).start()

    def chip_of(c):
        return ((cy + c // 2) % 2) * 2 + (cx + c % 2) % 2

    def in_plane():
        return [2 * chip_of(c) + (core + rep) % 2 for c in (1, 2, 3)]

    def send_fc1(i):
        early = i < EARLY
        for d in [flip(1)] + in_plane() if early else [flip(e) for e in range(1, 8)]:
            remote(
                fc1_w.at[:, pl.ds(pl.multiple_of(d * ff + i * tile, tile), tile)],
                fc1.at[span(me, rows_home), pl.ds(i * tile, tile)],
                w_send.at[0 if early else 2], w_recv.at[i], at_shard(d),
            ).start()

    def send_qkv():
        for e in range(1, 8):
            d = flip(e)
            for kind in range(kinds):
                remote(
                    qkv_w.at[:, span(kind * group + d, rows_home)],
                    wqkv.at[span(me, rows_home), pl.ds(kind * rows_home, rows_home)],
                    w_send.at[1], w_recv.at[TILES], at_shard(d),
                ).start()

    def fc1_part(i, count, sem):
        block = fc1.at[0:count * rows_home, pl.ds(i * tile, tile)]
        return local(block, block, sem)

    def pass_on(i):
        fc1_part(i, 4, w_recv.at[i]).wait()
        for q in in_plane():
            block = fc1.at[span(q, rows_home), pl.ds(i * tile, tile)]
            remote(block, block, x_send.at[0], x_recv.at[i], at_rep(near)).start()

    def ag_wait(a, e):
        buf = buffers[a]
        remote(own(buf, me), own(buf, flip(e)), ag_send.at[a, 0], ag_recv.at[a, e],
               at_shard(flip(e))).wait_recv()

    def forward(a, have, to, n):
        q = own(buffers[a], flip(have))
        remote(q, q, ag_send.at[a, n], ag_recv.at[a, have ^ to], at_shard(flip(to))).start()

    def relay(a):
        ag_wait(a, 2)
        forward(a, 2, 1, 4)

        @pl.when(core == 0)
        def _():
            forward(a, 2, 4, 3)

        ag_wait(a, 4)
        forward(a, 4, 1, 5)

        @pl.when(core == 1)
        def _():
            forward(a, 4, 2, 3)

    def sort_rows(source, put):
        for m in range(packs):
            def step(cb):
                cols = span(cb, wide)
                put(m, cols, dot(
                    select_ref[m], gst[source, m * pack_rows:(m + 1) * pack_rows, cols],
                    ((1,), (0,)),
                ))

            loop(width // wide, step)

    def put_gy(m, cols, value):
        keep = valid_ref[m * pack_rows:(m + 1) * pack_rows, :]
        gy[pl.ds(pl.multiple_of(me * rows_home + m * pack_rows, pack_rows), pack_rows), cols] = (
            value * keep
        ).astype(bf16)

    def put_tt(first):
        def put(m, cols, value):
            tt[first + m * pack_rows:first + (m + 1) * pack_rows, cols] = value.astype(bf16)

        return put

    few = 32

    def statistics(x):
        centered = x - jnp.mean(x, axis=1, keepdims=True)
        rstd = lax.rsqrt(jnp.mean(centered * centered, axis=1, keepdims=True) + 1e-05)
        return centered * rstd, rstd

    for i in range(EARLY):
        send_fc1(i)
    first_loads[0].wait()
    sort_rows(1, put_gy)
    send_own(0)
    first_loads[1].wait()
    sort_rows(0, put_tt(0))
    block = vecs.at[0:7]
    local(block, block, v_recv.at[0]).wait()
    for copy in loads:
        copy.wait()
    for q in range(group):
        cols = slice(q * rows_home, (q + 1) * rows_home)
        full[0:4, cols] = vecs[q, 0:4, :]
    for kind in range(kinds):
        piece = kind * group + me
        bq_row[0:1, kind * rows_home:(kind + 1) * rows_home] = vecs[
            piece // kinds, pl.ds(4 + piece % kinds, 1), :
        ]

    def norm_rows(rb):
        xhat, _ = statistics(tt[span(rb, few), :].astype(f32))
        hn[pl.ds(pl.multiple_of(me * rows_home + rb * few, few), few), :] = (
            xhat * full[0:1, :] + full[1:2, :]
        ).astype(bf16)

    loop(rows_home // few, norm_rows)
    send_own(1)
    for i in range(EARLY):
        pass_on(i)
    for a in range(2):
        relay(a)
    for i in range(EARLY, TILES):
        send_fc1(i)
    send_qkv()
    for a in range(2):
        ag_wait(a, 6)
        forward(a, 6, 1, 6)
    for a in range(2):
        for e in (1, 3, 5, 7):
            ag_wait(a, e)

    half = rows_home // 2
    units = 2 * grad.shape[0]

    def unit(u):
        at = (u // 2, pl.ds(pl.multiple_of((u % 2) * half, half), half), slice(None))
        return [ref.at[at] for ref in (grad, grad_a, grad_b, grad_t)]

    def chain_a(chunk):
        @pl.when(outer)
        def _():
            for u in (2 * chunk, 2 * chunk + 1):
                g, a, _, _ = unit(u)
                remote(g, a, za_s.at[u], za_r.at[u], at_rep(near)).start()

    def add_into(slot, ref):
        few = 32

        def step(rb):
            rows = span(rb, few)
            pb[slot, rows, :] = (pb[slot, rows, :].astype(f32) + ref[rows, :].astype(f32)).astype(bf16)

        loop(half // few, step)

    def b_load(u):
        g, a, _, _ = unit(u)
        return local(g, pb.at[u % SLOTS], zl.at[0]), local(a, va, zl.at[1])

    def b_first(u):
        g, a, _, _ = unit(u)
        remote(g, a, za_s.at[u], za_r.at[u], at_rep(near)).wait_recv()

        def clear():
            t = unit(u - SLOTS)[3]
            past = pb.at[u % SLOTS]
            remote(past, t, zc_s.at[u - SLOTS], zc_r.at[u - SLOTS], at_rep(near)).wait_send()
            local(past, t, zt.at[u - SLOTS]).wait()

        if not isinstance(u, int):
            pl.when(u >= SLOTS)(clear)
        elif u >= SLOTS:
            clear()
        for copy in b_load(u):
            copy.start()

    def b_second(u):
        for copy in b_load(u):
            copy.wait()
        add_into(u % SLOTS, va)
        remote(pb.at[u % SLOTS], unit(u)[2], zb_s.at[u], zb_r.at[u], at_rep(far)).start()

    def c_first(u):
        b = unit(u)[2]
        remote(pb.at[u % SLOTS], b, zb_s.at[u], zb_r.at[u], at_rep(far)).wait_recv()
        local(b, vb, zl.at[2]).start()

    def c_second(u):
        slot = u % SLOTS
        _, _, b, t = unit(u)
        local(b, vb, zl.at[2]).wait()
        remote(pb.at[slot], b, zb_s.at[u], zb_r.at[u], at_rep(far)).wait_send()
        add_into(slot, vb)
        remote(pb.at[slot], t, zc_s.at[u], zc_r.at[u], at_rep(near)).start()
        local(pb.at[slot], t, zt.at[u]).start()

    def half_step(k, odd):
        def known(u):
            return not isinstance(u, int) or 0 <= u < units

        @pl.when(inner)
        def _():
            if odd:
                if known(k):
                    b_second(k)
                if known(k - 2):
                    c_second(k - 2)
            else:
                if known(k):
                    b_first(k)
                if known(k - 2):
                    c_first(k - 2)

    done = [0]
    last_half = 2 * (units + 1) + 1

    def advance(count=1):
        for _ in range(count):
            if done[0] <= last_half:
                half_step(done[0] // 2, done[0] % 2)
                done[0] += 1

    scale_in = math.sqrt(2.0 / math.pi)

    def hidden(i):
        cols = slice(i * tile, (i + 1) * tile)
        bias = vec_in_rows[i]

        def step(rb, total):
            rows = span(rb, rows_home)
            u = dot(hn[rows, :], fc1[:, cols], ((1,), (0,))) + bias
            d = dot(gy[rows, :], fc2[cols, :], ((1,), (1,)))
            square = u * u
            t = jnp.tanh(scale_in * u * (1.0 + 0.044715 * square))
            a = 0.5 * u * (1.0 + t)
            slope = 0.5 * (1.0 + t) + 0.5 * u * (1.0 - t * t) * scale_in * (
                1.0 + 3 * 0.044715 * square
            )
            d = d * slope
            act[rows, cols] = a.astype(bf16)
            tt[0:tile, rows] = a.T.astype(bf16)
            low = d.astype(bf16)
            dup[rows, cols] = low
            tt[tile:2 * tile, rows] = d.T.astype(bf16)
            return total + jnp.sum(low.astype(f32), axis=0, keepdims=True)

        middle = lax.fori_loop(0, group // 2, step, jnp.zeros((1, tile), f32))
        if i:
            advance()
        sums[6 + i:7 + i, :] = lax.fori_loop(group // 2, group, step, middle)

    vec_in_rows = [vecs[me, 7 + i:8 + i, :] for i in range(TILES)]

    def grad_rows(first, height, slot, at):
        def step(cb):
            cols = span(cb, wide)
            gst[slot, at:at + height, cols] = dot(
                tt[first:first + height, :], gy[:, cols], ((1,), (0,))
            ).astype(bf16)

        loop(width // wide, step)

    def store_chunk(slot, chunk):
        return local(gst.at[slot], grad.at[chunk], st.at[slot])

    def place(chunk):
        return grad.at[chunk, :, span(me, rows_home)]

    def sent(slot):
        block = ast.at[slot, 0:7]
        local(block, block, g_send.at[slot]).wait()
        local(ast.at[slot, me], place(0), g_own.at[slot]).wait()

    def spread(first, slot, chunk):
        def step(db):
            g = dot(tt[first:first + rows_home, :], hn[:, span(db, rows_home)], ((1,), (0,)))
            ast[slot, db] = g.T.astype(bf16)

        loop(group, step)
        local(ast.at[slot, me], place(chunk), g_own.at[slot]).start()
        for e in range(1, 8):
            d = flip(e)
            remote(ast.at[slot, d], place(chunk), g_send.at[slot], g_recv.at[chunk],
                   at_shard(d)).start()

    def arrived(chunk):
        block = grad.at[chunk, :, 0:7 * rows_home]
        local(block, block, g_recv.at[chunk]).wait()
        chain_a(chunk)

    for i in range(TILES):
        if i < EARLY:
            fc1_part(i, 3, x_recv.at[i]).wait()
        else:
            fc1_part(i, 7, w_recv.at[i]).wait()
        hidden(i)
        if i:
            advance()
        grad_rows(0, tile, i % 2, 0)
        store_chunk(i % 2, i).start()
        store_chunk(i % 2, i).wait()
        chain_a(i)
        if i:
            advance()
        if i >= STAGES:
            sent(i % STAGES)
        spread(tile, i % STAGES, TILES + i)
        if i:
            advance()

    block = wqkv.at[0:7 * rows_home, :]
    local(block, block, w_recv.at[TILES]).wait()
    turn_by = ROT // 2

    def rotated(x, cosine, signed, low_half):
        other = jnp.where(
            low_half, pltpu.roll(x, x.shape[-1] - turn_by, x.ndim - 1),
            pltpu.roll(x, turn_by, x.ndim - 1),
        )
        return x * cosine + other * signed

    def project(sb):
        rows = span(sb, rows_home)
        tall = (packs, blocks, cap, PAIR)
        spots = pl.ds(pl.multiple_of(sb * cap, cap), cap)
        base_c, base_s = base_ref[0, spots, :], base_ref[1, spots, :]
        lane = lax.broadcasted_iota(jnp.int32, (rows_home, PAIR), 1)
        low_half = lane % HDIM < turn_by
        plain = lane % HDIM >= ROT
        parts_c, parts_s = [], []
        for m in range(packs):
            for t in range(blocks):
                row_c, row_s = turn_ref[m, t, 0:1, :], turn_ref[m, t, 1:2, :]
                parts_c.append(base_c * row_c - base_s * row_s)
                parts_s.append(base_s * row_c + base_c * row_s)
        cosine = jnp.where(plain, 1.0, jnp.concatenate(parts_c, axis=0))
        sine = jnp.concatenate(parts_s, axis=0)
        signed = jnp.where(plain, 0.0, jnp.where(low_half, -sine, sine))
        for kind in range(kinds):
            cols = slice(kind * rows_home, (kind + 1) * rows_home)
            r = dot(hn[rows, :], wqkv[:, cols], ((1,), (0,))) + bq_row[0:1, cols]
            for p in range(pairs):
                x = r[:, p * PAIR:(p + 1) * PAIR]
                if kind < 2:
                    x = rotated(x, cosine, signed, low_half)
                qkv[sb, :, :, :, kind * rows_home + p * PAIR:kind * rows_home + (p + 1) * PAIR] = (
                    x.astype(bf16).reshape(tall)
                )
        d = dot(gy[rows, :], dense[...], ((1,), (1,)))
        dout[sb] = d.astype(bf16).reshape(packs, blocks, cap, rows_home)

    loop(group // 2, project)
    advance()
    loop_tail = group // 2

    def project_tail(sb):
        project(sb + loop_tail)

    loop(group - loop_tail, project_tail)
    advance()
    sent(1)
    sent(2)
    for n in range(3):
        arrived(TILES + n)

    scale = 1.0 / math.sqrt(HDIM)
    lane = lax.broadcasted_iota(jnp.int32, (BLOCK, PAIR), 1)
    causal = lax.broadcasted_iota(jnp.int32, (BLOCK, BLOCK), 1) <= lax.broadcasted_iota(
        jnp.int32, (BLOCK, BLOCK), 0
    )
    zero = jnp.zeros((), bf16)
    first_head = lane < HDIM
    low_half = lane % HDIM < turn_by
    plain = lane % HDIM >= ROT

    def attend(p, m, steps):
        def lanes(kind):
            return pl.ds(pl.multiple_of(kind * rows_home + p * PAIR, PAIR), PAIR)

        def rows_of(kind, j):
            return qkv[:, m, j, :, lanes(kind)].reshape(BLOCK, PAIR)

        def turn_back(x, j):
            row_c, row_s = turn_ref[m, j, 0:1, :], turn_ref[m, j, 1:2, :]
            cosine = jnp.where(plain, 1.0, base_ref[0] * row_c - base_ref[1] * row_s)
            sine = base_ref[1] * row_c + base_ref[0] * row_s
            signed = jnp.where(plain, 0.0, jnp.where(low_half, sine, -sine))
            return rotated(x, cosine, signed, low_half)

        for j in range(blocks):
            ks[j * BLOCK:(j + 1) * BLOCK, :] = rows_of(1, j)
            vs[j * BLOCK:(j + 1) * BLOCK, :] = rows_of(2, j)
        dks[...] = jnp.zeros_like(dks)
        dvs[...] = jnp.zeros_like(dvs)

        def put(ref, j, kind, value):
            ref[:, m, j, :, lanes(kind)] = value.reshape(group, cap, PAIR)

        def summed(value):
            return jnp.sum(value.astype(f32), axis=0, keepdims=True)

        total_q = jnp.zeros((1, PAIR), f32)
        for j in range(blocks):
            first = max(0, j - MAXBLK + 1)
            keys_at = slice(first * BLOCK, (j + 1) * BLOCK)
            q_all = rows_of(0, j)
            do_all = dout[:, m, j, :, pl.ds(pl.multiple_of(p * PAIR, PAIR), PAIR)].reshape(BLOCK, PAIR)
            keys, values = ks[keys_at, :], vs[keys_at, :]
            bias = jnp.where(kid_ref[m, :, keys_at] == begin_ref[m, j], 0.0, NEG)
            long = (j - first) * BLOCK
            outs, dqs = [], []
            for head in range(PAIR // HDIM):
                mine = first_head if head == 0 else jnp.logical_not(first_head)
                q = jnp.where(mine, q_all, zero)
                do = jnp.where(mine, do_all, zero)
                scores = dot(q, keys, ((1,), (1,))) * scale + bias
                tail = jnp.where(causal, scores[:, long:], NEG)
                scores = jnp.concatenate([scores[:, :long], tail], axis=1) if long else tail
                top = jnp.max(scores, axis=1, keepdims=True)
                expo = jnp.exp(scores - top)
                probs = expo * (1.0 / jnp.sum(expo, axis=1, keepdims=True))
                low_probs = probs.astype(bf16)
                outs.append(dot(low_probs, values, ((1,), (0,))))
                dprobs = dot(do, values, ((1,), (1,)))
                weighted = probs * dprobs
                delta = jnp.sum(weighted, axis=1, keepdims=True)
                dscores = (weighted - probs * delta).astype(bf16)
                dqs.append(dot(dscores, keys, ((1,), (0,))))
                dks[keys_at, :] += dot(dscores, q, ((0,), (0,)))
                dvs[keys_at, :] += dot(low_probs, do, ((0,), (0,)))
            put(ob, j, 0, jnp.where(first_head, outs[0], outs[1]).astype(bf16))
            dq = turn_back(jnp.where(first_head, dqs[0], dqs[1]) * scale, j).astype(bf16)
            put(dqkv, j, 0, dq)
            total_q += summed(dq)
            if j in (3, 5):
                half_step(*steps[j // 4])
        total_k = jnp.zeros((1, PAIR), f32)
        total_v = jnp.zeros((1, PAIR), f32)
        for j in range(blocks):
            here = slice(j * BLOCK, (j + 1) * BLOCK)
            dk = turn_back(dks[here, :] * scale, j).astype(bf16)
            dv = dvs[here, :].astype(bf16)
            put(dqkv, j, 1, dk)
            put(dqkv, j, 2, dv)
            total_k += summed(dk)
            total_v += summed(dv)
        half_step(*steps[2])
        for kind, total in enumerate((total_q, total_k, total_v)):
            cols = pl.ds(pl.multiple_of(p * PAIR, PAIR), PAIR)
            past = sums[kind:kind + 1, cols] if m else 0.0
            sums[kind:kind + 1, cols] = past + total

    per = packs * 3
    if done[0] % 2:
        advance()
    start = done[0] // 2

    def attend_pair(p):
        for m in range(packs):
            steps = [(start + (per // 2) * p + (3 * m + n) // 2, (3 * m + n) % 2) for n in range(3)]
            attend(p, m, steps)

    loop(pairs, attend_pair)
    done[0] += per * pairs

    dense_chunk = 2 * TILES

    def turn_round(source, first, kind):
        def step(sb):
            lanes = slice(kind * rows_home, (kind + 1) * rows_home)
            t = source[sb, :, :, :, lanes].reshape(rows_home, rows_home).astype(f32)
            tt[first:first + rows_home, span(sb, rows_home)] = t.T.astype(bf16)

        loop(group, step)

    sent(0)
    arrived(TILES + 3)
    turn_round(ob, 0, 0)
    grad_rows(0, rows_home, 0, 0)
    store_chunk(0, dense_chunk).start()
    advance()
    for kind in range(kinds):
        turn_round(dqkv, (kind % 2) * rows_home, kind)
        spread((kind % 2) * rows_home, kind, dense_chunk + 1 + kind)
        advance()
    store_chunk(0, dense_chunk).wait()
    chain_a(dense_chunk)

    def part(which, q, cols):
        rows = span(q, rows_home)
        if which == 0:
            return dot(act[rows, :], fc2[:, cols], ((1,), (0,))) + dot(
                ob[q].reshape(rows_home, rows_home), dense[:, cols], ((1,), (0,))
            )
        return dot(dup[rows, :], fc1[cols, :], ((1,), (1,))) + dot(
            dqkv[q].reshape(rows_home, kinds * rows_home), wqkv[cols, :], ((1,), (1,))
        )

    chips = part_in.shape[1]

    def give(which, c):
        mine = own(hn, which * chips + c)
        rows = span(which * chips + c, rows_home)

        def step(cb):
            cols = span(cb, wide)
            hn[rows, cols] = part(which, 2 * c + 1 - core, cols).astype(bf16)

        loop(width // wide, step)
        remote(mine, part_in.at[which, c], d_send.at[which * chips + c],
               p_recv.at[which * chips + c], at_shard(flip(1))).start()

    for a in range(2):
        for n in range(7):
            buf = buffers[a]
            remote(own(buf, me), own(buf, me), ag_send.at[a, n], ag_recv.at[a, 1],
                   at_shard(flip(1))).wait_send()
    for which in range(2):
        for first in range(0, chips, 2):
            loop(2, lambda n: give(which, first + n))
            advance()
        sent(which)
        arrived(dense_chunk + 1 + which)
    sent(2)
    arrived(dense_chunk + 3)

    toward, across = 1 + core, 2 - core

    def total(which, c, n, extra):
        chip = chip_of(c)
        rows = span(which * chips + n, rows_home)
        block = part_in.at[which, chip]
        remote(block, block, d_send.at[0], p_recv.at[which * chips + chip],
               at_shard(flip(1))).wait_recv()
        copies = [local(block, tt.at[0:rows_home, :], load.at[0])]
        if extra:
            block = mid_in.at[which]
            remote(block, block, k_send.at[0], m_recv.at[which], at_shard(flip(2))).wait_recv()
            copies.append(local(block, tt.at[rows_home:2 * rows_home, :], load.at[1]))
        for copy in copies:
            copy.start()
        for copy in copies:
            copy.wait()

        def step(cb):
            cols = span(cb, wide)
            acc = part(which, 2 * chip + core, cols) + tt[0:rows_home, cols].astype(f32)
            if extra:
                acc = acc + tt[rows_home:2 * rows_home, cols].astype(f32)
            gy[rows, cols] = acc.astype(bf16)

        loop(width // wide, step)
        return own(gy, which * chips + n)

    def keep(which, c, n, target, recv, to):
        src = total(which, c, n, n == 2)
        if n == 3:
            local(src, target, k_send.at[which * chips + n]).start()
        else:
            remote(src, target, k_send.at[which * chips + n], recv,
                   at_shard(2 * chip_of(to) + core)).start()

    for which in range(2):
        keep(which, 3, 0, mid_in.at[which], m_recv.at[which], toward)
    advance()
    for which in range(2):
        keep(which, toward, 1, home.at[which, 1], h_recv.at[3 * which + 1], toward)
        advance()
    for which in range(2):
        keep(which, 0, 3, home.at[which, 0], None, 0)
    advance(WAIT)
    for which in range(2):
        keep(which, across, 2, home.at[which, 2], h_recv.at[3 * which + 2], across)
        advance()
    advance(HOLD)

    again = [local(tokens, gst.at[0], load.at[0]), local(cotangent, gst.at[1], load.at[1])]
    for copy in again:
        copy.start()
    again[0].wait()
    sort_rows(0, put_tt(0))
    again[1].wait()
    sort_rows(1, put_tt(rows_home))
    advance()
    for n in range(2 * chips):
        block = part_in.at[n // chips, n % chips]
        remote(block, block, d_send.at[n], p_recv.at[n], at_shard(flip(1))).wait_send()
    bring = []
    for which in range(2):
        block = home.at[which, 0]
        local(own(gy, which * chips + 3), block, k_send.at[which * chips + 3]).wait()
        for c in range(3):
            block = home.at[which, c]
            if c:
                remote(block, block, k_send.at[0], h_recv.at[3 * which + c],
                       at_shard(flip(2))).wait_recv()
            bring.append(local(block, own(hn, 3 * which + c), load.at[3 * which + c]))
            bring[-1].start()
    advance()
    for copy in bring:
        copy.wait()
    gain = full[0:1, :]
    out_bias = full[2:3, :] + full[3:4, :]
    full[8:16, :] = jnp.zeros((8, width), f32)

    def finish(rb):
        rows = span(rb, few)
        keep = valid_ref[rows, :]
        x = tt[rows, :].astype(f32)
        g = tt[pl.ds(pl.multiple_of(rows_home + rb * few, few), few), :].astype(f32)
        branch, dh = out_bias, 0.0
        for c in range(3):
            branch = branch + hn[pl.ds(pl.multiple_of(c * rows_home + rb * few, few), few), :].astype(f32)
            dh = dh + hn[
                pl.ds(pl.multiple_of((3 + c) * rows_home + rb * few, few), few), :
            ].astype(f32)
        gst[0, rows, :] = (x + branch * keep).astype(bf16)
        xhat, rstd = statistics(x)
        scaled = dh * gain
        dx = (
            scaled
            - jnp.mean(scaled, axis=1, keepdims=True)
            - xhat * jnp.mean(scaled * xhat, axis=1, keepdims=True)
        ) * rstd
        gst[1, rows, :] = (g + dx).astype(bf16)
        full[8:9, :] += jnp.sum(g * keep, axis=0, keepdims=True)
        full[9:10, :] += jnp.sum(dh * xhat, axis=0, keepdims=True)
        full[10:11, :] += jnp.sum(dh, axis=0, keepdims=True)

    loop(rows_home // few, finish)
    for which, out in enumerate((mixed_out, token_out)):
        for m in range(packs):
            rows = slice(m * pack_rows, (m + 1) * pack_rows)

            def step(cb):
                cols = span(cb, wide)
                tt[which * rows_home + m * pack_rows:which * rows_home + (m + 1) * pack_rows, cols] = dot(
                    select_ref[m], gst[which, rows, cols], ((0,), (0,))
                ).astype(bf16)

            loop(width // wide, step)
        local(tt.at[which * rows_home:(which + 1) * rows_home, :], out, load.at[which]).start()
    advance()

    for d in range(group):
        cols = slice(d * rows_home, (d + 1) * rows_home)
        vsend[d, 0:3, :] = full[8:11, cols]
        for n in range(kinds):
            piece = kinds * d + n
            vsend[d, 3 + n:4 + n, :] = jnp.where(
                me == piece % group, sums[piece // group:piece // group + 1, :], 0.0
            )
    for e in range(1, 8):
        d = flip(e)
        remote(vsend.at[d], vgot.at[me], v_send.at[1], v_recv.at[1], at_shard(d)).start()
    vgot[me] = vsend[me]
    block = vgot.at[0:7]
    local(block, block, v_recv.at[1]).wait()
    advance()
    total = vgot[0]
    for q in range(1, group):
        total = total + vgot[q]
    zgot[rep, 0:6, :] = total[0:6, :]
    zgot[rep, 6:6 + TILES, :] = sums[6:6 + TILES, :]
    for z in range(1, 4):
        remote(zgot.at[rep], zgot.at[rep], v_send.at[2], v_recv.at[2],
               at_rep((rep + z) % 4)).start()
    block = zgot.at[0:3]
    local(block, block, v_recv.at[2]).wait()
    vec_out[...] = (zgot[0] + zgot[1]) + (zgot[2] + zgot[3])
    local(block, block, v_send.at[2]).wait()
    block = vsend.at[0:7]
    local(block, block, v_send.at[1]).wait()
    block = vecs.at[0:7]
    local(block, block, v_send.at[0]).wait()

    advance(last_half + 1)

    @pl.when(outer)
    def _():
        def end(u):
            g, a, b, t = unit(u)
            remote(g, a, za_s.at[u], za_r.at[u], at_rep(near)).wait_send()
            remote(g, t, zc_s.at[u], zc_r.at[u], at_rep(near)).wait_recv()

        loop(units, end)

    @pl.when(inner)
    def _():
        for u in range(units - SLOTS, units):
            t = unit(u)[3]
            past = pb.at[u % SLOTS]
            remote(past, t, zc_s.at[u], zc_r.at[u], at_rep(near)).wait_send()
            local(past, t, zt.at[u]).wait()

    for which, out in enumerate((mixed_out, token_out)):
        local(tt.at[which * rows_home:(which + 1) * rows_home, :], out, load.at[which]).wait()
    for which in range(2):
        for n in range(3):
            block = home.at[which, n]
            remote(block, block, k_send.at[which * chips + n], m_recv.at[which],
                   at_shard(flip(2))).wait_send()
    for block, sem in (
        (fc1.at[0:4 * rows_home, 0:EARLY * tile], w_send.at[0]),
        (wqkv.at[0:7 * rows_home, :], w_send.at[1]),
        (fc1.at[0:7 * rows_home, EARLY * tile:], w_send.at[2]),
        (fc1.at[0:3 * rows_home, 0:EARLY * tile], x_send.at[0]),
    ):
        local(block, block, sem).wait()


def widen_kernel(sums, fc2, fc1, dense, qkv, low, high, in_sem, out_sem):
    chunks, rows, width = sums.shape
    tile = rows
    ff = fc2.shape[0]

    def bring(c):
        return pltpu.make_async_copy(sums.at[c], low.at[c % 3], in_sem.at[c % 3])

    def take(c):
        slot = high.at[c % 3]
        if c < TILES:
            pairs = [(slot, fc2.at[c * rows:(c + 1) * rows, :])]
        elif c < 2 * TILES:
            pairs = [
                (
                    slot.at[:, q * tile:(q + 1) * tile],
                    fc1.at[:, q * ff + (c - TILES) * tile:q * ff + (c - TILES + 1) * tile],
                )
                for q in range(width // tile)
            ]
        elif c == 2 * TILES:
            pairs = [(slot, dense)]
        else:
            k = c - 2 * TILES - 1
            pairs = [(slot, qkv.at[:, k * width:(k + 1) * width])]
        return [
            pltpu.make_async_copy(src, dst, out_sem.at[c % 3, n]) for n, (src, dst) in enumerate(pairs)
        ]

    for c in range(2):
        bring(c).start()
    for c in range(chunks):
        bring(c).wait()
        if c + 2 < chunks:
            bring(c + 2).start()
        if c >= 3:
            for copy in take(c - 3):
                copy.wait()

        def step(rb, _):
            at = pl.ds(pl.multiple_of(rb * 32, 32), 32)
            high[c % 3, at, :] = low[c % 3, at, :].astype(jnp.float32)
            return 0

        lax.fori_loop(0, rows // 32, step, 0)
        for copy in take(c):
            copy.start()
    for c in range(chunks - 3, chunks):
        for copy in take(c):
            copy.wait()


def fused(begins, key_id, base, turns, select, valid, vec, tokens, cotangent, fc1_w, qkv_w, fc2_w,
          dense_w, group):
    bf16, f32 = jnp.bfloat16, jnp.float32
    rows, width = tokens.shape
    ff = fc1_w.shape[1] // group
    tile = ff // TILES
    packs, blocks = begins.shape
    cap = rows // packs // blocks
    total = group * rows
    chips = group // 2
    chunks = 2 * TILES + 4
    chunk = jax.ShapeDtypeStruct((chunks, rows, width), bf16)
    parts = [jax.ShapeDtypeStruct((2, n, rows, width), bf16) for n in (chips, 3)]
    parts.append(jax.ShapeDtypeStruct((2, rows, width), bf16))
    rows_out = jax.ShapeDtypeStruct((rows, width), bf16)
    out_shape = [chunk] * 4 + parts + [rows_out] * 2 + [
        jax.ShapeDtypeStruct((VROWS, rows), f32)
    ]
    vmem = pl.BlockSpec(memory_space=pltpu.VMEM)
    anywhere = pl.BlockSpec(memory_space=pl.ANY)
    dma = pltpu.SemaphoreType.DMA
    per = (group, packs, blocks, cap)
    pack = blocks * BLOCK
    scratch = [
        pltpu.VMEM((total, width), bf16), pltpu.VMEM((total, width), bf16),
        pltpu.VMEM((width, ff), bf16), pltpu.VMEM((ff, width), bf16),
        pltpu.VMEM((width, 3 * rows), bf16), pltpu.VMEM((rows, width), bf16),
        pltpu.VMEM((total, ff), bf16), pltpu.VMEM((total, ff), bf16),
        pltpu.VMEM(per + (rows,), bf16), pltpu.VMEM(per + (3 * rows,), bf16),
        pltpu.VMEM(per + (3 * rows,), bf16), pltpu.VMEM(per + (rows,), bf16),
        pltpu.VMEM((pack, PAIR), bf16), pltpu.VMEM((pack, PAIR), bf16),
        pltpu.VMEM((pack, PAIR), f32), pltpu.VMEM((pack, PAIR), f32),
        pltpu.VMEM((2 * tile, total), bf16),
        pltpu.VMEM((2, rows, width), bf16), pltpu.VMEM((STAGES, group, rows, rows), bf16),
        pltpu.VMEM((SLOTS, rows // 2, width), bf16), pltpu.VMEM((rows // 2, width), bf16),
        pltpu.VMEM((rows // 2, width), bf16),
        pltpu.VMEM((group, VROWS, rows), f32), pltpu.VMEM((VROWS, width), f32),
        pltpu.VMEM((VROWS, rows), f32), pltpu.VMEM((group, VROWS, rows), f32),
        pltpu.VMEM((group, VROWS, rows), f32), pltpu.VMEM((4, VROWS, rows), f32),
        pltpu.VMEM((8, 3 * rows), f32),
        dma((9,)), dma((2, 7)), dma((2, 8)), dma((3,)), dma((TILES + 1,)), dma((1,)),
        dma((TILES,)), dma((2,)), dma((STAGES,)), dma((STAGES,)), dma((chunks,)),
        dma((2 * chunks,)), dma((2 * chunks,)), dma((2 * chunks,)), dma((2 * chunks,)),
        dma((2 * chunks,)), dma((2 * chunks,)), dma((2 * chunks,)), dma((3,)),
        dma((2 * chips,)), dma((2 * chips,)), dma((6,)), dma((2 * chips,)), dma((2,)), dma((3,)),
        dma((3,)),
    ]
    flops = 6 * total * width * (2 * ff + 4 * rows)
    outs = pl.pallas_call(
        fused_kernel,
        in_specs=[pl.BlockSpec(memory_space=pltpu.SMEM)] + [vmem] * 5 + [anywhere] * 7,
        out_specs=[anywhere] * 9 + [vmem],
        out_shape=out_shape,
        scratch_shapes=scratch,
        compiler_params=pltpu.CompilerParams(
            vmem_limit_bytes=60 << 20, collective_id=0, has_side_effects=True
        ),
        cost_estimate=pl.CostEstimate(
            flops=flops, bytes_accessed=64 << 20, transcendentals=total * ff
        ),
    )(begins, key_id, base, turns, select, valid, vec, tokens, cotangent, fc1_w, qkv_w, fc2_w, dense_w)
    sums = outs[3]
    shapes = ((ff, width), (rows, group * ff), (rows, width), (rows, 3 * width))
    grad_fc2, grad_fc1, grad_dense, grad_qkv = pl.pallas_call(
        widen_kernel,
        in_specs=[anywhere],
        out_specs=[anywhere] * 4,
        out_shape=[jax.ShapeDtypeStruct(shape, f32) for shape in shapes],
        scratch_shapes=[
            pltpu.VMEM((3, rows, width), bf16), pltpu.VMEM((3, rows, width), f32), dma((3,)),
            dma((3, group)),
        ],
        compiler_params=pltpu.CompilerParams(vmem_limit_bytes=24 << 20),
    )(sums)
    return outs[7], outs[8], outs[9], grad_qkv, grad_dense, grad_fc1, grad_fc2


def spread_layer(
    gy_home, hn_home, begins, key_id, qkv_weight, b_qkv, dense_weight, fc1_weight, b_fc1, fc2_weight
):
    bf16, f32 = jnp.bfloat16, jnp.float32
    group, reps = lax.axis_size("shard"), lax.axis_size("rep")
    width = gy_home.shape[1]
    rows = gy_home.shape[0] // MICRO
    cap = rows // group
    mine = width // group
    ff_mine = fc1_weight.shape[1] // group
    blocks = begins.shape[1]
    all_rows = MICRO * rows * group

    fc1 = lax.all_to_all(
        fc1_weight.reshape(mine, group, ff_mine).transpose(1, 0, 2), "shard", 0, 0, tiled=True
    ).reshape(width, ff_mine)
    w_qkv = lax.all_to_all(
        qkv_weight.reshape(mine, 3, group, mine).transpose(2, 0, 1, 3), "shard", 0, 0, tiled=True
    ).reshape(width, 3 * mine)

    gy = lax.all_gather(gy_home, "shard", axis=0, tiled=True)
    hn = lax.all_gather(hn_home, "shard", axis=0, tiled=True)

    upper = dot(hn, fc1, ((1,), (0,))) + b_fc1
    inner = math.sqrt(2.0 / math.pi) * (upper + 0.044715 * upper * upper * upper)
    curve = jnp.tanh(inner)
    act = (0.5 * upper * (1.0 + curve)).astype(bf16)
    slope = 0.5 * (1.0 + curve) + 0.5 * upper * (1.0 - curve * curve) * math.sqrt(
        2.0 / math.pi
    ) * (1.0 + 3 * 0.044715 * upper * upper)
    dup = (dot(gy, fc2_weight, ((1,), (1,))) * slope).astype(bf16)
    g_fc2 = dot(act, gy, ((0,), (0,)), f32).astype(bf16)
    g_fc1 = dot(hn, dup, ((0,), (0,)), f32).astype(bf16)

    def over_reps(part):
        return lax.psum_scatter(part, "rep", scatter_dimension=0, tiled=True)

    def from_reps(part):
        return lax.all_gather(part, "rep", axis=0, tiled=True)

    def by_rows(grad):
        cols = grad.shape[1]
        split = grad.reshape(group, reps, mine // reps, cols).transpose(1, 0, 2, 3)
        part = over_reps(split.reshape(reps * group, mine // reps, cols))
        part = lax.all_to_all(part, "shard", 0, 0, tiled=True)
        whole = from_reps(part)
        return whole.reshape(reps, group, mine // reps, cols)

    grad_fc2 = from_reps(over_reps(g_fc2)).astype(f32)
    grad_fc1 = by_rows(g_fc1).transpose(0, 2, 1, 3).reshape(mine, -1).astype(f32)

    qkv = dot(hn, w_qkv, ((1,), (0,))) + b_qkv
    dout = dot(gy, dense_weight, ((1,), (1,)))
    shape = (group, MICRO, blocks, cap)
    ob, dq, dk, dv = attention(
        begins, qkv.reshape(*shape, 3 * mine), dout.reshape(*shape, mine), key_id
    )
    ob = ob.reshape(all_rows, mine).astype(bf16)
    dqkv = jnp.concatenate(
        [part.reshape(all_rows, mine).astype(bf16) for part in (dq, dk, dv)], axis=1
    )
    g_qkv = dot(hn, dqkv, ((0,), (0,)), f32).astype(bf16)
    g_dense = dot(ob, gy, ((0,), (0,)), f32).astype(bf16)
    grad_dense = from_reps(over_reps(g_dense)).astype(f32)
    grad_qkv = by_rows(g_qkv).reshape(reps, group, mine // reps, 3, mine)
    grad_qkv = grad_qkv.transpose(0, 2, 3, 1, 4).reshape(mine, 3 * width).astype(f32)

    def home(part):
        got = lax.all_to_all(part.reshape(group, MICRO * rows, width), "shard", 0, 0, tiled=True)
        return jnp.sum(got.astype(f32), axis=0)

    out_part = (
        dot(act, fc2_weight, ((1,), (0,))) + dot(ob, dense_weight, ((1,), (0,)))
    ).astype(bf16)
    dh_part = (dot(dqkv, w_qkv, ((1,), (1,))) + dot(dup, fc1, ((1,), (1,)))).astype(bf16)
    v_qkv = jnp.sum(dqkv.astype(f32), axis=0).reshape(3, mine)
    v_fc1 = jnp.sum(dup.astype(f32), axis=0)
    return (
        home(out_part), home(dh_part), grad_qkv, grad_dense, grad_fc1, grad_fc2, v_qkv, v_fc1
    )


def fused_layer(
    tokens, cotangent, select, valid_home, begins, key_id, ln_gain, ln_bias, qkv_weight, qkv_bias,
    dense_weight, dense_bias, fc1_weight, fc1_bias, fc2_weight, fc2_bias,
):
    f32 = jnp.float32
    group = lax.axis_size("shard")
    rows = tokens.shape[0]
    half = ROT // 2
    lane = np.arange(PAIR) % HDIM
    freqs = np.exp(-math.log(10000.0) * np.arange(half) * 2.0 / ROT).astype(np.float32)[lane % half]
    spots = np.arange(BLOCK)[:, None] * freqs[None, :].astype(np.float64)
    base = jnp.asarray(np.stack([np.cos(spots), np.sin(spots)]).astype(np.float32))
    steps = np.arange(MAXBLK)[:, None] * BLOCK * freqs[None, :].astype(np.float64)
    table = jnp.asarray(np.stack([np.cos(steps), np.sin(steps)], axis=1).astype(np.float32))
    blocks = jnp.arange(begins.shape[1], dtype=jnp.int32)
    offset = blocks[None, :] - begins
    turns = jnp.sum(jnp.where(
        offset[:, :, None, None, None] == jnp.arange(MAXBLK, dtype=jnp.int32)[:, None, None],
        table, 0.0,
    ), axis=2)
    vec = jnp.concatenate(
        [ln_gain, ln_bias, dense_bias, fc2_bias, qkv_bias, fc1_bias]
    ).astype(f32).reshape(-1, rows)
    vec = jnp.pad(vec, ((0, VROWS - vec.shape[0]), (0, 0)))
    mixed, token_grad, sums, grad_qkv, grad_dense, grad_fc1, grad_fc2 = fused(
        begins, key_id, base, turns, select, valid_home.astype(f32), vec, tokens, cotangent,
        fc1_weight, qkv_weight, fc2_weight, dense_weight, group,
    )
    bias_out, gain_grad, lnb_grad = sums[0], sums[1], sums[2]
    return (
        mixed, token_grad, gain_grad, lnb_grad, grad_qkv, sums[3:6].reshape(-1), grad_dense,
        bias_out, grad_fc1, sums[6:6 + TILES].reshape(-1), grad_fc2, bias_out,
    )


def body(
    tokens, cotangent, placement_order, seq_lengths, ln_gain, ln_bias, qkv_weight, qkv_bias,
    dense_weight, dense_bias, fc1_weight, fc1_bias, fc2_weight, fc2_bias,
):
    bf16, f32 = jnp.bfloat16, jnp.float32
    group = lax.axis_size("shard")
    reps = lax.axis_size("rep")
    me = lax.axis_index("shard")
    width = tokens.shape[1]
    rows = tokens.shape[0] // MICRO
    cap = rows // group
    mine = width // group
    ff_mine = fc1_weight.shape[1] // group
    blocks = seq_lengths.shape[2]
    all_rows = MICRO * rows * group

    begins, limits = block_begins(seq_lengths[0])
    spot = jnp.arange(BLOCK, dtype=jnp.int32)
    index = jnp.arange(blocks, dtype=jnp.int32)
    position = (index[None, :, None] - begins[:, :, None]) * BLOCK + spot[None, None, :]
    valid = position < limits[:, :, None]
    key_id = jnp.where(valid, begins[:, :, None], -1).reshape(MICRO, 1, blocks * BLOCK)

    orders = placement_order[0, 0]
    select = (orders[:, None, :] == jnp.arange(rows, dtype=jnp.int32)[None, :, None]).astype(bf16)

    valid_home = lax.dynamic_index_in_dim(
        valid.reshape(MICRO, group, group, cap), me, 2, keepdims=False
    ).reshape(MICRO * rows, 1)
    held = 2 * MICRO * rows * group * (2 * width + 2 * ff_mine + 7 * mine)
    held += 2 * width * (2 * ff_mine + 4 * mine)
    if (group, reps) == (8, 4) and cap % 16 == 0 and held <= FUSED_BYTES:
        return fused_layer(
            tokens, cotangent, select, valid_home, begins, key_id, ln_gain, ln_bias, qkv_weight,
            qkv_bias, dense_weight, dense_bias, fc1_weight, fc1_bias, fc2_weight, fc2_bias,
        )

    pieces = (ln_gain, ln_bias, dense_bias, fc2_bias, qkv_bias, fc1_bias)
    packed = jnp.concatenate(pieces)
    spread = lax.all_gather(packed, "shard", axis=0).astype(f32)
    full, at = [], 0
    for piece in pieces:
        full.append(spread[:, at:at + piece.shape[0]].reshape(-1))
        at += piece.shape[0]
    gain, lnb, b_dense, b_fc2, b_qkv, b_fc1 = full
    b_qkv = lax.dynamic_slice_in_dim(b_qkv.reshape(3, width), me * mine, mine, 1).reshape(-1)
    b_fc1 = lax.dynamic_slice_in_dim(b_fc1, me * ff_mine, ff_mine, 0)

    def arrange(array):
        return jnp.einsum(
            "mti,mid->mtd", select, array.reshape(MICRO, rows, width),
            preferred_element_type=f32,
        ).astype(bf16).reshape(MICRO * rows, width)

    x_home, g_home = arrange(tokens), arrange(cotangent)
    gy_home = jnp.where(valid_home, g_home, jnp.zeros((), bf16))
    x32 = x_home.astype(f32)
    centered = x32 - jnp.mean(x32, axis=1, keepdims=True)
    rstd = lax.rsqrt(jnp.mean(centered * centered, axis=1, keepdims=True) + 1e-05)
    hn_home = (centered * rstd * gain + lnb).astype(bf16)
    split = (
        gy_home, hn_home, begins, key_id, qkv_weight, b_qkv, dense_weight, fc1_weight, b_fc1,
        fc2_weight,
    )
    result = spread_layer(*split)
    out_sum, dh, grad_qkv, grad_dense, grad_fc1, grad_fc2, v_qkv, v_fc1 = result
    branch = out_sum + (b_dense + b_fc2)
    mixed = (x32 + jnp.where(valid_home, branch, 0.0)).astype(bf16)
    xhat = centered * rstd
    scaled = dh * gain
    dx = (
        scaled
        - jnp.mean(scaled, axis=1, keepdims=True)
        - xhat * jnp.mean(scaled * xhat, axis=1, keepdims=True)
    ) * rstd
    token_grad = (g_home.astype(f32) + dx).astype(bf16)

    def back(array):
        return jnp.einsum(
            "mti,mtd->mid", select, array.reshape(MICRO, rows, width),
            preferred_element_type=f32,
        ).astype(bf16).reshape(MICRO * rows, width)

    v_out = jnp.sum(gy_home.astype(f32), axis=0)
    v_gain = jnp.sum(dh * xhat, axis=0)
    v_lnb = jnp.sum(dh, axis=0)
    mixed_vec = jnp.concatenate([v_qkv.reshape(-1), v_fc1, v_out, v_gain, v_lnb])
    table = lax.all_gather(mixed_vec, ("rep", "shard"), axis=0).reshape(reps, group, -1)
    table = jnp.sum(table, axis=0)
    at = 3 * mine
    bias_qkv = table[:, :at].reshape(group, 3, mine).transpose(1, 0, 2).reshape(-1)
    bias_qkv = lax.dynamic_slice_in_dim(bias_qkv, me * 3 * mine, 3 * mine, 0)
    bias_fc1 = lax.dynamic_index_in_dim(table[:, at:at + ff_mine], me, 0, keepdims=False)
    full = jnp.sum(table[:, at + ff_mine:], axis=0).reshape(3, group, mine)
    bias_out, gain_grad, lnb_grad = lax.dynamic_index_in_dim(full, me, 1, keepdims=False)
    return (
        back(mixed), back(token_grad), gain_grad, lnb_grad, grad_qkv, bias_qkv, grad_dense,
        bias_out, grad_fc1, bias_fc1, grad_fc2, bias_out,
    )


def solution(mesh):
    rows = P(("rep", "shard"), None)
    vector, matrix = P("shard"), P("shard", None)
    layer = (vector, vector, matrix, vector, matrix, vector, matrix, vector, matrix, vector)
    return jax.shard_map(
        body,
        mesh=mesh,
        in_specs=(rows, rows, P("rep", "shard", None, None), P("rep", None, None)) + layer,
        out_specs=(rows, rows) + layer,
        check_vma=False,
    )
```

```python
import math

import jax
import jax.numpy as jnp
import numpy as np
from jax import lax
from jax.experimental import pallas as pl
from jax.experimental.pallas import tpu as pltpu
from jax.sharding import PartitionSpec as P

HEADS = 32
HDIM = 64
ROT = 32
BLOCK = 128
MICRO = 2
MAXBLK = 8
PAIR = 2 * HDIM
NEG = -1e30
FUSED_BYTES = 48 << 20


def dot(left, right, dims, out=jnp.float32):
    return lax.dot_general(left, right, (dims, ((), ())), preferred_element_type=out)


def block_begins(lengths):
    blocks = jnp.arange(lengths.shape[1], dtype=jnp.int32)
    started = (lengths[:, None, :] > 0) & (blocks[None, None, :] <= blocks[None, :, None])
    begins = jnp.max(jnp.where(started, blocks[None, None, :], 0), axis=2)
    own = begins[:, :, None] == blocks[None, None, :]
    limits = jnp.sum(jnp.where(own, lengths[:, None, :], 0), axis=2)
    return begins, limits


def rotary_tables():
    half = ROT // 2
    lane = np.arange(PAIR) % HDIM
    freqs = np.exp(-math.log(10000.0) * np.arange(half) * 2.0 / ROT).astype(np.float32)
    position = np.arange(MAXBLK * BLOCK, dtype=np.float32)
    angles = (position[:, None] * freqs[lane % half][None, :]).astype(np.float64)
    sines = np.sin(angles)
    cosine = np.where(lane < ROT, np.cos(angles), 1.0)
    signed = np.where(lane < half, -sines, np.where(lane < ROT, sines, 0.0))
    return [jnp.asarray(t.astype(np.float32)) for t in (cosine, signed)]


def attention_kernel(begin_ref, q_ref, k_ref, v_ref, do_ref, cos_ref, sin_ref, kid_ref,
                     ob_ref, dq_ref, dk_ref, dv_ref, ks, vs, dks, dvs):
    micro = pl.program_id(0)
    blocks = q_ref.shape[1]
    lane = lax.broadcasted_iota(jnp.int32, (BLOCK, PAIR), 1)
    half = ROT // 2

    def rows(ref, j):
        return ref[:, j].reshape(BLOCK, PAIR)

    def table(ref, j):
        return ref[pl.ds(pl.multiple_of((j - begin_ref[micro, j]) * BLOCK, BLOCK), BLOCK), :]

    def turn(x, j, back):
        other = jnp.where(
            lane % HDIM < half, pltpu.roll(x, PAIR - half, 1), pltpu.roll(x, half, 1)
        ) * table(sin_ref, j)
        straight = x * table(cos_ref, j)
        return straight - other if back else straight + other

    for j in range(blocks):
        ks[j * BLOCK:(j + 1) * BLOCK, :] = turn(rows(k_ref, j), j, False).astype(jnp.bfloat16)
        vs[j * BLOCK:(j + 1) * BLOCK, :] = rows(v_ref, j).astype(jnp.bfloat16)
    dks[...] = jnp.zeros_like(dks)
    dvs[...] = jnp.zeros_like(dvs)
    causal = lax.broadcasted_iota(jnp.int32, (BLOCK, BLOCK), 1) <= lax.broadcasted_iota(
        jnp.int32, (BLOCK, BLOCK), 0
    )
    scale = 1.0 / math.sqrt(HDIM)
    zero = jnp.zeros((), jnp.bfloat16)
    for j in range(blocks):
        first = max(0, j - MAXBLK + 1)
        span = slice(first * BLOCK, (j + 1) * BLOCK)
        q_all = turn(rows(q_ref, j), j, False).astype(jnp.bfloat16)
        do_all = rows(do_ref, j).astype(jnp.bfloat16)
        keys, values = ks[span, :], vs[span, :]
        same = kid_ref[:, span] == begin_ref[micro, j]
        bias = jnp.where(same, 0.0, NEG)
        width = (j + 1 - first) * BLOCK
        outs, dqs = [], []
        for head in range(PAIR // HDIM):
            mine = (lane >= head * HDIM) & (lane < (head + 1) * HDIM)
            q = jnp.where(mine, q_all, zero)
            do = jnp.where(mine, do_all, zero)
            scores = dot(q, keys, ((1,), (1,))) * scale + bias
            tail = jnp.where(causal, scores[:, width - BLOCK:], NEG)
            if width > BLOCK:
                scores = jnp.concatenate([scores[:, :width - BLOCK], tail], axis=1)
            else:
                scores = tail
            top = jnp.max(scores, axis=1, keepdims=True)
            expo = jnp.exp(scores - top)
            probs = expo / jnp.sum(expo, axis=1, keepdims=True)
            low_probs = probs.astype(jnp.bfloat16)
            outs.append(dot(low_probs, values, ((1,), (0,))))
            dprobs = dot(do, values, ((1,), (1,)))
            weighted = probs * dprobs
            delta = jnp.sum(weighted, axis=1, keepdims=True)
            dscores = (weighted - probs * delta).astype(jnp.bfloat16)
            dqs.append(dot(dscores, keys, ((1,), (0,))))
            dks[span, :] += dot(dscores, q, ((0,), (0,)))
            dvs[span, :] += dot(low_probs, do, ((0,), (0,)))
        first_head = lane < HDIM
        shape = (q_ref.shape[0], q_ref.shape[2], PAIR)
        ob = jnp.where(first_head, outs[0], outs[1])
        ob_ref[:, j] = ob.astype(jnp.bfloat16).astype(jnp.float32).reshape(shape)
        dq = turn(jnp.where(first_head, dqs[0], dqs[1]) * scale, j, True)
        dq_ref[:, j] = dq.astype(jnp.bfloat16).astype(jnp.float32).reshape(shape)
    for j in range(blocks):
        here = slice(j * BLOCK, (j + 1) * BLOCK)
        shape = (q_ref.shape[0], q_ref.shape[2], PAIR)
        dk = turn(dks[here, :] * scale, j, True)
        dk_ref[:, j] = dk.astype(jnp.bfloat16).astype(jnp.float32).reshape(shape)
        dv_ref[:, j] = dvs[here, :].astype(jnp.bfloat16).astype(jnp.float32).reshape(shape)


def attention(begins, qkv, dout, kid):
    group, micros, blocks, cap, _ = qkv.shape
    width = dout.shape[-1]
    pairs = width // PAIR
    total = blocks * BLOCK

    def rows_spec(offset):
        return pl.BlockSpec(
            (group, None, blocks, cap, PAIR), lambda m, p, *_: (0, m, 0, 0, offset + p)
        )

    table_spec = pl.BlockSpec((MAXBLK * BLOCK, PAIR), lambda m, p, *_: (0, 0))
    out = jax.ShapeDtypeStruct(dout.shape, jnp.float32)
    work = micros * pairs * 2 * blocks * (min(blocks, MAXBLK) + 1) // 2 * BLOCK * BLOCK
    return pl.pallas_call(
        attention_kernel,
        grid_spec=pltpu.PrefetchScalarGridSpec(
            num_scalar_prefetch=1,
            grid=(micros, pairs),
            in_specs=[
                rows_spec(0), rows_spec(pairs), rows_spec(2 * pairs), rows_spec(0),
                table_spec, table_spec,
                pl.BlockSpec((None, 1, total), lambda m, p, *_: (m, 0, 0)),
            ],
            out_specs=[rows_spec(0)] * 4,
            scratch_shapes=[
                pltpu.VMEM((total, PAIR), jnp.bfloat16),
                pltpu.VMEM((total, PAIR), jnp.bfloat16),
                pltpu.VMEM((total, PAIR), jnp.float32),
                pltpu.VMEM((total, PAIR), jnp.float32),
            ],
        ),
        out_shape=[out] * 4,
        compiler_params=pltpu.CompilerParams(vmem_limit_bytes=48 << 20),
        cost_estimate=pl.CostEstimate(
            flops=12 * work * PAIR, bytes_accessed=8 * dout.size * 4, transcendentals=work
        ),
    )(begins, qkv, qkv, qkv, dout, *rotary_tables(), kid)


MESH = pl.DeviceIdType.MESH
SLOTS = 5
TILES = 4
VROWS = 16
HOLD = 4
WAIT = 5
STAGES = 3
EARLY = 1


def fused_kernel(
    begin_ref, kid_ref, base_ref, turn_ref, select_ref, valid_ref, vec_in,
    tokens, cotangent, fc1_w, qkv_w, fc2_w, dense_w,
    grad, grad_a, grad_b, grad_t, part_in, home, mid_in, mixed_out, token_out, vec_out,
    gy, hn, fc1, fc2, wqkv, dense, act, dup, ob, dqkv, qkv, dout, ks, vs, dks, dvs, tt, gst, ast,
    pb, va, vb, vecs, full, sums, vsend, vgot, zgot, bq_row,
    load, ag_send, ag_recv, w_send, w_recv, x_send, x_recv, st, g_send, g_own, g_recv, za_s, za_r, zb_s, zb_r, zc_s,
    zc_r, zt, zl, d_send, p_recv, h_recv, k_send, m_recv, v_send, v_recv,
):
    bf16, f32 = jnp.bfloat16, jnp.float32
    me, rep = lax.axis_index("shard"), lax.axis_index("rep")
    core, cx, cy = me % 2, (me // 2) % 2, me // 4
    near = rep + 1 - 2 * (rep % 2)
    far = 3 - rep
    inner = (rep == 1) | (rep == 2)
    outer = (rep == 0) | (rep == 3)
    rows_home = tokens.shape[0]
    width = tokens.shape[1]
    group = width // rows_home
    ff = fc1.shape[1]
    tile = ff // TILES
    wide = 512
    packs = kid_ref.shape[0]
    pack_rows = rows_home // packs
    blocks = kid_ref.shape[2] // BLOCK
    cap = qkv.shape[3]
    pairs = rows_home // PAIR
    kinds = 3

    def flip(e):
        return ((cy + e // 4) % 2) * 4 + ((cx + (e // 2) % 2) % 2) * 2 + (core + e % 2) % 2

    def at_shard(d):
        return {"shard": d}

    def at_rep(d):
        return {"rep": d}

    def remote(src, dst, send, recv, dev):
        return pltpu.make_async_remote_copy(
            src_ref=src, dst_ref=dst, send_sem=send, recv_sem=recv, device_id=dev,
            device_id_type=MESH,
        )

    def local(src, dst, sem):
        return pltpu.make_async_copy(src, dst, sem)

    def span(i, size):
        return pl.ds(pl.multiple_of(i * size, size), size)

    def own(ref, q):
        return ref.at[span(q, rows_home), :]

    def loop(count, step):
        def run(i, _):
            step(i)
            return 0

        lax.fori_loop(0, count, run, 0)

    first_loads = [
        local(cotangent, gst.at[1], load.at[1]),
        local(tokens, gst.at[0], load.at[0]),
    ]
    loads = [
        local(fc1_w.at[:, span(me, ff)], own(fc1, me), load.at[2]),
        local(fc2_w, fc2, load.at[3]),
        local(dense_w, dense, load.at[4]),
        local(vec_in, vecs.at[me], load.at[5]),
    ] + [
        local(
            qkv_w.at[:, span(kind * group + me, rows_home)],
            wqkv.at[span(me, rows_home), pl.ds(kind * rows_home, rows_home)], load.at[6 + kind],
        )
        for kind in range(kinds)
    ]
    for copy in first_loads + loads:
        copy.start()

    barrier = pltpu.get_barrier_semaphore()
    for e in range(1, 8):
        pl.semaphore_signal(barrier, inc=1, device_id=at_shard(flip(e)), device_id_type=MESH)
    for z in range(1, 4):
        pl.semaphore_signal(
            barrier, inc=1, device_id=at_rep((rep + z) % 4), device_id_type=MESH
        )
    pl.semaphore_wait(barrier, 10)

    for e in range(1, 8):
        remote(vec_in, vecs.at[me], v_send.at[0], v_recv.at[0], at_shard(flip(e))).start()
    buffers = (gy, hn)

    def send_own(a):
        buf = buffers[a]
        for n, e in enumerate((2, 4, 1)):
            remote(own(buf, me), own(buf, me), ag_send.at[a, n], ag_recv.at[a, e],
                   at_shard(flip(e))).start()

    def chip_of(c):
        return ((cy + c // 2) % 2) * 2 + (cx + c % 2) % 2

    def in_plane():
        return [2 * chip_of(c) + (core + rep) % 2 for c in (1, 2, 3)]

    def send_fc1(i):
        early = i < EARLY
        for d in [flip(1)] + in_plane() if early else [flip(e) for e in range(1, 8)]:
            remote(
                fc1_w.at[:, pl.ds(pl.multiple_of(d * ff + i * tile, tile), tile)],
                fc1.at[span(me, rows_home), pl.ds(i * tile, tile)],
                w_send.at[0 if early else 2], w_recv.at[i], at_shard(d),
            ).start()

    def send_qkv():
        for e in range(1, 8):
            d = flip(e)
            for kind in range(kinds):
                remote(
                    qkv_w.at[:, span(kind * group + d, rows_home)],
                    wqkv.at[span(me, rows_home), pl.ds(kind * rows_home, rows_home)],
                    w_send.at[1], w_recv.at[TILES], at_shard(d),
                ).start()

    def fc1_part(i, count, sem):
        block = fc1.at[0:count * rows_home, pl.ds(i * tile, tile)]
        return local(block, block, sem)

    def pass_on(i):
        fc1_part(i, 4, w_recv.at[i]).wait()
        for q in in_plane():
            block = fc1.at[span(q, rows_home), pl.ds(i * tile, tile)]
            remote(block, block, x_send.at[0], x_recv.at[i], at_rep(near)).start()

    def ag_wait(a, e):
        buf = buffers[a]
        remote(own(buf, me), own(buf, flip(e)), ag_send.at[a, 0], ag_recv.at[a, e],
               at_shard(flip(e))).wait_recv()

    def forward(a, have, to, n):
        q = own(buffers[a], flip(have))
        remote(q, q, ag_send.at[a, n], ag_recv.at[a, have ^ to], at_shard(flip(to))).start()

    def relay(a):
        ag_wait(a, 2)
        forward(a, 2, 1, 4)

        @pl.when(core == 0)
        def _():
            forward(a, 2, 4, 3)

        ag_wait(a, 4)
        forward(a, 4, 1, 5)

        @pl.when(core == 1)
        def _():
            forward(a, 4, 2, 3)

    def sort_rows(source, put):
        for m in range(packs):
            def step(cb):
                cols = span(cb, wide)
                put(m, cols, dot(
                    select_ref[m], gst[source, m * pack_rows:(m + 1) * pack_rows, cols],
                    ((1,), (0,)),
                ))

            loop(width // wide, step)

    def put_gy(m, cols, value):
        keep = valid_ref[m * pack_rows:(m + 1) * pack_rows, :]
        gy[pl.ds(pl.multiple_of(me * rows_home + m * pack_rows, pack_rows), pack_rows), cols] = (
            value * keep
        ).astype(bf16)

    def put_tt(first):
        def put(m, cols, value):
            tt[first + m * pack_rows:first + (m + 1) * pack_rows, cols] = value.astype(bf16)

        return put

    few = 32

    def statistics(x):
        centered = x - jnp.mean(x, axis=1, keepdims=True)
        rstd = lax.rsqrt(jnp.mean(centered * centered, axis=1, keepdims=True) + 1e-05)
        return centered * rstd, rstd

    for i in range(EARLY):
        send_fc1(i)
    first_loads[0].wait()
    sort_rows(1, put_gy)
    send_own(0)
    first_loads[1].wait()
    sort_rows(0, put_tt(0))
    block = vecs.at[0:7]
    local(block, block, v_recv.at[0]).wait()
    for copy in loads:
        copy.wait()
    for q in range(group):
        cols = slice(q * rows_home, (q + 1) * rows_home)
        full[0:4, cols] = vecs[q, 0:4, :]
    for kind in range(kinds):
        piece = kind * group + me
        bq_row[0:1, kind * rows_home:(kind + 1) * rows_home] = vecs[
            piece // kinds, pl.ds(4 + piece % kinds, 1), :
        ]

    def norm_rows(rb):
        xhat, _ = statistics(tt[span(rb, few), :].astype(f32))
        hn[pl.ds(pl.multiple_of(me * rows_home + rb * few, few), few), :] = (
            xhat * full[0:1, :] + full[1:2, :]
        ).astype(bf16)

    loop(rows_home // few, norm_rows)
    send_own(1)
    for i in range(EARLY):
        pass_on(i)
    for a in range(2):
        relay(a)
    for i in range(EARLY, TILES):
        send_fc1(i)
    send_qkv()
    for a in range(2):
        ag_wait(a, 6)
        forward(a, 6, 1, 6)
    for a in range(2):
        for e in (1, 3, 5, 7):
            ag_wait(a, e)

    half = rows_home // 2
    units = 2 * grad.shape[0]

    def unit(u):
        at = (u // 2, pl.ds(pl.multiple_of((u % 2) * half, half), half), slice(None))
        return [ref.at[at] for ref in (grad, grad_a, grad_b, grad_t)]

    def chain_a(chunk):
        @pl.when(outer)
        def _():
            for u in (2 * chunk, 2 * chunk + 1):
                g, a, _, _ = unit(u)
                remote(g, a, za_s.at[u], za_r.at[u], at_rep(near)).start()

    def add_into(slot, ref):
        few = 32

        def step(rb):
            rows = span(rb, few)
            pb[slot, rows, :] = pb[slot, rows, :] + ref[rows, :]

        loop(half // few, step)

    def b_load(u):
        g, a, _, _ = unit(u)
        return local(g, pb.at[u % SLOTS], zl.at[0]), local(a, va, zl.at[1])

    def b_first(u):
        g, a, _, _ = unit(u)
        remote(g, a, za_s.at[u], za_r.at[u], at_rep(near)).wait_recv()

        def clear():
            t = unit(u - SLOTS)[3]
            past = pb.at[u % SLOTS]
            remote(past, t, zc_s.at[u - SLOTS], zc_r.at[u - SLOTS], at_rep(near)).wait_send()
            local(past, t, zt.at[u - SLOTS]).wait()

        if not isinstance(u, int):
            pl.when(u >= SLOTS)(clear)
        elif u >= SLOTS:
            clear()
        for copy in b_load(u):
            copy.start()

    def b_second(u):
        for copy in b_load(u):
            copy.wait()
        add_into(u % SLOTS, va)
        remote(pb.at[u % SLOTS], unit(u)[2], zb_s.at[u], zb_r.at[u], at_rep(far)).start()

    def c_first(u):
        b = unit(u)[2]
        remote(pb.at[u % SLOTS], b, zb_s.at[u], zb_r.at[u], at_rep(far)).wait_recv()
        local(b, vb, zl.at[2]).start()

    def c_second(u):
        slot = u % SLOTS
        _, _, b, t = unit(u)
        local(b, vb, zl.at[2]).wait()
        remote(pb.at[slot], b, zb_s.at[u], zb_r.at[u], at_rep(far)).wait_send()
        add_into(slot, vb)
        remote(pb.at[slot], t, zc_s.at[u], zc_r.at[u], at_rep(near)).start()
        local(pb.at[slot], t, zt.at[u]).start()

    def half_step(k, odd):
        def known(u):
            return not isinstance(u, int) or 0 <= u < units

        @pl.when(inner)
        def _():
            if odd:
                if known(k):
                    b_second(k)
                if known(k - 2):
                    c_second(k - 2)
            else:
                if known(k):
                    b_first(k)
                if known(k - 2):
                    c_first(k - 2)

    done = [0]
    last_half = 2 * (units + 1) + 1

    def advance(count=1):
        for _ in range(count):
            if done[0] <= last_half:
                half_step(done[0] // 2, done[0] % 2)
                done[0] += 1

    scale_in = math.sqrt(2.0 / math.pi)

    def hidden(i):
        cols = slice(i * tile, (i + 1) * tile)
        bias = vec_in_rows[i]

        def step(rb, total):
            rows = span(rb, rows_home)
            u = dot(hn[rows, :], fc1[:, cols], ((1,), (0,))) + bias
            d = dot(gy[rows, :], fc2[cols, :], ((1,), (1,)))
            square = u * u
            t = jnp.tanh(scale_in * u * (1.0 + 0.044715 * square))
            a = 0.5 * u * (1.0 + t)
            slope = 0.5 * (1.0 + t) + 0.5 * u * (1.0 - t * t) * scale_in * (
                1.0 + 3 * 0.044715 * square
            )
            d = d * slope
            act[rows, cols] = a.astype(bf16)
            tt[0:tile, rows] = a.T.astype(bf16)
            low = d.astype(bf16)
            dup[rows, cols] = low
            tt[tile:2 * tile, rows] = d.T.astype(bf16)
            return total + jnp.sum(low.astype(f32), axis=0, keepdims=True)

        middle = lax.fori_loop(0, group // 2, step, jnp.zeros((1, tile), f32))
        if i:
            advance()
        sums[6 + i:7 + i, :] = lax.fori_loop(group // 2, group, step, middle)

    vec_in_rows = [vecs[me, 7 + i:8 + i, :] for i in range(TILES)]

    def grad_rows(first, height, slot, at):
        def step(cb):
            cols = span(cb, wide)
            gst[slot, at:at + height, cols] = dot(
                tt[first:first + height, :], gy[:, cols], ((1,), (0,))
            ).astype(bf16)

        loop(width // wide, step)

    def store_chunk(slot, chunk):
        return local(gst.at[slot], grad.at[chunk], st.at[slot])

    def place(chunk):
        return grad.at[chunk, :, span(me, rows_home)]

    def sent(slot):
        block = ast.at[slot, 0:7]
        local(block, block, g_send.at[slot]).wait()
        local(ast.at[slot, me], place(0), g_own.at[slot]).wait()

    def spread(first, slot, chunk):
        def step(db):
            g = dot(tt[first:first + rows_home, :], hn[:, span(db, rows_home)], ((1,), (0,)))
            ast[slot, db] = g.T.astype(bf16)

        loop(group, step)
        local(ast.at[slot, me], place(chunk), g_own.at[slot]).start()
        for e in range(1, 8):
            d = flip(e)
            remote(ast.at[slot, d], place(chunk), g_send.at[slot], g_recv.at[chunk],
                   at_shard(d)).start()

    def arrived(chunk):
        block = grad.at[chunk, :, 0:7 * rows_home]
        local(block, block, g_recv.at[chunk]).wait()
        chain_a(chunk)

    for i in range(TILES):
        if i < EARLY:
            fc1_part(i, 3, x_recv.at[i]).wait()
        else:
            fc1_part(i, 7, w_recv.at[i]).wait()
        hidden(i)
        if i:
            advance()
        grad_rows(0, tile, i % 2, 0)
        store_chunk(i % 2, i).start()
        store_chunk(i % 2, i).wait()
        chain_a(i)
        if i:
            advance()
        if i >= STAGES:
            sent(i % STAGES)
        spread(tile, i % STAGES, TILES + i)
        if i:
            advance()

    block = wqkv.at[0:7 * rows_home, :]
    local(block, block, w_recv.at[TILES]).wait()
    turn_by = ROT // 2

    def rotated(x, cosine, signed, low_half):
        other = jnp.where(
            low_half, pltpu.roll(x, x.shape[-1] - turn_by, x.ndim - 1),
            pltpu.roll(x, turn_by, x.ndim - 1),
        )
        return x * cosine + other * signed

    def project(sb):
        rows = span(sb, rows_home)
        tall = (packs, blocks, cap, PAIR)
        spots = pl.ds(pl.multiple_of(sb * cap, cap), cap)
        base_c, base_s = base_ref[0, spots, :], base_ref[1, spots, :]
        lane = lax.broadcasted_iota(jnp.int32, (rows_home, PAIR), 1)
        low_half = lane % HDIM < turn_by
        plain = lane % HDIM >= ROT
        parts_c, parts_s = [], []
        for m in range(packs):
            for t in range(blocks):
                row_c, row_s = turn_ref[m, t, 0:1, :], turn_ref[m, t, 1:2, :]
                parts_c.append(base_c * row_c - base_s * row_s)
                parts_s.append(base_s * row_c + base_c * row_s)
        cosine = jnp.where(plain, 1.0, jnp.concatenate(parts_c, axis=0))
        sine = jnp.concatenate(parts_s, axis=0)
        signed = jnp.where(plain, 0.0, jnp.where(low_half, -sine, sine))
        for kind in range(kinds):
            cols = slice(kind * rows_home, (kind + 1) * rows_home)
            r = dot(hn[rows, :], wqkv[:, cols], ((1,), (0,))) + bq_row[0:1, cols]
            for p in range(pairs):
                x = r[:, p * PAIR:(p + 1) * PAIR]
                if kind < 2:
                    x = rotated(x, cosine, signed, low_half)
                qkv[sb, :, :, :, kind * rows_home + p * PAIR:kind * rows_home + (p + 1) * PAIR] = (
                    x.astype(bf16).reshape(tall)
                )
        d = dot(gy[rows, :], dense[...], ((1,), (1,)))
        dout[sb] = d.astype(bf16).reshape(packs, blocks, cap, rows_home)

    loop(group // 2, project)
    advance()
    loop_tail = group // 2

    def project_tail(sb):
        project(sb + loop_tail)

    loop(group - loop_tail, project_tail)
    advance()
    sent(1)
    sent(2)
    for n in range(3):
        arrived(TILES + n)

    scale = 1.0 / math.sqrt(HDIM)
    lane = lax.broadcasted_iota(jnp.int32, (BLOCK, PAIR), 1)
    causal = lax.broadcasted_iota(jnp.int32, (BLOCK, BLOCK), 1) <= lax.broadcasted_iota(
        jnp.int32, (BLOCK, BLOCK), 0
    )
    zero = jnp.zeros((), bf16)
    first_head = lane < HDIM
    low_half = lane % HDIM < turn_by
    plain = lane % HDIM >= ROT

    def attend(p, m, steps):
        def lanes(kind):
            return pl.ds(pl.multiple_of(kind * rows_home + p * PAIR, PAIR), PAIR)

        def rows_of(kind, j):
            return qkv[:, m, j, :, lanes(kind)].reshape(BLOCK, PAIR)

        def turn_back(x, j):
            row_c, row_s = turn_ref[m, j, 0:1, :], turn_ref[m, j, 1:2, :]
            cosine = jnp.where(plain, 1.0, base_ref[0] * row_c - base_ref[1] * row_s)
            sine = base_ref[1] * row_c + base_ref[0] * row_s
            signed = jnp.where(plain, 0.0, jnp.where(low_half, sine, -sine))
            return rotated(x, cosine, signed, low_half)

        for j in range(blocks):
            ks[j * BLOCK:(j + 1) * BLOCK, :] = rows_of(1, j)
            vs[j * BLOCK:(j + 1) * BLOCK, :] = rows_of(2, j)
        dks[...] = jnp.zeros_like(dks)
        dvs[...] = jnp.zeros_like(dvs)

        def put(ref, j, kind, value):
            ref[:, m, j, :, lanes(kind)] = value.reshape(group, cap, PAIR)

        def summed(value):
            return jnp.sum(value.astype(f32), axis=0, keepdims=True)

        total_q = jnp.zeros((1, PAIR), f32)
        for j in range(blocks):
            first = max(0, j - MAXBLK + 1)
            keys_at = slice(first * BLOCK, (j + 1) * BLOCK)
            q_all = rows_of(0, j)
            do_all = dout[:, m, j, :, pl.ds(pl.multiple_of(p * PAIR, PAIR), PAIR)].reshape(BLOCK, PAIR)
            keys, values = ks[keys_at, :], vs[keys_at, :]
            bias = jnp.where(kid_ref[m, :, keys_at] == begin_ref[m, j], 0.0, NEG)
            long = (j - first) * BLOCK
            outs, dqs = [], []
            for head in range(PAIR // HDIM):
                mine = first_head if head == 0 else jnp.logical_not(first_head)
                q = jnp.where(mine, q_all, zero)
                do = jnp.where(mine, do_all, zero)
                scores = dot(q, keys, ((1,), (1,))) * scale + bias
                tail = jnp.where(causal, scores[:, long:], NEG)
                scores = jnp.concatenate([scores[:, :long], tail], axis=1) if long else tail
                top = jnp.max(scores, axis=1, keepdims=True)
                expo = jnp.exp(scores - top)
                probs = expo * (1.0 / jnp.sum(expo, axis=1, keepdims=True))
                low_probs = probs.astype(bf16)
                outs.append(dot(low_probs, values, ((1,), (0,))))
                dprobs = dot(do, values, ((1,), (1,)))
                weighted = probs * dprobs
                delta = jnp.sum(weighted, axis=1, keepdims=True)
                dscores = (weighted - probs * delta).astype(bf16)
                dqs.append(dot(dscores, keys, ((1,), (0,))))
                dks[keys_at, :] += dot(dscores, q, ((0,), (0,)))
                dvs[keys_at, :] += dot(low_probs, do, ((0,), (0,)))
            put(ob, j, 0, jnp.where(first_head, outs[0], outs[1]).astype(bf16))
            dq = turn_back(jnp.where(first_head, dqs[0], dqs[1]) * scale, j).astype(bf16)
            put(dqkv, j, 0, dq)
            total_q += summed(dq)
            if j in (3, 5):
                half_step(*steps[j // 4])
        total_k = jnp.zeros((1, PAIR), f32)
        total_v = jnp.zeros((1, PAIR), f32)
        for j in range(blocks):
            here = slice(j * BLOCK, (j + 1) * BLOCK)
            dk = turn_back(dks[here, :] * scale, j).astype(bf16)
            dv = dvs[here, :].astype(bf16)
            put(dqkv, j, 1, dk)
            put(dqkv, j, 2, dv)
            total_k += summed(dk)
            total_v += summed(dv)
        half_step(*steps[2])
        for kind, total in enumerate((total_q, total_k, total_v)):
            cols = pl.ds(pl.multiple_of(p * PAIR, PAIR), PAIR)
            past = sums[kind:kind + 1, cols] if m else 0.0
            sums[kind:kind + 1, cols] = past + total

    per = packs * 3
    if done[0] % 2:
        advance()
    start = done[0] // 2

    def attend_pair(p):
        for m in range(packs):
            steps = [(start + (per // 2) * p + (3 * m + n) // 2, (3 * m + n) % 2) for n in range(3)]
            attend(p, m, steps)

    loop(pairs, attend_pair)
    done[0] += per * pairs

    dense_chunk = 2 * TILES

    def turn_round(source, first, kind):
        def step(sb):
            lanes = slice(kind * rows_home, (kind + 1) * rows_home)
            t = source[sb, :, :, :, lanes].reshape(rows_home, rows_home).astype(f32)
            tt[first:first + rows_home, span(sb, rows_home)] = t.T.astype(bf16)

        loop(group, step)

    sent(0)
    arrived(TILES + 3)
    turn_round(ob, 0, 0)
    grad_rows(0, rows_home, 0, 0)
    store_chunk(0, dense_chunk).start()
    advance()
    for kind in range(kinds):
        turn_round(dqkv, (kind % 2) * rows_home, kind)
        spread((kind % 2) * rows_home, kind, dense_chunk + 1 + kind)
        advance()
    store_chunk(0, dense_chunk).wait()
    chain_a(dense_chunk)

    def part(which, q, cols):
        rows = span(q, rows_home)
        if which == 0:
            return dot(act[rows, :], fc2[:, cols], ((1,), (0,))) + dot(
                ob[q].reshape(rows_home, rows_home), dense[:, cols], ((1,), (0,))
            )
        return dot(dup[rows, :], fc1[cols, :], ((1,), (1,))) + dot(
            dqkv[q].reshape(rows_home, kinds * rows_home), wqkv[cols, :], ((1,), (1,))
        )

    chips = part_in.shape[1]

    def give(which, c):
        mine = own(hn, which * chips + c)
        rows = span(which * chips + c, rows_home)

        def step(cb):
            cols = span(cb, wide)
            hn[rows, cols] = part(which, 2 * c + 1 - core, cols).astype(bf16)

        loop(width // wide, step)
        remote(mine, part_in.at[which, c], d_send.at[which * chips + c],
               p_recv.at[which * chips + c], at_shard(flip(1))).start()

    for a in range(2):
        for n in range(7):
            buf = buffers[a]
            remote(own(buf, me), own(buf, me), ag_send.at[a, n], ag_recv.at[a, 1],
                   at_shard(flip(1))).wait_send()
    for which in range(2):
        for first in range(0, chips, 2):
            loop(2, lambda n: give(which, first + n))
            advance()
        sent(which)
        arrived(dense_chunk + 1 + which)
    sent(2)
    arrived(dense_chunk + 3)

    toward, across = 1 + core, 2 - core

    def total(which, c, n, extra):
        chip = chip_of(c)
        rows = span(which * chips + n, rows_home)
        block = part_in.at[which, chip]
        remote(block, block, d_send.at[0], p_recv.at[which * chips + chip],
               at_shard(flip(1))).wait_recv()
        copies = [local(block, tt.at[0:rows_home, :], load.at[0])]
        if extra:
            block = mid_in.at[which]
            remote(block, block, k_send.at[0], m_recv.at[which], at_shard(flip(2))).wait_recv()
            copies.append(local(block, tt.at[rows_home:2 * rows_home, :], load.at[1]))
        for copy in copies:
            copy.start()
        for copy in copies:
            copy.wait()

        def step(cb):
            cols = span(cb, wide)
            acc = part(which, 2 * chip + core, cols) + tt[0:rows_home, cols].astype(f32)
            if extra:
                acc = acc + tt[rows_home:2 * rows_home, cols].astype(f32)
            gy[rows, cols] = acc.astype(bf16)

        loop(width // wide, step)
        return own(gy, which * chips + n)

    def keep(which, c, n, target, recv, to):
        src = total(which, c, n, n == 2)
        if n == 3:
            local(src, target, k_send.at[which * chips + n]).start()
        else:
            remote(src, target, k_send.at[which * chips + n], recv,
                   at_shard(2 * chip_of(to) + core)).start()

    for which in range(2):
        keep(which, 3, 0, mid_in.at[which], m_recv.at[which], toward)
    advance()
    for which in range(2):
        keep(which, toward, 1, home.at[which, 1], h_recv.at[3 * which + 1], toward)
        advance()
    for which in range(2):
        keep(which, 0, 3, home.at[which, 0], None, 0)
    advance(WAIT)
    for which in range(2):
        keep(which, across, 2, home.at[which, 2], h_recv.at[3 * which + 2], across)
        advance()
    advance(HOLD)

    again = [local(tokens, gst.at[0], load.at[0]), local(cotangent, gst.at[1], load.at[1])]
    for copy in again:
        copy.start()
    again[0].wait()
    sort_rows(0, put_tt(0))
    again[1].wait()
    sort_rows(1, put_tt(rows_home))
    advance()
    for n in range(2 * chips):
        block = part_in.at[n // chips, n % chips]
        remote(block, block, d_send.at[n], p_recv.at[n], at_shard(flip(1))).wait_send()
    bring = []
    for which in range(2):
        block = home.at[which, 0]
        local(own(gy, which * chips + 3), block, k_send.at[which * chips + 3]).wait()
        for c in range(3):
            block = home.at[which, c]
            if c:
                remote(block, block, k_send.at[0], h_recv.at[3 * which + c],
                       at_shard(flip(2))).wait_recv()
            bring.append(local(block, own(hn, 3 * which + c), load.at[3 * which + c]))
            bring[-1].start()
    advance()
    for copy in bring:
        copy.wait()
    gain = full[0:1, :]
    out_bias = full[2:3, :] + full[3:4, :]
    full[8:16, :] = jnp.zeros((8, width), f32)

    def finish(rb):
        rows = span(rb, few)
        keep = valid_ref[rows, :]
        x = tt[rows, :].astype(f32)
        g = tt[pl.ds(pl.multiple_of(rows_home + rb * few, few), few), :].astype(f32)
        branch, dh = out_bias, 0.0
        for c in range(3):
            branch = branch + hn[pl.ds(pl.multiple_of(c * rows_home + rb * few, few), few), :].astype(f32)
            dh = dh + hn[
                pl.ds(pl.multiple_of((3 + c) * rows_home + rb * few, few), few), :
            ].astype(f32)
        gst[0, rows, :] = (x + branch * keep).astype(bf16)
        xhat, rstd = statistics(x)
        scaled = dh * gain
        dx = (
            scaled
            - jnp.mean(scaled, axis=1, keepdims=True)
            - xhat * jnp.mean(scaled * xhat, axis=1, keepdims=True)
        ) * rstd
        gst[1, rows, :] = (g + dx).astype(bf16)
        full[8:9, :] += jnp.sum(g * keep, axis=0, keepdims=True)
        full[9:10, :] += jnp.sum(dh * xhat, axis=0, keepdims=True)
        full[10:11, :] += jnp.sum(dh, axis=0, keepdims=True)

    loop(rows_home // few, finish)
    for which, out in enumerate((mixed_out, token_out)):
        for m in range(packs):
            rows = slice(m * pack_rows, (m + 1) * pack_rows)

            def step(cb):
                cols = span(cb, wide)
                tt[which * rows_home + m * pack_rows:which * rows_home + (m + 1) * pack_rows, cols] = dot(
                    select_ref[m], gst[which, rows, cols], ((0,), (0,))
                ).astype(bf16)

            loop(width // wide, step)
        local(tt.at[which * rows_home:(which + 1) * rows_home, :], out, load.at[which]).start()
    advance()

    for d in range(group):
        cols = slice(d * rows_home, (d + 1) * rows_home)
        vsend[d, 0:3, :] = full[8:11, cols]
        for n in range(kinds):
            piece = kinds * d + n
            vsend[d, 3 + n:4 + n, :] = jnp.where(
                me == piece % group, sums[piece // group:piece // group + 1, :], 0.0
            )
    for e in range(1, 8):
        d = flip(e)
        remote(vsend.at[d], vgot.at[me], v_send.at[1], v_recv.at[1], at_shard(d)).start()
    vgot[me] = vsend[me]
    block = vgot.at[0:7]
    local(block, block, v_recv.at[1]).wait()
    advance()
    total = vgot[0]
    for q in range(1, group):
        total = total + vgot[q]
    zgot[rep, 0:6, :] = total[0:6, :]
    zgot[rep, 6:6 + TILES, :] = sums[6:6 + TILES, :]
    for z in range(1, 4):
        remote(zgot.at[rep], zgot.at[rep], v_send.at[2], v_recv.at[2],
               at_rep((rep + z) % 4)).start()
    block = zgot.at[0:3]
    local(block, block, v_recv.at[2]).wait()
    vec_out[...] = (zgot[0] + zgot[1]) + (zgot[2] + zgot[3])
    local(block, block, v_send.at[2]).wait()
    block = vsend.at[0:7]
    local(block, block, v_send.at[1]).wait()
    block = vecs.at[0:7]
    local(block, block, v_send.at[0]).wait()

    advance(last_half + 1)

    @pl.when(outer)
    def _():
        def end(u):
            g, a, b, t = unit(u)
            remote(g, a, za_s.at[u], za_r.at[u], at_rep(near)).wait_send()
            remote(g, t, zc_s.at[u], zc_r.at[u], at_rep(near)).wait_recv()

        loop(units, end)

    @pl.when(inner)
    def _():
        for u in range(units - SLOTS, units):
            t = unit(u)[3]
            past = pb.at[u % SLOTS]
            remote(past, t, zc_s.at[u], zc_r.at[u], at_rep(near)).wait_send()
            local(past, t, zt.at[u]).wait()

    for which, out in enumerate((mixed_out, token_out)):
        local(tt.at[which * rows_home:(which + 1) * rows_home, :], out, load.at[which]).wait()
    for which in range(2):
        for n in range(3):
            block = home.at[which, n]
            remote(block, block, k_send.at[which * chips + n], m_recv.at[which],
                   at_shard(flip(2))).wait_send()
    for block, sem in (
        (fc1.at[0:4 * rows_home, 0:EARLY * tile], w_send.at[0]),
        (wqkv.at[0:7 * rows_home, :], w_send.at[1]),
        (fc1.at[0:7 * rows_home, EARLY * tile:], w_send.at[2]),
        (fc1.at[0:3 * rows_home, 0:EARLY * tile], x_send.at[0]),
    ):
        local(block, block, sem).wait()


def widen_kernel(sums, fc2, fc1, dense, qkv, low, high, in_sem, out_sem):
    chunks, rows, width = sums.shape
    tile = rows
    ff = fc2.shape[0]

    def bring(c):
        return pltpu.make_async_copy(sums.at[c], low.at[c % 3], in_sem.at[c % 3])

    def take(c):
        slot = high.at[c % 3]
        if c < TILES:
            pairs = [(slot, fc2.at[c * rows:(c + 1) * rows, :])]
        elif c < 2 * TILES:
            pairs = [
                (
                    slot.at[:, q * tile:(q + 1) * tile],
                    fc1.at[:, q * ff + (c - TILES) * tile:q * ff + (c - TILES + 1) * tile],
                )
                for q in range(width // tile)
            ]
        elif c == 2 * TILES:
            pairs = [(slot, dense)]
        else:
            k = c - 2 * TILES - 1
            pairs = [(slot, qkv.at[:, k * width:(k + 1) * width])]
        return [
            pltpu.make_async_copy(src, dst, out_sem.at[c % 3, n]) for n, (src, dst) in enumerate(pairs)
        ]

    for c in range(2):
        bring(c).start()
    for c in range(chunks):
        bring(c).wait()
        if c + 2 < chunks:
            bring(c + 2).start()
        if c >= 3:
            for copy in take(c - 3):
                copy.wait()

        def step(rb, _):
            at = pl.ds(pl.multiple_of(rb * 32, 32), 32)
            high[c % 3, at, :] = low[c % 3, at, :].astype(jnp.float32)
            return 0

        lax.fori_loop(0, rows // 32, step, 0)
        for copy in take(c):
            copy.start()
    for c in range(chunks - 3, chunks):
        for copy in take(c):
            copy.wait()


def fused(begins, key_id, base, turns, select, valid, vec, tokens, cotangent, fc1_w, qkv_w, fc2_w,
          dense_w, group):
    bf16, f32 = jnp.bfloat16, jnp.float32
    rows, width = tokens.shape
    ff = fc1_w.shape[1] // group
    tile = ff // TILES
    packs, blocks = begins.shape
    cap = rows // packs // blocks
    total = group * rows
    chips = group // 2
    chunks = 2 * TILES + 4
    chunk = jax.ShapeDtypeStruct((chunks, rows, width), bf16)
    parts = [jax.ShapeDtypeStruct((2, n, rows, width), bf16) for n in (chips, 3)]
    parts.append(jax.ShapeDtypeStruct((2, rows, width), bf16))
    rows_out = jax.ShapeDtypeStruct((rows, width), bf16)
    out_shape = [chunk] * 4 + parts + [rows_out] * 2 + [
        jax.ShapeDtypeStruct((VROWS, rows), f32)
    ]
    vmem = pl.BlockSpec(memory_space=pltpu.VMEM)
    anywhere = pl.BlockSpec(memory_space=pl.ANY)
    dma = pltpu.SemaphoreType.DMA
    per = (group, packs, blocks, cap)
    pack = blocks * BLOCK
    scratch = [
        pltpu.VMEM((total, width), bf16), pltpu.VMEM((total, width), bf16),
        pltpu.VMEM((width, ff), bf16), pltpu.VMEM((ff, width), bf16),
        pltpu.VMEM((width, 3 * rows), bf16), pltpu.VMEM((rows, width), bf16),
        pltpu.VMEM((total, ff), bf16), pltpu.VMEM((total, ff), bf16),
        pltpu.VMEM(per + (rows,), bf16), pltpu.VMEM(per + (3 * rows,), bf16),
        pltpu.VMEM(per + (3 * rows,), bf16), pltpu.VMEM(per + (rows,), bf16),
        pltpu.VMEM((pack, PAIR), bf16), pltpu.VMEM((pack, PAIR), bf16),
        pltpu.VMEM((pack, PAIR), f32), pltpu.VMEM((pack, PAIR), f32),
        pltpu.VMEM((2 * tile, total), bf16),
        pltpu.VMEM((2, rows, width), bf16), pltpu.VMEM((STAGES, group, rows, rows), bf16),
        pltpu.VMEM((SLOTS, rows // 2, width), bf16), pltpu.VMEM((rows // 2, width), bf16),
        pltpu.VMEM((rows // 2, width), bf16),
        pltpu.VMEM((group, VROWS, rows), f32), pltpu.VMEM((VROWS, width), f32),
        pltpu.VMEM((VROWS, rows), f32), pltpu.VMEM((group, VROWS, rows), f32),
        pltpu.VMEM((group, VROWS, rows), f32), pltpu.VMEM((4, VROWS, rows), f32),
        pltpu.VMEM((8, 3 * rows), f32),
        dma((9,)), dma((2, 7)), dma((2, 8)), dma((3,)), dma((TILES + 1,)), dma((1,)),
        dma((TILES,)), dma((2,)), dma((STAGES,)), dma((STAGES,)), dma((chunks,)),
        dma((2 * chunks,)), dma((2 * chunks,)), dma((2 * chunks,)), dma((2 * chunks,)),
        dma((2 * chunks,)), dma((2 * chunks,)), dma((2 * chunks,)), dma((3,)),
        dma((2 * chips,)), dma((2 * chips,)), dma((6,)), dma((2 * chips,)), dma((2,)), dma((3,)),
        dma((3,)),
    ]
    flops = 6 * total * width * (2 * ff + 4 * rows)
    outs = pl.pallas_call(
        fused_kernel,
        in_specs=[pl.BlockSpec(memory_space=pltpu.SMEM)] + [vmem] * 5 + [anywhere] * 7,
        out_specs=[anywhere] * 9 + [vmem],
        out_shape=out_shape,
        scratch_shapes=scratch,
        compiler_params=pltpu.CompilerParams(
            vmem_limit_bytes=60 << 20, collective_id=0, has_side_effects=True
        ),
        cost_estimate=pl.CostEstimate(
            flops=flops, bytes_accessed=64 << 20, transcendentals=total * ff
        ),
    )(begins, key_id, base, turns, select, valid, vec, tokens, cotangent, fc1_w, qkv_w, fc2_w, dense_w)
    sums = outs[3]
    shapes = ((ff, width), (rows, group * ff), (rows, width), (rows, 3 * width))
    grad_fc2, grad_fc1, grad_dense, grad_qkv = pl.pallas_call(
        widen_kernel,
        in_specs=[anywhere],
        out_specs=[anywhere] * 4,
        out_shape=[jax.ShapeDtypeStruct(shape, f32) for shape in shapes],
        scratch_shapes=[
            pltpu.VMEM((3, rows, width), bf16), pltpu.VMEM((3, rows, width), f32), dma((3,)),
            dma((3, group)),
        ],
        compiler_params=pltpu.CompilerParams(vmem_limit_bytes=58 << 20),
    )(sums)
    return outs[7], outs[8], outs[9], grad_qkv, grad_dense, grad_fc1, grad_fc2


def spread_layer(
    gy_home, hn_home, begins, key_id, qkv_weight, b_qkv, dense_weight, fc1_weight, b_fc1, fc2_weight
):
    bf16, f32 = jnp.bfloat16, jnp.float32
    group, reps = lax.axis_size("shard"), lax.axis_size("rep")
    width = gy_home.shape[1]
    rows = gy_home.shape[0] // MICRO
    cap = rows // group
    mine = width // group
    ff_mine = fc1_weight.shape[1] // group
    blocks = begins.shape[1]
    all_rows = MICRO * rows * group

    fc1 = lax.all_to_all(
        fc1_weight.reshape(mine, group, ff_mine).transpose(1, 0, 2), "shard", 0, 0, tiled=True
    ).reshape(width, ff_mine)
    w_qkv = lax.all_to_all(
        qkv_weight.reshape(mine, 3, group, mine).transpose(2, 0, 1, 3), "shard", 0, 0, tiled=True
    ).reshape(width, 3 * mine)

    gy = lax.all_gather(gy_home, "shard", axis=0, tiled=True)
    hn = lax.all_gather(hn_home, "shard", axis=0, tiled=True)

    upper = dot(hn, fc1, ((1,), (0,))) + b_fc1
    inner = math.sqrt(2.0 / math.pi) * (upper + 0.044715 * upper * upper * upper)
    curve = jnp.tanh(inner)
    act = (0.5 * upper * (1.0 + curve)).astype(bf16)
    slope = 0.5 * (1.0 + curve) + 0.5 * upper * (1.0 - curve * curve) * math.sqrt(
        2.0 / math.pi
    ) * (1.0 + 3 * 0.044715 * upper * upper)
    dup = (dot(gy, fc2_weight, ((1,), (1,))) * slope).astype(bf16)
    g_fc2 = dot(act, gy, ((0,), (0,)), f32).astype(bf16)
    g_fc1 = dot(hn, dup, ((0,), (0,)), f32).astype(bf16)

    def over_reps(part):
        return lax.psum_scatter(part, "rep", scatter_dimension=0, tiled=True)

    def from_reps(part):
        return lax.all_gather(part, "rep", axis=0, tiled=True)

    def by_rows(grad):
        cols = grad.shape[1]
        split = grad.reshape(group, reps, mine // reps, cols).transpose(1, 0, 2, 3)
        part = over_reps(split.reshape(reps * group, mine // reps, cols))
        part = lax.all_to_all(part, "shard", 0, 0, tiled=True)
        whole = from_reps(part)
        return whole.reshape(reps, group, mine // reps, cols)

    grad_fc2 = from_reps(over_reps(g_fc2)).astype(f32)
    grad_fc1 = by_rows(g_fc1).transpose(0, 2, 1, 3).reshape(mine, -1).astype(f32)

    qkv = dot(hn, w_qkv, ((1,), (0,))) + b_qkv
    dout = dot(gy, dense_weight, ((1,), (1,)))
    shape = (group, MICRO, blocks, cap)
    ob, dq, dk, dv = attention(
        begins, qkv.reshape(*shape, 3 * mine), dout.reshape(*shape, mine), key_id
    )
    ob = ob.reshape(all_rows, mine).astype(bf16)
    dqkv = jnp.concatenate(
        [part.reshape(all_rows, mine).astype(bf16) for part in (dq, dk, dv)], axis=1
    )
    g_qkv = dot(hn, dqkv, ((0,), (0,)), f32).astype(bf16)
    g_dense = dot(ob, gy, ((0,), (0,)), f32).astype(bf16)
    grad_dense = from_reps(over_reps(g_dense)).astype(f32)
    grad_qkv = by_rows(g_qkv).reshape(reps, group, mine // reps, 3, mine)
    grad_qkv = grad_qkv.transpose(0, 2, 3, 1, 4).reshape(mine, 3 * width).astype(f32)

    def home(part):
        got = lax.all_to_all(part.reshape(group, MICRO * rows, width), "shard", 0, 0, tiled=True)
        return jnp.sum(got.astype(f32), axis=0)

    out_part = (
        dot(act, fc2_weight, ((1,), (0,))) + dot(ob, dense_weight, ((1,), (0,)))
    ).astype(bf16)
    dh_part = (dot(dqkv, w_qkv, ((1,), (1,))) + dot(dup, fc1, ((1,), (1,)))).astype(bf16)
    v_qkv = jnp.sum(dqkv.astype(f32), axis=0).reshape(3, mine)
    v_fc1 = jnp.sum(dup.astype(f32), axis=0)
    return (
        home(out_part), home(dh_part), grad_qkv, grad_dense, grad_fc1, grad_fc2, v_qkv, v_fc1
    )


def fused_layer(
    tokens, cotangent, select, valid_home, begins, key_id, ln_gain, ln_bias, qkv_weight, qkv_bias,
    dense_weight, dense_bias, fc1_weight, fc1_bias, fc2_weight, fc2_bias,
):
    f32 = jnp.float32
    group = lax.axis_size("shard")
    rows = tokens.shape[0]
    half = ROT // 2
    lane = np.arange(PAIR) % HDIM
    freqs = np.exp(-math.log(10000.0) * np.arange(half) * 2.0 / ROT).astype(np.float32)[lane % half]
    spots = np.arange(BLOCK)[:, None] * freqs[None, :].astype(np.float64)
    base = jnp.asarray(np.stack([np.cos(spots), np.sin(spots)]).astype(np.float32))
    steps = np.arange(MAXBLK)[:, None] * BLOCK * freqs[None, :].astype(np.float64)
    table = jnp.asarray(np.stack([np.cos(steps), np.sin(steps)], axis=1).astype(np.float32))
    blocks = jnp.arange(begins.shape[1], dtype=jnp.int32)
    offset = blocks[None, :] - begins
    turns = jnp.sum(jnp.where(
        offset[:, :, None, None, None] == jnp.arange(MAXBLK, dtype=jnp.int32)[:, None, None],
        table, 0.0,
    ), axis=2)
    vec, at = 0.0, 0
    for piece in (ln_gain, ln_bias, dense_bias, fc2_bias, qkv_bias, fc1_bias):
        after = VROWS * rows - at - piece.shape[0]
        vec = vec + jnp.pad(piece.astype(f32), (at, after))
        at += piece.shape[0]
    vec = vec.reshape(VROWS, rows)
    mixed, token_grad, sums, grad_qkv, grad_dense, grad_fc1, grad_fc2 = fused(
        begins, key_id, base, turns, select, valid_home.astype(f32), vec, tokens, cotangent,
        fc1_weight, qkv_weight, fc2_weight, dense_weight, group,
    )
    bias_out, gain_grad, lnb_grad = sums[0], sums[1], sums[2]
    return (
        mixed, token_grad, gain_grad, lnb_grad, grad_qkv, sums[3:6].reshape(-1), grad_dense,
        bias_out, grad_fc1, sums[6:6 + TILES].reshape(-1), grad_fc2, bias_out,
    )


def body(
    tokens, cotangent, placement_order, seq_lengths, ln_gain, ln_bias, qkv_weight, qkv_bias,
    dense_weight, dense_bias, fc1_weight, fc1_bias, fc2_weight, fc2_bias,
):
    bf16, f32 = jnp.bfloat16, jnp.float32
    group = lax.axis_size("shard")
    reps = lax.axis_size("rep")
    me = lax.axis_index("shard")
    width = tokens.shape[1]
    rows = tokens.shape[0] // MICRO
    cap = rows // group
    mine = width // group
    ff_mine = fc1_weight.shape[1] // group
    blocks = seq_lengths.shape[2]
    all_rows = MICRO * rows * group

    begins, limits = block_begins(seq_lengths[0])
    spot = jnp.arange(BLOCK, dtype=jnp.int32)
    index = jnp.arange(blocks, dtype=jnp.int32)
    position = (index[None, :, None] - begins[:, :, None]) * BLOCK + spot[None, None, :]
    valid = position < limits[:, :, None]
    key_id = jnp.where(valid, begins[:, :, None], -1).reshape(MICRO, 1, blocks * BLOCK)

    orders = placement_order[0, 0]
    select = (orders[:, None, :] == jnp.arange(rows, dtype=jnp.int32)[None, :, None]).astype(bf16)

    valid_home = lax.dynamic_index_in_dim(
        valid.reshape(MICRO, group, group, cap), me, 2, keepdims=False
    ).reshape(MICRO * rows, 1)
    held = 2 * MICRO * rows * group * (2 * width + 2 * ff_mine + 7 * mine)
    held += 2 * width * (2 * ff_mine + 4 * mine)
    if (group, reps) == (8, 4) and cap % 16 == 0 and held <= FUSED_BYTES:
        return fused_layer(
            tokens, cotangent, select, valid_home, begins, key_id, ln_gain, ln_bias, qkv_weight,
            qkv_bias, dense_weight, dense_bias, fc1_weight, fc1_bias, fc2_weight, fc2_bias,
        )

    pieces = (ln_gain, ln_bias, dense_bias, fc2_bias, qkv_bias, fc1_bias)
    packed = jnp.concatenate(pieces)
    spread = lax.all_gather(packed, "shard", axis=0).astype(f32)
    full, at = [], 0
    for piece in pieces:
        full.append(spread[:, at:at + piece.shape[0]].reshape(-1))
        at += piece.shape[0]
    gain, lnb, b_dense, b_fc2, b_qkv, b_fc1 = full
    b_qkv = lax.dynamic_slice_in_dim(b_qkv.reshape(3, width), me * mine, mine, 1).reshape(-1)
    b_fc1 = lax.dynamic_slice_in_dim(b_fc1, me * ff_mine, ff_mine, 0)

    def arrange(array):
        return jnp.einsum(
            "mti,mid->mtd", select, array.reshape(MICRO, rows, width),
            preferred_element_type=f32,
        ).astype(bf16).reshape(MICRO * rows, width)

    x_home, g_home = arrange(tokens), arrange(cotangent)
    gy_home = jnp.where(valid_home, g_home, jnp.zeros((), bf16))
    x32 = x_home.astype(f32)
    centered = x32 - jnp.mean(x32, axis=1, keepdims=True)
    rstd = lax.rsqrt(jnp.mean(centered * centered, axis=1, keepdims=True) + 1e-05)
    hn_home = (centered * rstd * gain + lnb).astype(bf16)
    split = (
        gy_home, hn_home, begins, key_id, qkv_weight, b_qkv, dense_weight, fc1_weight, b_fc1,
        fc2_weight,
    )
    result = spread_layer(*split)
    out_sum, dh, grad_qkv, grad_dense, grad_fc1, grad_fc2, v_qkv, v_fc1 = result
    branch = out_sum + (b_dense + b_fc2)
    mixed = (x32 + jnp.where(valid_home, branch, 0.0)).astype(bf16)
    xhat = centered * rstd
    scaled = dh * gain
    dx = (
        scaled
        - jnp.mean(scaled, axis=1, keepdims=True)
        - xhat * jnp.mean(scaled * xhat, axis=1, keepdims=True)
    ) * rstd
    token_grad = (g_home.astype(f32) + dx).astype(bf16)

    def back(array):
        return jnp.einsum(
            "mti,mtd->mid", select, array.reshape(MICRO, rows, width),
            preferred_element_type=f32,
        ).astype(bf16).reshape(MICRO * rows, width)

    v_out = jnp.sum(gy_home.astype(f32), axis=0)
    v_gain = jnp.sum(dh * xhat, axis=0)
    v_lnb = jnp.sum(dh, axis=0)
    mixed_vec = jnp.concatenate([v_qkv.reshape(-1), v_fc1, v_out, v_gain, v_lnb])
    table = lax.all_gather(mixed_vec, ("rep", "shard"), axis=0).reshape(reps, group, -1)
    table = jnp.sum(table, axis=0)
    at = 3 * mine
    bias_qkv = table[:, :at].reshape(group, 3, mine).transpose(1, 0, 2).reshape(-1)
    bias_qkv = lax.dynamic_slice_in_dim(bias_qkv, me * 3 * mine, 3 * mine, 0)
    bias_fc1 = lax.dynamic_index_in_dim(table[:, at:at + ff_mine], me, 0, keepdims=False)
    full = jnp.sum(table[:, at + ff_mine:], axis=0).reshape(3, group, mine)
    bias_out, gain_grad, lnb_grad = lax.dynamic_index_in_dim(full, me, 1, keepdims=False)
    return (
        back(mixed), back(token_grad), gain_grad, lnb_grad, grad_qkv, bias_qkv, grad_dense,
        bias_out, grad_fc1, bias_fc1, grad_fc2, bias_out,
    )


def solution(mesh):
    rows = P(("rep", "shard"), None)
    vector, matrix = P("shard"), P("shard", None)
    layer = (vector, vector, matrix, vector, matrix, vector, matrix, vector, matrix, vector)
    return jax.shard_map(
        body,
        mesh=mesh,
        in_specs=(rows, rows, P("rep", "shard", None, None), P("rep", None, None)) + layer,
        out_specs=(rows, rows) + layer,
        check_vma=False,
    )
```
